32 devices in a mesh: dp: 8 (over z, x), tensor: 4 (over y, core).
Axes of the slice: x: 2, y: 2, z: 4, core: 2. Of those that a mesh axis runs over, the one named last changes fastest.
Arguments:
- inputs: bfloat16 [8192, 768], P('dp'), may hold values from -6 to 6
- memory: bfloat16 [32, 1500, 768], P('dp'), may hold values from -6 to 6
- segments: int32 [8192], P('dp'), may hold values from 0 to 3, as said below
- documents: int32 [8192], P('dp'), may hold values from 0 to 31, as said below
- cotangent: bfloat16 [8192, 768], P('dp'), may hold values from -6 to 6
- norm_gain: float32 [3, 768], replicated, may hold values from 0.5 to 1.5
- norm_shift: float32 [3, 768], replicated, may hold values from -2 to 2
- attn_in: bfloat16 [3, 768, 768], P(None, None, 'tensor'), may hold values from -0.21875 to 0.21875
- attn_bias: float32 [2, 768], P(None, 'tensor'), may hold values from -2 to 2
- attn_out: bfloat16 [768, 768], P('tensor'), may hold values from -1.5 to 1.5
- cross_in: bfloat16 [3, 768, 768], P(None, None, 'tensor'), may hold values from -0.21875 to 0.21875
- cross_bias: float32 [2, 768], P(None, 'tensor'), may hold values from -2 to 2
- cross_out: bfloat16 [768, 768], P('tensor'), may hold values from -4 to 4
- fc_in: bfloat16 [768, 3072], P(None, 'tensor'), may hold values from -0.21875 to 0.21875
- fc_in_bias: float32 [3072], P('tensor'), may hold values from -3 to 3
- fc_out: bfloat16 [3072, 768], P('tensor'), may hold values from -0.4375 to 0.4375
- out_bias: float32 [3, 768], replicated, may hold values from -2 to 2
Outputs:
- output: bfloat16 [8192, 768], P('dp')
- input_grad: float32 [8192, 768], P('dp')
- memory_grad: bfloat16 [32, 1500, 768], P('dp', None, 'tensor')
- grad_norm_gain: float32 [3, 768], replicated
- grad_norm_shift: float32 [3, 768], replicated
- grad_attn_in: float32 [3, 768, 768], P(None, 'dp', 'tensor')
- grad_attn_bias: float32 [2, 768], P(None, 'tensor')
- grad_attn_out: float32 [768, 768], P('tensor', 'dp')
- grad_cross_in: float32 [3, 768, 768], P(None, 'dp', 'tensor')
- grad_cross_bias: float32 [2, 768], P(None, 'tensor')
- grad_cross_out: float32 [768, 768], P('tensor', 'dp')
- grad_fc_in: float32 [768, 3072], P('dp', 'tensor')
- grad_fc_in_bias: float32 [3072], P('tensor')
- grad_fc_out: float32 [3072, 768], P('tensor', 'dp')
- grad_out_bias: float32 [3, 768], replicated
The draws below stay inside these ranges and needn't reach their ends.
Inputs may be any that keep to these rules, and one draw needn't show every extreme that they name: Within each sequence of 1024 tokens, segments never falls and takes every value 0 to 3; each document has at least 204 tokens. For a token of sequence i, documents is i * 4 plus a value fixed by its segment number; the 4 documents of a sequence read 4 different memories.
All inputs are finite; a program needn't handle non-finite values.
Results may differ from the reference program's by a relative error of at most 0.024.
Values may be sent and summed in bfloat16 or wider, within the bound.
No kernel may reach another device: no remote copies, remote signals or barrier semaphores. Data moves between devices by JAX's collectives and lax.ppermute only.
A program may use at most 256 MiB of HBM per device.

```python
import jax
import jax.numpy as jnp
from jax import lax

D = 768
HEADS = 12
HEAD = 64
FF = 3072
FRAMES = 1500
DOCS = 4
SEQ_LEN = 1024
TOKENS = 8192
MEMS = 32
N_DP = 8


def doc_layout(key):
    weight_key = jax.random.fold_in(key, 101)
    order_key = jax.random.fold_in(key, 202)
    sequences = TOKENS // SEQ_LEN
    shares = jax.random.randint(weight_key, (sequences, DOCS), 1, 64, dtype=jnp.int32)
    shortest = SEQ_LEN // 5
    leftover = SEQ_LEN - DOCS * shortest
    additions = shares * leftover // jnp.sum(shares, axis=1, keepdims=True)
    lengths = shortest + additions
    lengths = lengths.at[:, DOCS - 1].add(SEQ_LEN - jnp.sum(lengths, axis=1))
    boundaries = jnp.cumsum(lengths, axis=1)
    positions = jnp.arange(SEQ_LEN, dtype=jnp.int32)
    segment_ids = jnp.sum((positions[None, :, None] >= boundaries[:, None, :DOCS - 1]).astype(jnp.int32), axis=-1)
    ranking = jax.random.randint(order_key, (sequences, DOCS), 0, 1 << 20, dtype=jnp.int32) * DOCS + jnp.arange(DOCS, dtype=jnp.int32)[None, :]
    ordering = jnp.argsort(ranking, axis=1).astype(jnp.int32)
    mapped = jnp.take_along_axis(ordering, segment_ids, axis=1)
    doc_ids = mapped + (jnp.arange(sequences, dtype=jnp.int32) * DOCS)[:, None]
    return (segment_ids.reshape(-1).astype(jnp.int32), doc_ids.reshape(-1).astype(jnp.int32))


def draw_segments(key, part):
    return doc_layout(key)[0]


def draw_documents(key, part):
    return doc_layout(key)[1]


def with_spikes(entries, stream_key, source, target, shards_of, factor):
    owner, partner = [(jnp.arange(entries.shape[dim]) // (entries.shape[dim] // shards_of)).reshape([-1 if axis == dim else 1 for axis in range(entries.ndim)]) for dim in (source, target)]
    chosen = jax.random.permutation(stream_key, shards_of)[partner]
    strong = (owner == chosen) | (owner == (partner + shards_of // 2) % shards_of)
    return jnp.where(strong, factor * entries, entries)


def steps_of(key, dims, cuts, low, high):
    gain = 1.0
    for dim, parts in cuts:
        steps = jax.random.uniform(jax.random.fold_in(jax.random.fold_in(key, 6), dim), (parts,), jnp.float32, low / len(cuts), high / len(cuts))
        gain = gain * jnp.repeat(jnp.exp(steps), dims[dim] // parts).reshape((-1,) + (1,) * (len(dims) - 1 - dim))
    return gain


def normal_values(stream_key, extent, spread, reach, cuts=(), kind=jnp.bfloat16):
    values = spread * jax.random.normal(stream_key, extent, jnp.float32)
    if cuts:
        values = values * steps_of(stream_key, extent, cuts, -0.22, 0.18)
    return jnp.clip(values, -reach, reach).astype(kind)


def heavy_noise(rng, dims, spread, reach, shards, heavy, held_as=jnp.bfloat16):
    values = spread * jax.random.normal(rng, dims, jnp.float32)
    if shards:
        values = values * steps_of(rng, dims, shards, -0.22, 0.18)
    return jnp.clip(with_spikes(values, jax.random.fold_in(rng, 3), *heavy), -reach, reach).astype(held_as)


def setup_inputs(seed: int = 0) -> dict:
    keys = jax.random.split(jax.random.key(seed), 18)
    inputs = normal_values(keys[0], (TOKENS, D), 1.0, 6.0, ((0, 8),))
    memory = normal_values(keys[1], (MEMS, FRAMES, D), 1.0, 6.0, ((0, 8),))
    segments = draw_segments(jax.random.fold_in(keys[17], 71), 0)
    documents = draw_documents(jax.random.fold_in(keys[17], 71), 0)
    cotangent = heavy_noise(keys[4], (TOKENS, D), 1.0, 6.0, ((0, 8),), (0, 1, 8, 2.0))
    norm_gain = jnp.clip(1.0 + 0.1 * jax.random.normal(keys[5], (3, D), jnp.float32), 0.5, 1.5)
    norm_shift = normal_values(keys[6], (3, D), 0.3, 2.0, (), jnp.float32)
    attn_in = normal_values(keys[7], (3, D, D), D ** -0.5, 0.21875, ((2, 4),))
    attn_bias = normal_values(keys[8], (2, D), 0.3, 2.0, ((1, 4),), jnp.float32)
    attn_out = normal_values(keys[9], (D, D), (max(D // 48, 1)) ** -0.5, 1.5, ((0, 4),))
    cross_in = normal_values(keys[10], (3, D, D), D ** -0.5, 0.21875, ((2, 4),))
    cross_bias = normal_values(keys[11], (2, D), 0.3, 2.0, ((1, 4),), jnp.float32)
    cross_out = normal_values(keys[12], (D, D), (max(D // 384, 1)) ** -0.5, 4.0, ((0, 4),))
    fc_in = normal_values(keys[13], (D, FF), D ** -0.5, 0.21875, ((1, 4),))
    fc_in_bias = normal_values(keys[14], (FF,), 0.5, 3.0, ((0, 4),), jnp.float32)
    fc_out = normal_values(keys[15], (FF, D), (max(FF // 16, 1)) ** -0.5, 0.4375, ((0, 4),))
    out_bias = normal_values(keys[16], (3, D), 0.3, 2.0, (), jnp.float32)
    return dict(inputs=inputs, memory=memory, segments=segments, documents=documents, cotangent=cotangent, norm_gain=norm_gain, norm_shift=norm_shift, attn_in=attn_in, attn_bias=attn_bias, attn_out=attn_out, cross_in=cross_in, cross_bias=cross_bias, cross_out=cross_out, fc_in=fc_in, fc_in_bias=fc_in_bias, fc_out=fc_out, out_bias=out_bias)


@jax.custom_vjp
def low(v):
    return lax.optimization_barrier(v.astype(jnp.bfloat16)).astype(jnp.float32)

@jax.custom_vjp
def low_back(v):
    return v

def low_keep(v):
    return (low(v), None)

def low_pass(kept, grad):
    return (grad,)

def back_keep(v):
    return (v, None)

def back_low(kept, grad):
    return (low(grad),)
low.defvjp(low_keep, low_pass)
low_back.defvjp(back_keep, back_low)
EPSILON = 1e-05
PRECISE = lax.Precision.HIGHEST

def layer_norm(values, gain_row, shift_row):
    centred = values - lax.optimization_barrier(jnp.mean(values, axis=-1, keepdims=True))
    inverse = lax.rsqrt(lax.optimization_barrier(jnp.mean(centred * centred, axis=-1, keepdims=True)) + EPSILON)
    return centred * inverse * gain_row + shift_row

def attend(query_rows, key_rows, value_rows, query_ids, key_ids, causal):
    length = query_rows.shape[0]
    per_block = min(512, length)
    number = length // per_block
    factor = HEAD ** (-0.5)
    blocks = query_rows.reshape(number, per_block, HEADS, HEAD)
    key_heads = key_rows.reshape(-1, HEADS, HEAD)
    value_heads = value_rows.reshape(-1, HEADS, HEAD)
    key_pos = jnp.arange(key_rows.shape[0], dtype=jnp.int32)
    block_ids = query_ids.reshape(number, per_block)
    block_pos = jnp.arange(length, dtype=jnp.int32).reshape(number, per_block)

    @jax.checkpoint
    def one_block(inputs):
        block_rows, ids_here, pos_here = inputs
        scores = low_back(jnp.einsum('bhe,she->hbs', block_rows, key_heads, precision=PRECISE) * factor)
        allowed = ids_here[:, None] == key_ids[None, :]
        if causal:
            allowed = allowed & (key_pos[None, :] <= pos_here[:, None])
        scores = jnp.where(allowed[None], scores, -1e+30)
        weights = low(jax.nn.softmax(scores, axis=-1))
        return jnp.einsum('hbs,she->bhe', weights, value_heads, precision=PRECISE)
    mixture = lax.map(one_block, (blocks, block_ids, block_pos))
    return mixture.reshape(length, HEADS * HEAD)

def layer(residual, memory_rows, params, segment_ids, doc_ids):
    norm_gain, norm_shift, attn_in, attn_bias, attn_out, cross_in, cross_bias, cross_out, fc_in, fc_in_bias, fc_out, out_bias = params
    first_in = low(layer_norm(residual, norm_gain[0], norm_shift[0]))
    projected = jnp.einsum('td,ndh->nth', first_in, attn_in, precision=PRECISE)
    self_query = low(low_back(projected[0] + attn_bias[0]))
    self_key = low(low_back(projected[1]))
    self_value = low(low_back(projected[2] + attn_bias[1]))
    self_mixed = low(low_back(attend(self_query, self_key, self_value, segment_ids, segment_ids, True)))
    after_self = residual + low_back(jnp.dot(self_mixed, attn_out, precision=PRECISE)) + out_bias[0]
    second_in = low(layer_norm(after_self, norm_gain[1], norm_shift[1]))
    cross_query = low(low_back(jnp.dot(second_in, cross_in[0], precision=PRECISE) + cross_bias[0]))
    cross_key = low(low_back(jnp.dot(memory_rows, cross_in[1], precision=PRECISE)))
    cross_value = low(low_back(jnp.dot(memory_rows, cross_in[2], precision=PRECISE) + cross_bias[1]))
    frame_docs = jnp.arange(memory_rows.shape[0], dtype=jnp.int32) // FRAMES
    cross_mixed = low(low_back(attend(cross_query, cross_key, cross_value, doc_ids, frame_docs, False)))
    after_cross = after_self + low_back(jnp.dot(cross_mixed, cross_out, precision=PRECISE)) + out_bias[1]
    third_in = low(layer_norm(after_cross, norm_gain[2], norm_shift[2]))
    hidden_pre = low_back(jnp.dot(third_in, fc_in, precision=PRECISE) + fc_in_bias)
    activated = low(jax.nn.gelu(hidden_pre, approximate=False))
    return after_cross + low_back(jnp.dot(activated, fc_out, precision=PRECISE)) + out_bias[2]

def reference(inputs, memory, segments, documents, cotangent, norm_gain, norm_shift, attn_in, attn_bias, attn_out, cross_in, cross_bias, cross_out, fc_in, fc_in_bias, fc_out, out_bias):
    params = tuple((item.astype(jnp.float32) for item in (norm_gain, norm_shift, attn_in, attn_bias, attn_out, cross_in, cross_bias, cross_out, fc_in, fc_in_bias, fc_out, out_bias)))
    sequences = inputs.astype(jnp.float32).reshape(N_DP, SEQ_LEN, D)
    memories = memory.astype(jnp.float32).reshape(N_DP, DOCS * FRAMES, D)
    segment_rows = segments.reshape(N_DP, SEQ_LEN)
    doc_rows = documents.reshape(N_DP, SEQ_LEN)
    grad_seqs = cotangent.astype(jnp.float32).reshape(N_DP, SEQ_LEN, D)

    def one_sequence(totals, items):
        residual, memory_rows, segment_ids, doc_ids, grad_rows, number = items
        local_docs = doc_ids - number * DOCS

        def forward(residual_in, memory_in, params_in):
            return layer(residual_in, memory_in, params_in, segment_ids, local_docs)
        result, pullback = jax.vjp(forward, residual, memory_rows, params)
        grad_input, grad_memory, grad_params = pullback(grad_rows)
        totals = jax.tree.map(jnp.add, totals, grad_params)
        return (totals, (result.astype(jnp.bfloat16), grad_input, grad_memory.astype(jnp.bfloat16)))
    start_totals = jax.tree.map(jnp.zeros_like, params)
    totals, (outputs, input_grads, memory_grads) = lax.scan(one_sequence, start_totals, (sequences, memories, segment_rows, doc_rows, grad_seqs, jnp.arange(N_DP, dtype=jnp.int32)))
    return (outputs.reshape(TOKENS, D), input_grads.reshape(TOKENS, D), memory_grads.reshape(MEMS, FRAMES, D), totals[0], totals[1], totals[2], totals[3], totals[4], totals[5], totals[6], totals[7], totals[8], totals[9], totals[10], totals[11])
```

```python
import jax
import jax.numpy as jnp
from jax import lax
from jax.experimental import pallas as pl
from jax.experimental.layout import Layout, with_layout_constraint
from jax.experimental.pallas import tpu as pltpu
from jax.sharding import PartitionSpec as P

HEAD = 64
PAIR = 2 * HEAD
BLOCK = 128
ROWS = 160
EPSILON = 1e-05
LOG2E = 1.4426950408889634
SCALE = HEAD ** (-0.5)
NEG = -1e30
BIG = 1e30
BF = jnp.bfloat16
F32 = jnp.float32
VMEM = 56 << 20
COST = 4

NT = (((1,), (1,)), ((), ()))
NN = (((1,), (0,)), ((), ()))
TN = (((0,), (0,)), ((), ()))


def dot(left, right, dims=NN):
    return lax.dot_general(left, right, dims, preferred_element_type=F32)


def norm_parts(values):
    centred = values - jnp.mean(values, axis=-1, keepdims=True)
    inverse = lax.rsqrt(jnp.mean(centred * centred, axis=-1, keepdims=True) + EPSILON)
    return centred * inverse, inverse


def call(kernel, grid, in_specs, out_specs, out_shape, scratch, cost, name):
    flops, exps, moved = cost
    return pl.pallas_call(
        kernel,
        grid_spec=pltpu.PrefetchScalarGridSpec(
            num_scalar_prefetch=1,
            grid=grid,
            in_specs=in_specs,
            out_specs=out_specs,
            scratch_shapes=scratch,
        ),
        out_shape=out_shape,
        compiler_params=pltpu.CompilerParams(
            dimension_semantics=("arbitrary",) * len(grid), vmem_limit_bytes=VMEM
        ),
        cost_estimate=pl.CostEstimate(
            flops=COST * flops + 1, transcendentals=COST * exps, bytes_accessed=COST * moved + 1
        ),
        name=name,
    )


def whole(*shape):
    zeros = (0,) * len(shape)
    return pl.BlockSpec(shape, lambda *_: zeros)


def shaped(shape, dtype):
    return jax.ShapeDtypeStruct(shape, dtype)


def two_heads(rows):
    lane = lax.broadcasted_iota(jnp.int32, rows.shape, 1)
    zero = jnp.zeros_like(rows)
    return jnp.concatenate(
        [jnp.where(lane < HEAD, rows, zero), jnp.where(lane < HEAD, zero, rows)], axis=0
    )


def pick_heads(both):
    row = lax.broadcasted_iota(jnp.int32, (PAIR, BLOCK), 0)
    return jnp.where(row < HEAD, both[:, :BLOCK], both[:, BLOCK:]).T


def row_lanes(first):
    lane = lax.broadcasted_iota(jnp.int32, (1, 2 * BLOCK), 1)
    return first + jnp.where(lane < BLOCK, lane, lane - BLOCK)


def flip(matrix):
    return matrix.astype(F32).T.astype(BF)


def split_out(scal, total, send_ref, keep_ref, half):
    core = scal[0]
    here = pl.multiple_of(core * half, half)
    there = pl.multiple_of((1 - core) * half, half)
    keep_ref[...] = total[pl.ds(here, half), :]
    send_ref[...] = total[pl.ds(there, half), :].astype(BF)


def join_halves(scal, own_ref, other_ref, full_ref, half):
    core = scal[0]
    full_ref[pl.ds(pl.multiple_of(core * half, half), half), :] = own_ref[...]
    full_ref[pl.ds(pl.multiple_of((1 - core) * half, half), half), :] = other_ref[...]


def join_weights(own_ref, peer_ref, full_ref):
    part = own_ref.shape[-2]
    full_ref[..., :part, :] = own_ref[...]
    full_ref[..., part:, :] = peer_ref[...]


def pair_rows(pair):
    return pl.ds(pl.multiple_of(pair * PAIR, PAIR), PAIR)


def self_mask(scal, count, first):
    rows = row_lanes(first)
    edge_one, edge_two = scal[3], scal[4]
    begin = jnp.where(rows >= edge_two, edge_two, jnp.where(rows >= edge_one, edge_one, 0))
    keys = lax.broadcasted_iota(jnp.int32, (count, 2 * BLOCK), 0)
    return (keys >= begin) & (keys <= rows)


def self_forward_kernel(
    scal, x_ref, gain_ref, shift_ref, w_own, w_peer, b_ref, wo_own, wo_peer,
    h_ref, q_ref, k_ref, v_ref, o_ref, lse_ref, send_ref, keep_ref, total, vt, w_ref, wo_ref,
):
    pair = pl.program_id(0)
    rows = x_ref.shape[0]

    @pl.when(pair == 0)
    def _():
        join_weights(w_own, w_peer, w_ref)
        join_weights(wo_own, wo_peer, wo_ref)
        normed, _ = norm_parts(x_ref[...].astype(F32))
        h_ref[...] = (normed * gain_ref[...] + shift_ref[...]).astype(BF)
        total[...] = jnp.zeros_like(total)

    hidden = h_ref[...]
    here = pair_rows(pair)
    q_ref[...] = (dot(hidden, w_ref[0, here, :], NT) + b_ref[0:1, :]).astype(BF)
    k_ref[...] = dot(hidden, w_ref[1, here, :], NT).astype(BF)
    v_ref[...] = (dot(hidden, w_ref[2, here, :], NT) + b_ref[1:2, :]).astype(BF)
    vt[...] = flip(v_ref[...])
    for block in range(rows // BLOCK):
        first = block * BLOCK
        count = first + BLOCK
        queries = two_heads(q_ref[first : first + BLOCK, :])
        scores = dot(k_ref[:count, :], queries, NT)
        scores = jnp.where(self_mask(scal, count, first), scores, NEG)
        largest = jnp.max(scores, axis=0, keepdims=True)
        chances = jnp.exp2((scores - largest) * (SCALE * LOG2E))
        totals = jnp.sum(chances, axis=0, keepdims=True)
        mixed = dot(vt[:, :count], chances.astype(BF)) * (1.0 / totals)
        o_ref[first : first + BLOCK, :] = pick_heads(mixed).astype(BF)
        lse_ref[0, block] = largest * (SCALE * LOG2E) + jnp.log(totals) * LOG2E
    total[...] += dot(o_ref[...], wo_ref[here, :])

    @pl.when(pair == pl.num_programs(0) - 1)
    def _():
        split_out(scal, total, send_ref, keep_ref, rows // 2)


def self_forward(scal, x_win, gain, shift, w_in, bias, w_out):
    rows, width = x_win.shape
    part = w_out[0].shape[0]
    pairs = 2 * part // PAIR
    blocks = rows // BLOCK
    by_pair = pl.BlockSpec((rows, PAIR), lambda p, s: (0, p))
    feats = pairs * PAIR
    return call(
        self_forward_kernel,
        (pairs,),
        [
            whole(rows, width),
            whole(1, width),
            whole(1, width),
            whole(3, part, width),
            whole(3, part, width),
            pl.BlockSpec((2, PAIR), lambda p, s: (0, p)),
            whole(part, width),
            whole(part, width),
        ],
        [
            whole(rows, width),
            by_pair,
            by_pair,
            by_pair,
            by_pair,
            pl.BlockSpec((1, blocks, 1, 2 * BLOCK), lambda p, s: (p, 0, 0, 0)),
            whole(rows // 2, width),
            whole(rows // 2, width),
        ],
        [
            shaped((rows, width), BF),
            shaped((rows, feats), BF),
            shaped((rows, feats), BF),
            shaped((rows, feats), BF),
            shaped((rows, feats), BF),
            shaped((pairs, blocks, 1, 2 * BLOCK), F32),
            shaped((rows // 2, width), BF),
            shaped((rows // 2, width), F32),
        ],
        [
            pltpu.VMEM((rows, width), F32),
            pltpu.VMEM((PAIR, rows), BF),
            pltpu.VMEM((3, feats, width), BF),
            pltpu.VMEM((feats, width), BF),
        ],
        (8 * rows * width * feats + 4 * rows * rows * feats, rows * rows * 6, 12 << 20),
        "self_forward",
    )(scal, x_win, gain, shift, *w_in, bias, *w_out)


def self_backward_kernel(
    scal, own_ref, other_ref, wo_own, wo_peer, q_ref, k_ref, v_ref, lse_ref, w_own, w_peer,
    dx_ref, dq_ref, dk_ref, dv_ref, sum_ref, send_ref, keep_ref,
    total, kt, do, dks, dvs, w_ref, wo_ref,
):
    pair = pl.program_id(0)
    rows = q_ref.shape[0]

    @pl.when(pair == 0)
    def _():
        join_halves(scal, own_ref, other_ref, dx_ref, rows // 2)
        join_weights(w_own, w_peer, w_ref)
        join_weights(wo_own, wo_peer, wo_ref)
        total[...] = jnp.zeros_like(total)

    here = pair_rows(pair)
    do[...] = dot(dx_ref[...], wo_ref[here, :], NT).astype(BF)
    kt[...] = flip(k_ref[...])
    dks[...] = jnp.zeros_like(dks)
    dvs[...] = jnp.zeros_like(dvs)
    for block in range(rows // BLOCK):
        first = block * BLOCK
        count = first + BLOCK
        queries = two_heads(q_ref[first : first + BLOCK, :])
        grads = two_heads(do[first : first + BLOCK, :])
        scores = dot(k_ref[:count, :], queries, NT)
        chances = jnp.exp2(scores * (SCALE * LOG2E) - lse_ref[0, block])
        chances = jnp.where(self_mask(scal, count, first), chances, 0.0)
        prob_grad = dot(v_ref[:count, :], grads, NT)
        shared = jnp.sum(chances * prob_grad, axis=0, keepdims=True)
        score_grad = (chances * (prob_grad - shared)).astype(BF)
        dvs[:count, :] += dot(chances.astype(BF), grads)
        dks[:count, :] += dot(score_grad, queries)
        dq_ref[first : first + BLOCK, :] = (
            pick_heads(dot(kt[:, :count], score_grad)) * SCALE
        ).astype(BF)
    dk_ref[...] = (dks[...] * SCALE).astype(BF)
    dv_ref[...] = dvs[...].astype(BF)
    sum_ref[0:1, :] = jnp.sum(dq_ref[...].astype(F32), axis=0, keepdims=True)
    sum_ref[1:2, :] = jnp.sum(dv_ref[...].astype(F32), axis=0, keepdims=True)
    total[...] += (
        dot(dq_ref[...], w_ref[0, here, :])
        + dot(dk_ref[...], w_ref[1, here, :])
        + dot(dv_ref[...], w_ref[2, here, :])
    )

    @pl.when(pair == pl.num_programs(0) - 1)
    def _():
        split_out(scal, total, send_ref, keep_ref, rows // 2)


def self_backward(scal, own, other, w_out, q, k, v, lse, w_in):
    rows, feats = q.shape
    width = own.shape[1]
    pairs = feats // PAIR
    blocks = rows // BLOCK
    half = rows // 2
    by_pair = pl.BlockSpec((rows, PAIR), lambda p, s: (0, p))
    return call(
        self_backward_kernel,
        (pairs,),
        [
            whole(half, width),
            whole(half, width),
            whole(feats // 2, width),
            whole(feats // 2, width),
            by_pair,
            by_pair,
            by_pair,
            pl.BlockSpec((1, blocks, 1, 2 * BLOCK), lambda p, s: (p, 0, 0, 0)),
            whole(3, feats // 2, width),
            whole(3, feats // 2, width),
        ],
        [
            whole(rows, width),
            by_pair,
            by_pair,
            by_pair,
            pl.BlockSpec((2, PAIR), lambda p, s: (0, p)),
            whole(half, width),
            whole(half, width),
        ],
        [
            shaped((rows, width), BF),
            shaped((rows, feats), BF),
            shaped((rows, feats), BF),
            shaped((rows, feats), BF),
            shaped((2, feats), F32),
            shaped((half, width), BF),
            shaped((half, width), F32),
        ],
        [
            pltpu.VMEM((rows, width), F32),
            pltpu.VMEM((PAIR, rows), BF),
            pltpu.VMEM((rows, PAIR), BF),
            pltpu.VMEM((rows, PAIR), F32),
            pltpu.VMEM((rows, PAIR), F32),
            pltpu.VMEM((3, feats, width), BF),
            pltpu.VMEM((feats, width), BF),
        ],
        (8 * rows * width * feats + 10 * rows * rows * feats, rows * rows * 6, 14 << 20),
        "self_backward",
    )(scal, own, other, *w_out, q, k, v, lse, *w_in)


def add_norm_kernel(scal, base_ref, keep_ref, got_ref, bias_ref, gain_ref, shift_ref, x_ref, h_ref):
    value = base_ref[...].astype(F32) + (keep_ref[...] + got_ref[...].astype(F32)) + bias_ref[...]
    x_ref[...] = value
    normed, _ = norm_parts(value)
    h_ref[...] = (normed * gain_ref[...] + shift_ref[...]).astype(BF)


def add_norm(scal, base, keep, got, bias, gain, shift, by_core):
    half, width = keep.shape
    steps = half // ROWS
    block = pl.BlockSpec((ROWS, width), lambda i, s: (i, 0))
    base_spec = pl.BlockSpec((ROWS, width), lambda i, s: (s[0] * steps + i, 0)) if by_core else block
    return call(
        add_norm_kernel,
        (steps,),
        [base_spec, block, block] + [whole(1, width)] * 3,
        [block] * 2,
        [shaped((half, width), F32), shaped((half, width), BF)],
        [],
        (0, 0, 0),
        "add_norm",
    )(scal, base, keep, got, bias, gain, shift)


def norm_back_kernel(scal, base_ref, keep_ref, got_ref, x_ref, gain_ref, dx_ref, low_ref, sum_ref):
    step, steps = pl.program_id(0), pl.num_programs(0)
    base = base_ref[...].astype(F32)
    grad = keep_ref[...] + got_ref[...].astype(F32)
    row = (scal[0] * steps + step) * ROWS + lax.broadcasted_iota(jnp.int32, (ROWS, 1), 0)
    valid = (row >= scal[5]) & (row < scal[8])
    grad = jnp.where(valid, grad, 0.0)
    base = jnp.where(valid, base, 0.0)
    normed, inverse = norm_parts(x_ref[...].astype(F32))
    scaled = grad * gain_ref[...]
    total = base + inverse * (
        scaled
        - jnp.mean(scaled, axis=-1, keepdims=True)
        - normed * jnp.mean(scaled * normed, axis=-1, keepdims=True)
    )
    dx_ref[...] = total
    low_ref[...] = total.astype(BF)

    @pl.when(step == 0)
    def _():
        sum_ref[...] = jnp.zeros_like(sum_ref)

    sum_ref[0:1, :] += jnp.sum(grad * normed, axis=0, keepdims=True)
    sum_ref[1:2, :] += jnp.sum(grad, axis=0, keepdims=True)
    sum_ref[2:3, :] += jnp.sum(total, axis=0, keepdims=True)
    sum_ref[3:4, :] += jnp.sum(base, axis=0, keepdims=True)


def norm_back(scal, base, keep, got, x, gain, base_by_core, x_by_core):
    half, width = keep.shape

    steps = half // ROWS
    block = pl.BlockSpec((ROWS, width), lambda i, s: (i, 0))
    cored = pl.BlockSpec((ROWS, width), lambda i, s: (s[0] * steps + i, 0))

    def spec(by_core):
        return cored if by_core else block

    return call(
        norm_back_kernel,
        (steps,),
        [spec(base_by_core), block, block, spec(x_by_core), whole(1, width)],
        [block, block, whole(4, width)],
        [shaped((half, width), F32), shaped((half, width), BF), shaped((4, width), F32)],
        [],
        (0, 0, 0),
        "norm_back",
    )(scal, base, keep, got, x, gain)


def pieces(total, size):
    return [(first, min(size, total - first)) for first in range(0, total, size)]


def memory_project_kernel(scal, mem_ref, w_own, w_peer, b_ref, k_ref, v_ref, w_ref):
    @pl.when(pl.program_id(0) == 0)
    def _():
        join_weights(w_own, w_peer, w_ref)

    frames = mem_ref.shape[1]
    padded = k_ref.shape[1]
    tail = padded - BLOCK
    k_ref[0, tail:padded, :] = jnp.zeros((BLOCK, k_ref.shape[2]), BF)
    v_ref[0, tail:padded, :] = jnp.zeros((BLOCK, k_ref.shape[2]), BF)
    for first, size in pieces(frames, 256):
        rows = mem_ref[0, first : first + size, :]
        k_ref[0, first : first + size, :] = dot(rows, w_ref[1], NT).astype(BF)
        v_ref[0, first : first + size, :] = (dot(rows, w_ref[2], NT) + b_ref[...]).astype(BF)


def memory_project(scal, memory, w_kv, bias, padded):
    _, frames, width = memory.shape
    part = w_kv[0].shape[1]
    feats = 2 * part
    out = pl.BlockSpec((1, padded, feats), lambda j, s: (j, 0, 0))
    return call(
        memory_project_kernel,
        (2,),
        [
            pl.BlockSpec((1, frames, width), lambda j, s: (s[9 + j], 0, 0)),
            whole(3, part, width),
            whole(3, part, width),
            whole(1, feats),
        ],
        [out, out],
        [shaped((2, padded, feats), BF)] * 2,
        [pltpu.VMEM((3, feats, width), BF)],
        (8 * frames * width * feats, 0, 12 << 20),
        "memory_project",
    )(scal, memory, *w_kv, bias)


def block_span(scal, doc):
    low, high = scal[5 + 2 * doc], scal[6 + 2 * doc]
    return low, high, low // BLOCK, (high + BLOCK - 1) // BLOCK


def cross_forward_kernel(
    scal, own_ref, other_ref, wq_own, wq_peer, bq_ref, k_ref, v_ref, wo_own, wo_peer,
    h_ref, q_ref, o_ref, lse_ref, send_ref, keep_ref, total, vt, s_ref, wq_ref, wo_ref, *, frames,
):
    pair, doc = pl.program_id(0), pl.program_id(1)
    rows = q_ref.shape[0]
    padded = k_ref.shape[1]

    @pl.when((pair == 0) & (doc == 0))
    def _():
        join_halves(scal, own_ref, other_ref, h_ref, rows // 2)
        join_weights(wq_own.at[0], wq_peer.at[0], wq_ref)
        join_weights(wo_own, wo_peer, wo_ref)
        total[...] = jnp.zeros_like(total)

    here = pair_rows(pair)

    @pl.when(doc == 0)
    def _():
        q_ref[...] = (dot(h_ref[...], wq_ref[here, :], NT) + bq_ref[...]).astype(BF)
        o_ref[...] = jnp.zeros_like(o_ref)
        lse_ref[...] = jnp.zeros_like(lse_ref)

    vt[...] = flip(v_ref[0])
    low, high, start, stop = block_span(scal, doc)

    def one_block(block, carry):
        first = pl.multiple_of(block * BLOCK, BLOCK)
        queries = two_heads(q_ref[pl.ds(first, BLOCK), :])
        s_ref[...] = dot(k_ref[0], queries, NT)
        s_ref[frames:padded, :] = jnp.full((padded - frames, 2 * BLOCK), NEG, F32)
        scores = s_ref[...]
        largest = jnp.max(scores, axis=0, keepdims=True)
        chances = jnp.exp2((scores - largest) * (SCALE * LOG2E))
        totals = jnp.sum(chances, axis=0, keepdims=True)
        number = row_lanes(first)
        inside = (number >= low) & (number < high)
        mixed = dot(vt[...], chances.astype(BF)) * jnp.where(inside, 1.0 / totals, 0.0)
        o_ref[pl.ds(first, BLOCK), :] += pick_heads(mixed).astype(BF)
        log_total = largest * (SCALE * LOG2E) + jnp.log(totals) * LOG2E
        lse_ref[0, block] = jnp.where(inside, log_total, lse_ref[0, block])
        return carry

    lax.fori_loop(start, stop, one_block, 0)

    @pl.when(doc == 1)
    def _():
        total[...] += dot(o_ref[...], wo_ref[here, :])

    @pl.when((doc == 1) & (pair == pl.num_programs(0) - 1))
    def _():
        split_out(scal, total, send_ref, keep_ref, rows // 2)


def cross_forward(scal, own, other, wq, bq, k, v, w_out, frames):
    half, width = own.shape
    rows = 2 * half
    _, padded, feats = k.shape
    pairs = feats // PAIR
    blocks = rows // BLOCK
    by_pair = pl.BlockSpec((rows, PAIR), lambda p, j, s: (0, p))
    keyed = pl.BlockSpec((1, padded, PAIR), lambda p, j, s: (j, 0, p))

    def kernel(*refs):
        cross_forward_kernel(*refs, frames=frames)

    return call(
        kernel,
        (pairs, 2),
        [
            whole(half, width),
            whole(half, width),
            whole(1, feats // 2, width),
            whole(1, feats // 2, width),
            pl.BlockSpec((1, PAIR), lambda p, j, s: (0, p)),
            keyed,
            keyed,
            whole(feats // 2, width),
            whole(feats // 2, width),
        ],
        [
            whole(rows, width),
            by_pair,
            by_pair,
            pl.BlockSpec((1, blocks, 1, 2 * BLOCK), lambda p, j, s: (p, 0, 0, 0)),
            whole(half, width),
            whole(half, width),
        ],
        [
            shaped((rows, width), BF),
            shaped((rows, feats), BF),
            shaped((rows, feats), BF),
            shaped((pairs, blocks, 1, 2 * BLOCK), F32),
            shaped((half, width), BF),
            shaped((half, width), F32),
        ],
        [
            pltpu.VMEM((rows, width), F32),
            pltpu.VMEM((PAIR, padded), BF),
            pltpu.VMEM((padded, 2 * BLOCK), F32),
            pltpu.VMEM((feats, width), BF),
            pltpu.VMEM((feats, width), BF),
        ],
        (4 * rows * width * feats + 4 * rows * padded * feats, rows * padded * 6, 14 << 20),
        "cross_forward",
    )(scal, own, other, *wq, bq, k, v, *w_out)


def cross_backward_kernel(
    scal, own_ref, other_ref, wo_own, wo_peer, q_ref, lse_ref, k_ref, v_ref, wq_own, wq_peer,
    dx_ref, dq_ref, dk_ref, dv_ref, sum_ref, send_ref, keep_ref,
    total, kt, do, dks, dvs, wq_ref, wo_ref, *, frames,
):
    pair, doc = pl.program_id(0), pl.program_id(1)
    rows = q_ref.shape[0]

    @pl.when((pair == 0) & (doc == 0))
    def _():
        join_halves(scal, own_ref, other_ref, dx_ref, rows // 2)
        join_weights(wq_own.at[0], wq_peer.at[0], wq_ref)
        join_weights(wo_own, wo_peer, wo_ref)
        total[...] = jnp.zeros_like(total)

    here = pair_rows(pair)

    @pl.when(doc == 0)
    def _():
        do[...] = dot(dx_ref[...], wo_ref[here, :], NT).astype(BF)
        dq_ref[...] = jnp.zeros_like(dq_ref)

    kt[...] = flip(k_ref[0])
    dks[...] = jnp.zeros_like(dks)
    dvs[...] = jnp.zeros_like(dvs)
    low, high, start, stop = block_span(scal, doc)

    def one_block(block, carry):
        first = pl.multiple_of(block * BLOCK, BLOCK)
        queries = two_heads(q_ref[pl.ds(first, BLOCK), :])
        grads = two_heads(do[pl.ds(first, BLOCK), :])
        number = row_lanes(first)
        inside = (number >= low) & (number < high)
        log_total = jnp.where(inside, lse_ref[0, block], BIG)
        chances = jnp.exp2(dot(k_ref[0], queries, NT) * (SCALE * LOG2E) - log_total)
        prob_grad = dot(v_ref[0], grads, NT)
        shared = jnp.sum(chances * prob_grad, axis=0, keepdims=True)
        score_grad = (chances * (prob_grad - shared)).astype(BF)
        dvs[...] += dot(chances.astype(BF), grads)
        dks[...] += dot(score_grad, queries)
        dq_ref[pl.ds(first, BLOCK), :] += (pick_heads(dot(kt[...], score_grad)) * SCALE).astype(BF)
        return carry

    lax.fori_loop(start, stop, one_block, 0)
    tail = jnp.zeros((dks.shape[0] - frames, PAIR), F32)
    dks[frames:, :] = tail
    dvs[frames:, :] = tail
    dk_ref[0] = (dks[...] * SCALE).T.astype(BF)
    dv_ref[0] = dvs[...].T.astype(BF)

    @pl.when(doc == 1)
    def _():
        sum_ref[...] = jnp.sum(dq_ref[...].astype(F32), axis=0, keepdims=True)
        total[...] += dot(dq_ref[...], wq_ref[here, :])

    @pl.when((doc == 1) & (pair == pl.num_programs(0) - 1))
    def _():
        split_out(scal, total, send_ref, keep_ref, rows // 2)


def cross_backward(scal, own, other, w_out, q, lse, k, v, wq, frames):
    half, width = own.shape
    rows = 2 * half
    _, padded, feats = k.shape
    pairs = feats // PAIR
    blocks = rows // BLOCK
    by_pair = pl.BlockSpec((rows, PAIR), lambda p, j, s: (0, p))
    keyed = pl.BlockSpec((1, padded, PAIR), lambda p, j, s: (j, 0, p))
    turned = pl.BlockSpec((1, PAIR, padded), lambda p, j, s: (j, p, 0))

    def kernel(*refs):
        cross_backward_kernel(*refs, frames=frames)

    return call(
        kernel,
        (pairs, 2),
        [
            whole(half, width),
            whole(half, width),
            whole(feats // 2, width),
            whole(feats // 2, width),
            by_pair,
            pl.BlockSpec((1, blocks, 1, 2 * BLOCK), lambda p, j, s: (p, 0, 0, 0)),
            keyed,
            keyed,
            whole(1, feats // 2, width),
            whole(1, feats // 2, width),
        ],
        [
            whole(rows, width),
            by_pair,
            turned,
            turned,
            pl.BlockSpec((1, PAIR), lambda p, j, s: (0, p)),
            whole(half, width),
            whole(half, width),
        ],
        [
            shaped((rows, width), BF),
            shaped((rows, feats), BF),
            shaped((2, feats, padded), BF),
            shaped((2, feats, padded), BF),
            shaped((1, feats), F32),
            shaped((half, width), BF),
            shaped((half, width), F32),
        ],
        [
            pltpu.VMEM((rows, width), F32),
            pltpu.VMEM((PAIR, padded), BF),
            pltpu.VMEM((rows, PAIR), BF),
            pltpu.VMEM((padded, PAIR), F32),
            pltpu.VMEM((padded, PAIR), F32),
            pltpu.VMEM((feats, width), BF),
            pltpu.VMEM((feats, width), BF),
        ],
        (4 * rows * width * feats + 10 * rows * padded * feats, rows * padded * 6, 18 << 20),
        "cross_backward",
    )(scal, own, other, *w_out, q, lse, k, v, *wq)


def place_rows(scal, refs, full_ref):
    core, chip, edge = scal[0], scal[1], scal[2]
    half = refs[0].shape[0]
    shift = full_ref.shape[0] - 2 * half
    for number, ref in enumerate(refs):
        which_chip = chip if number < 2 else 1 - chip
        which_core = core if number % 2 == 0 else 1 - core
        first = pl.multiple_of(which_chip * shift + which_core * half, 64)
        row = first + lax.broadcasted_iota(jnp.int32, (half, 1), 0)
        valid = (row < edge) == (which_chip == 0)
        full_ref[pl.ds(first, half), :] = jnp.where(
            valid, ref[...].astype(full_ref.dtype), full_ref[pl.ds(first, half), :]
        )


def place_kernel(scal, a_ref, b_ref, c_ref, d_ref, out_ref):
    place_rows(scal, (a_ref, b_ref, c_ref, d_ref), out_ref)


def place(scal, parts, length, dtype):
    half, width = parts[0].shape
    return call(
        place_kernel,
        (1,),
        [whole(half, width)] * 4,
        whole(length, width),
        shaped((length, width), dtype),
        [],
        (0, 0, 0),
        "place_rows",
    )(scal, *parts)


def feed_forward_kernel(
    scal, a_ref, b_ref, c_ref, d_ref, dy_ref, wi_ref, bi_ref, wo_ref,
    h_ref, g_ref, du_ref, dh_ref, sum_ref,
):
    step = pl.program_id(0)
    size = dy_ref.shape[0]

    @pl.when(step == 0)
    def _():
        place_rows(scal, (a_ref, b_ref, c_ref, d_ref), h_ref)
        sum_ref[...] = jnp.zeros_like(sum_ref)

    rows = h_ref[pl.ds(pl.multiple_of(step * size, size), size), :]
    value = dot(rows, wi_ref[...]) + bi_ref[...]
    normal = 0.5 + 0.5 * lax.erf(value * (0.5**0.5))
    g_ref[...] = (value * normal).astype(BF)
    density = jnp.exp2(value * value * (-0.5 * LOG2E)) * 0.3989422804014327
    grad = dot(dy_ref[...], wo_ref[...], NT) * (normal + value * density)
    low = grad.astype(BF)
    du_ref[...] = low
    sum_ref[...] += jnp.sum(low.astype(F32), axis=0, keepdims=True)
    dh_ref[...] = dot(low, wi_ref[...], NT)


def feed_forward(scal, parts, dy, w_in, b_in, w_out):
    length, width = dy.shape
    hidden = w_in.shape[1]
    half = parts[0].shape[0]
    size = 256
    return call(
        feed_forward_kernel,
        (length // size,),
        [whole(half, width)] * 4
        + [
            pl.BlockSpec((size, width), lambda i, s: (i, 0)),
            whole(width, hidden),
            whole(1, hidden),
            whole(hidden, width),
        ],
        [
            whole(length, width),
            pl.BlockSpec((size, hidden), lambda i, s: (i, 0)),
            pl.BlockSpec((size, hidden), lambda i, s: (i, 0)),
            pl.BlockSpec((size, width), lambda i, s: (i, 0)),
            whole(1, hidden),
        ],
        [
            shaped((length, width), BF),
            shaped((length, hidden), BF),
            shaped((length, hidden), BF),
            shaped((length, width), F32),
            shaped((1, hidden), F32),
        ],
        [],
        (6 * length * width * hidden, 2 * length * hidden, 14 << 20),
        "feed_forward",
    )(scal, *parts, dy, w_in, b_in, w_out)


def memory_back_kernel(scal, dk_ref, dv_ref, w_own, w_peer, send_ref, keep_ref, w_ref):
    core, chip = scal[0], scal[1]
    part = keep_ref.shape[2]
    frames = keep_ref.shape[3]

    @pl.when(pl.program_id(0) == 0)
    def _():
        for number in range(2):
            w_ref[number, :, : w_own.shape[1]] = flip(w_own[1 + number])
            w_ref[number, :, w_own.shape[1] :] = flip(w_peer[1 + number])

    dk = dk_ref[0]
    dv = dv_ref[0]
    for slot in range(2):
        which = chip if slot == 0 else 1 - chip
        near = pl.ds(pl.multiple_of((2 * which + core) * part, 64), part)
        far = pl.ds(pl.multiple_of((2 * which + 1 - core) * part, 64), part)
        keep = dot(w_ref[0, near, :], dk) + dot(w_ref[1, near, :], dv)
        keep_ref[slot, 0] = keep[:, :frames]
        send = dot(w_ref[0, far, :], dk) + dot(w_ref[1, far, :], dv)
        send_ref[slot, 0] = send[:, :frames].astype(BF)


def memory_back(scal, dk, dv, w_in, frames):
    _, feats, padded = dk.shape
    _, part, width = w_in[0].shape
    share = width // 4
    out = pl.BlockSpec((2, 1, share, frames), lambda j, s: (0, j, 0, 0))
    keyed = pl.BlockSpec((1, feats, padded), lambda j, s: (j, 0, 0))
    return call(
        memory_back_kernel,
        (2,),
        [keyed, keyed, whole(3, part, width), whole(3, part, width)],
        [out, out],
        [shaped((2, 2, share, frames), BF), shaped((2, 2, share, frames), F32)],
        [pltpu.VMEM((2, width, feats), BF)],
        (8 * frames * width * feats, 0, 14 << 20),
        "memory_back",
    )(scal, dk, dv, *w_in)


def memory_place_kernel(scal, keep_ref, got_ref, far_ref, out_ref):
    source = pl.program_id(0)

    @pl.when(source < 2)
    def _():
        out_ref[...] = (keep_ref[0] + got_ref[0].astype(F32)).astype(BF)

    @pl.when(source >= 2)
    def _():
        out_ref[...] = far_ref[...]


def memory_place(scal, keep, got, far):
    _, _, share, frames = keep.shape
    near = pl.BlockSpec((1, 1, share, frames), lambda i, s: (0, jnp.minimum(i, 1), 0, 0))
    return call(
        memory_place_kernel,
        (4,),
        [near, near, pl.BlockSpec((1, share, frames), lambda i, s: (jnp.maximum(i - 2, 0), 0, 0))],
        pl.BlockSpec((1, share, frames), lambda i, s: (s[9 + i], 0, 0)),
        shaped((4, share, frames), BF),
        [],
        (0, 0, 0),
        "memory_place",
    )(scal, keep, got, far)


def memory_weights_kernel(scal, mem_ref, dk_ref, dv_ref, gk_ref, gv_ref, sum_ref, gk, gv, tail_ref):
    doc = pl.program_id(0)
    frames = mem_ref.shape[1]
    body = frames // BLOCK * BLOCK

    @pl.when(doc == 0)
    def _():
        gk[...] = jnp.zeros_like(gk)
        gv[...] = jnp.zeros_like(gv)
        sum_ref[...] = jnp.zeros_like(sum_ref)
        tail_ref[...] = jnp.zeros_like(tail_ref)

    tail_ref[: frames - body, :] = mem_ref[0, body:, :]
    rows = mem_ref[0, :body, :]
    tail = tail_ref[...]
    gk[...] += dot(dk_ref[0, :, :body], rows) + dot(dk_ref[0, :, body:], tail)
    gv[...] += dot(dv_ref[0, :, :body], rows) + dot(dv_ref[0, :, body:], tail)
    ones = jnp.ones((8, dv_ref.shape[2]), BF)
    sum_ref[...] += dot(ones, dv_ref[0], NT)[0:1]

    @pl.when(doc == 1)
    def _():
        gk_ref[...] = gk[...].T
        gv_ref[...] = gv[...].T


def memory_weights(scal, memory, dk, dv):
    _, frames, width = memory.shape
    _, feats, padded = dk.shape
    keyed = pl.BlockSpec((1, feats, padded), lambda j, s: (j, 0, 0))
    return call(
        memory_weights_kernel,
        (2,),
        [pl.BlockSpec((1, frames, width), lambda j, s: (s[9 + j], 0, 0)), keyed, keyed],
        [whole(width, feats), whole(width, feats), whole(1, feats)],
        [shaped((width, feats), F32), shaped((width, feats), F32), shaped((1, feats), F32)],
        [
            pltpu.VMEM((feats, width), F32),
            pltpu.VMEM((feats, width), F32),
            pltpu.VMEM((BLOCK, width), BF),
        ],
        (8 * frames * width * feats, 0, 14 << 20),
        "memory_weights",
    )(scal, memory, dk, dv)


def per_device(
    inputs, memory, segments, documents, cotangent, norm_gain, norm_shift, attn_in, attn_bias,
    attn_out, cross_in, cross_bias, cross_out, fc_in, fc_in_bias, fc_out, out_bias, n_dp,
):
    length, width = inputs.shape
    docs, frames, _ = memory.shape
    padded = -(-frames // BLOCK) * BLOCK
    longest = length - 2 * (length // 5)
    rows = min(length, -(-longest // BLOCK) * BLOCK)
    half = rows // 2
    shift = length - rows
    slot = lax.axis_index("tensor")
    core, chip = slot % 2, slot // 2
    place_dp = lax.axis_index("dp")
    bits = n_dp.bit_length() - 1

    def swap(value, axis, bit):
        size = n_dp if axis == "dp" else 4
        return lax.ppermute(value, axis, [(i, i ^ bit) for i in range(size)])

    def to_core(value):
        return swap(value, "tensor", 1)

    def to_chip(value):
        return swap(value, "tensor", 2)

    numbers = jnp.arange(docs, dtype=jnp.int32)
    edges = jnp.sum((segments[None, :] < numbers[:, None]).astype(jnp.int32), axis=1)
    which = jnp.max(jnp.where(segments[None, :] == numbers[:, None], documents[None, :], 0), axis=1)
    which = which - place_dp * docs
    first_chip = chip == 0
    edge_one = jnp.where(first_chip, edges[1], edges[2] - shift)
    edge_two = jnp.where(first_chip, edges[2], edges[3] - shift)
    mine = jnp.where(first_chip, which, jnp.roll(which, 2))
    scal = jnp.concatenate(
        [
            jnp.stack(
                [
                    core,
                    chip,
                    edges[2],
                    edge_one,
                    edge_two,
                    jnp.where(first_chip, 0, edge_one),
                    jnp.where(first_chip, edge_one, edge_two),
                    jnp.where(first_chip, edge_one, edge_two),
                    jnp.where(first_chip, edge_two, rows),
                ]
            ),
            mine,
        ]
    ).astype(jnp.int32)

    def after(value, *earlier):
        return lax.optimization_barrier((value, earlier))[0]

    attn_in = jnp.swapaxes(attn_in, 1, 2)
    cross_in = jnp.swapaxes(cross_in, 1, 2)
    w_self = (attn_in, to_chip(attn_in))
    w_self_out = (attn_out, to_chip(attn_out))
    biases = jnp.concatenate([attn_bias, cross_bias], axis=0)
    biases = jnp.concatenate([biases, to_chip(biases)], axis=1)
    w_cross = (cross_in, to_chip(after(cross_in, w_self[1])))
    w_cross_out = (cross_out, to_chip(after(cross_out, w_self[1])))

    memory = with_layout_constraint(memory, Layout(major_to_minor=(0, 1, 2)))
    memory, peer_in = lax.optimization_barrier((memory, w_self[1]))
    w_self = (attn_in, peer_in)
    x_win = lax.dynamic_slice_in_dim(inputs, chip * shift, rows)
    dy_win = lax.dynamic_slice_in_dim(cotangent, chip * shift, rows)

    def row(matrix, index):
        return matrix[index : index + 1]

    h1, q1, k1, v1, o1, lse1, send, keep = self_forward(
        scal, x_win, row(norm_gain, 0), row(norm_shift, 0), w_self, biases[0:2], w_self_out
    )
    k2, v2 = memory_project(scal, memory, w_cross, biases[3:4], padded)
    x1, h2_own = add_norm(
        scal, x_win, keep, to_core(send), row(out_bias, 0), row(norm_gain, 1), row(norm_shift, 1), True
    )
    h2, q2, o2, lse2, send, keep = cross_forward(
        scal, h2_own, to_core(h2_own), w_cross, biases[2:3], k2, v2, w_cross_out, frames
    )
    x2, h3_own = add_norm(
        scal, x1, keep, to_core(send), row(out_bias, 1), row(norm_gain, 2), row(norm_shift, 2), False
    )

    def spread(value):
        far = to_chip(value)
        return (value, to_core(value), far, to_core(far))

    h3, g, du, dh3_part, fc_sum = feed_forward(
        scal, spread(h3_own), cotangent, fc_in, fc_in_bias[None], fc_out
    )

    def cut(value, which_chip, which_core):
        return lax.dynamic_slice_in_dim(value, which_chip * shift + which_core * half, half)

    def core_shares(value):
        send = jnp.stack([cut(value, chip, 1 - core), cut(value, 1 - chip, 1 - core)]).astype(BF)
        got = to_core(send).astype(F32)
        return cut(value, chip, core) + got[0], (cut(value, 1 - chip, core) + got[1]).astype(BF)

    near, far = core_shares(dh3_part)
    got = to_chip(far)
    near_out, far_out = core_shares(dot(g, fc_out))
    du, g_low = after((du, g), far)
    fc_in_grad, fc_out_grad = dot(h3, du, TN), dot(cotangent, g_low, TN)
    dx2, dx2_low, sums_three = norm_back(scal, dy_win, near, got, x2, row(norm_gain, 2), True, False)
    got_out = to_chip(after(far_out, got))

    def pick_bit(value, axis, bit):
        mine = (place_dp >> bit) & 1
        stay = lax.dynamic_index_in_dim(value, mine, axis, keepdims=False)
        return stay, lax.dynamic_index_in_dim(value, 1 - mine, axis, keepdims=False).astype(BF)

    def weights_chain(matrices, order, doubled):
        left = list(range(bits - 1, -1, -1))
        shape = (2,) * bits + (width // n_dp, matrices[0].shape[1])
        value = None
        for number, bit in enumerate(order):
            if bit == "chip":
                part = value.shape[-1] // 2
                got = yield value[..., part:].astype(BF), "tensor", 2
                value = value[..., :part] + got.astype(F32)
                continue
            axis = left.index(bit)
            left.remove(bit)
            if number == 0:
                both = [pick_bit(matrix.reshape(shape), axis, bit) for matrix in matrices]
                got = yield jnp.stack([send for _, send in both]), "dp", 1 << bit
                value = jnp.stack([stay + got[i].astype(F32) for i, (stay, _) in enumerate(both)])
            else:
                stay, send = pick_bit(value, 1 + axis, bit)
                got = yield send, "dp", 1 << bit
                value = stay + got.astype(F32)
        return value

    others = list(range(2, bits))
    mlp = weights_chain([fc_in_grad, fc_out_grad], [0, 1] + others, False)
    mlp_sent = next(mlp)
    mlp_got = swap(*mlp_sent)

    dx2_other = after(to_core(dx2_low), mlp_sent[0], far_out)
    dx2_full, dq2, dk2, dv2, q2_sum, send, keep = cross_backward(
        scal, dx2_low, dx2_other, w_cross_out, q2, lse2, k2, v2, w_cross, frames
    )
    gk, gv, v2_sum = memory_weights(scal, memory, dk2, dv2)
    cross = [
        weights_chain([gk, gv], [0, 1, "chip"] + others, True),
        weights_chain([dot(h2, dq2, TN), dot(dx2_full, o2, TN)], [1, 0, "chip"] + others, True),
    ]
    cross_sent = [next(chain) for chain in cross]
    cross_got = [swap(*sent) for sent in cross_sent]
    mlp_got, got_out = after((mlp_got, got_out), q2_sum)
    mlp_sent = mlp.send(mlp_got)
    mlp_got = swap(*mlp_sent)
    out_own = (x2 + (near_out + got_out.astype(F32)) + out_bias[2]).astype(BF)
    out_far = to_chip(out_own)

    dk2 = after(dk2, cross_sent[0][0], cross_sent[1][0], mlp_sent[0], out_own)
    mem_send, mem_keep = memory_back(scal, dk2, dv2, w_cross, frames)
    mem_got = to_core(mem_send)
    keep = after(keep, mem_send)
    dx1, dx1_low, sums_two = norm_back(
        scal, dx2, keep, to_core(send), x1, row(norm_gain, 1), False, False
    )
    mem_far = (mem_keep[1] + mem_got[1].astype(F32)).astype(BF)
    cross_got = after(cross_got, mem_send)
    cross_sent = [chain.send(got) for chain, got in zip(cross, cross_got)]
    cross_got = [swap(*sent) for sent in cross_sent]
    dx1_other = after(to_core(dx1_low), mem_far, cross_sent[0][0], cross_sent[1][0])
    dx1_full, dq1, dk1, dv1, self_sum, send, keep = self_backward(
        scal, dx1_low, dx1_other, w_self_out, q1, k1, v1, lse1, w_self
    )
    mlp_got, cross_got, out_far = after((mlp_got, cross_got, out_far), self_sum)
    own = [
        weights_chain([dot(h1, dk1, TN), dot(h1, dv1, TN)], [0, 1, "chip"] + others, True),
        weights_chain([dot(h1, dq1, TN), dot(dx1_full, o1, TN)], [1, 0, "chip"] + others, True),
    ]
    own_sent = [next(chain) for chain in own]
    keep = after(keep, own_sent[0][0], own_sent[1][0])
    input_own, input_low, sums_one = norm_back(
        scal, dx1, keep, to_core(send), x_win, row(norm_gain, 0), False, True
    )
    out_own, mlp_got, cross_got = after((out_own, mlp_got, cross_got), sums_one)
    mem_far = to_chip(mem_far)
    input_low = after(input_low, mem_far)

    def input_chain(value):
        far = yield value, "tensor", 2
        near, far_other = yield jnp.stack([value, far]), "tensor", 1
        return value, near, far, far_other

    def output_chain(value, far):
        near, far_other = yield jnp.stack([value, far]), "tensor", 1
        return value, near, far, far_other

    part = self_sum.shape[1] // 2

    def sums_chain():
        heads = jnp.concatenate([self_sum, q2_sum, v2_sum])
        sums = jnp.concatenate(
            [sums_one, sums_two, sums_three, jnp.pad(heads, ((0, 0), (0, width - 2 * part))), fc_sum]
        )
        number = jnp.arange(sums.shape[0])[:, None]
        near, far, far_other = yield sums, "tensor", (1, 2, 3)
        turned = jnp.where(number < 16, jnp.roll(far, -part, axis=1), 0.0)
        rows_sum = (sums + near) + (far + far_other)
        sums = jnp.where(number < 12, rows_sum, sums + turned)
        for bit in range(0, bits - 1, 2):
            one, two, three = yield sums, "dp", (1 << bit, 2 << bit, 3 << bit)
            sums = (sums + one) + (two + three)
        if bits % 2:
            got = yield sums, "dp", 1 << (bits - 1)
            sums = sums + got
        return sums

    chains = [
        (0, own[0], own_sent[0]),
        (0, own[1], own_sent[1]),
        (0, input_chain(input_low), None),
        (0, mlp, mlp.send(mlp_got)),
        (1, sums_chain(), None),
        (1, cross[0], cross[0].send(cross_got[0])),
        (1, cross[1], cross[1].send(cross_got[1])),
        (1, output_chain(out_own, out_far), None),
    ]

    def swap_all(value, axis, which):
        if isinstance(which, tuple):
            return tuple(swap(value, axis, bit) for bit in which)
        return swap(value, axis, which)

    results = [None] * len(chains)
    pending = {}
    number = 0
    while number < 2 or pending:
        for i, (start, chain, sent) in enumerate(chains):
            if start == number:
                pending[i] = next(chain) if sent is None else sent
        sends = lax.optimization_barrier(tuple(sent[0] for sent in pending.values()))
        gots = tuple(swap_all(value, *sent[1:]) for value, sent in zip(sends, pending.values()))
        gots = lax.optimization_barrier(gots)
        later = {}
        for i, got in zip(pending, gots):
            try:
                later[i] = chains[i][1].send(got)
            except StopIteration as stop:
                results[i] = stop.value
        pending = later
        number += 1
    own_share = results[0], results[1]
    input_grad = place(scal, results[2], length, F32)
    mlp_share = results[3]
    sums = results[4]
    cross_share = results[5], results[6]
    output = place(scal, results[7], length, BF)
    memory_grad = jnp.swapaxes(memory_place(scal, mem_keep, mem_got, mem_far), 1, 2)
    heads = sums[12:16, :part]

    def pick(*rows_of):
        return jnp.concatenate([sums[i : i + 1] for i in rows_of])

    return (
        output,
        input_grad,
        memory_grad,
        pick(0, 4, 8),
        pick(1, 5, 9),
        jnp.stack([own_share[1][0], own_share[0][0], own_share[0][1]]),
        heads[0:2],
        own_share[1][1].T,
        jnp.stack([cross_share[1][0], cross_share[0][0], cross_share[0][1]]),
        heads[2:4],
        cross_share[1][1].T,
        mlp_share[0],
        sums[16],
        mlp_share[1].T,
        pick(6, 10, 11),
    )


def solution(mesh):
    n_dp = mesh.shape["dp"]

    def run(*args):
        return per_device(*args, n_dp)

    return jax.shard_map(
        run,
        mesh=mesh,
        in_specs=(
            P("dp", None),
            P("dp", None, None),
            P("dp"),
            P("dp"),
            P("dp", None),
            P(),
            P(),
            P(None, None, "tensor"),
            P(None, "tensor"),
            P("tensor", None),
            P(None, None, "tensor"),
            P(None, "tensor"),
            P("tensor", None),
            P(None, "tensor"),
            P("tensor"),
            P("tensor", None),
            P(),
        ),
        out_specs=(
            P("dp", None),
            P("dp", None),
            P("dp", None, "tensor"),
            P(),
            P(),
            P(None, "dp", "tensor"),
            P(None, "tensor"),
            P("tensor", "dp"),
            P(None, "dp", "tensor"),
            P(None, "tensor"),
            P("tensor", "dp"),
            P("dp", "tensor"),
            P("tensor"),
            P("tensor", "dp"),
            P(),
        ),
        check_vma=False,
    )
```

```python
import jax
import jax.numpy as jnp
from jax import lax
from jax.experimental import pallas as pl
from jax.experimental.layout import Layout, with_layout_constraint
from jax.experimental.pallas import tpu as pltpu
from jax.sharding import PartitionSpec as P

HEAD = 64
PAIR = 2 * HEAD
BLOCK = 128
ROWS = 160
EPSILON = 1e-05
LOG2E = 1.4426950408889634
SCALE = HEAD ** (-0.5)
NEG = -1e30
BIG = 1e30
BF = jnp.bfloat16
F32 = jnp.float32
VMEM = 24 << 20
CROSS_VMEM = 40 << 20
SELF_VMEM = 32 << 20
WEIGHTS_VMEM = 32 << 20
PROJECT = 512
FEED = 256
COST = 4

NT = (((1,), (1,)), ((), ()))
NN = (((1,), (0,)), ((), ()))
TN = (((0,), (0,)), ((), ()))


def dot(left, right, dims=NN):
    return lax.dot_general(left, right, dims, preferred_element_type=F32)


def norm_parts(values):
    centred = values - jnp.mean(values, axis=-1, keepdims=True)
    inverse = lax.rsqrt(jnp.mean(centred * centred, axis=-1, keepdims=True) + EPSILON)
    return centred * inverse, inverse


def call(kernel, grid, in_specs, out_specs, out_shape, scratch, cost, name, vmem=VMEM):
    flops, exps, moved = cost
    return pl.pallas_call(
        kernel,
        grid_spec=pltpu.PrefetchScalarGridSpec(
            num_scalar_prefetch=1,
            grid=grid,
            in_specs=in_specs,
            out_specs=out_specs,
            scratch_shapes=scratch,
        ),
        out_shape=out_shape,
        compiler_params=pltpu.CompilerParams(
            dimension_semantics=("arbitrary",) * len(grid), vmem_limit_bytes=vmem
        ),
        cost_estimate=pl.CostEstimate(
            flops=COST * flops + 1, transcendentals=COST * exps, bytes_accessed=COST * moved + 1
        ),
        name=name,
    )


def whole(*shape):
    zeros = (0,) * len(shape)
    return pl.BlockSpec(shape, lambda *_: zeros)


def shaped(shape, dtype):
    return jax.ShapeDtypeStruct(shape, dtype)


def two_heads(rows):
    lane = lax.broadcasted_iota(jnp.int32, rows.shape, 1)
    zero = jnp.zeros_like(rows)
    return jnp.concatenate(
        [jnp.where(lane < HEAD, rows, zero), jnp.where(lane < HEAD, zero, rows)], axis=0
    )


def pick_heads(both):
    row = lax.broadcasted_iota(jnp.int32, (PAIR, BLOCK), 0)
    return jnp.where(row < HEAD, both[:, :BLOCK], both[:, BLOCK:]).T


def row_lanes(first):
    lane = lax.broadcasted_iota(jnp.int32, (1, 2 * BLOCK), 1)
    return first + jnp.where(lane < BLOCK, lane, lane - BLOCK)


def flip(matrix):
    return matrix.astype(F32).T.astype(BF)


def split_out(scal, total, send_ref, keep_ref, half):
    core = scal[0]
    here = pl.multiple_of(core * half, half)
    there = pl.multiple_of((1 - core) * half, half)
    keep_ref[...] = total[pl.ds(here, half), :]
    send_ref[...] = total[pl.ds(there, half), :].astype(BF)


def join_halves(scal, own_ref, other_ref, full_ref, half):
    core = scal[0]
    full_ref[pl.ds(pl.multiple_of(core * half, half), half), :] = own_ref[...]
    full_ref[pl.ds(pl.multiple_of((1 - core) * half, half), half), :] = other_ref[...]


def join_weights(own_ref, peer_ref, full_ref):
    part = own_ref.shape[-2]
    full_ref[..., :part, :] = own_ref[...]
    full_ref[..., part:, :] = peer_ref[...]


def join_stack(own_ref, peer_ref, full_ref):
    count, part, _ = own_ref.shape
    for number in range(count):
        first = 2 * part * number
        full_ref[first : first + part, :] = own_ref[number]
        full_ref[first + part : first + 2 * part, :] = peer_ref[number]


def put_weights(out_ref, group, rows):
    part = rows.shape[0] // 4
    for side in range(2):
        one = rows[side * part : (side + 1) * part]
        two = rows[(2 + side) * part : (3 + side) * part]
        out_ref[group, side] = jnp.concatenate([one, two], axis=0).T


def self_mask(scal, count, first):
    rows = row_lanes(first)
    edge_one, edge_two = scal[3], scal[4]
    begin = jnp.where(rows >= edge_two, edge_two, jnp.where(rows >= edge_one, edge_one, 0))
    keys = lax.broadcasted_iota(jnp.int32, (count, 2 * BLOCK), 0)
    return (keys >= begin) & (keys <= rows)


def self_forward_kernel(
    scal, x_ref, gain_ref, shift_ref, w_own, w_peer, b_ref, wo_own, wo_peer,
    h_ref, q_ref, k_ref, v_ref, o_ref, lse_ref, send_ref, keep_ref, total, vt, w_ref, wo_ref,
):
    rows = x_ref.shape[0]
    join_stack(w_own, w_peer, w_ref)
    join_weights(wo_own, wo_peer, wo_ref)
    normed, _ = norm_parts(x_ref[...].astype(F32))
    h_ref[...] = (normed * gain_ref[...] + shift_ref[...]).astype(BF)
    part = q_ref.shape[1]
    projected = dot(h_ref[...], w_ref[...], NT)
    q_ref[...] = (projected[:, :part] + b_ref[0:1, :]).astype(BF)
    k_ref[...] = projected[:, part : 2 * part].astype(BF)
    v_ref[...] = (projected[:, 2 * part :] + b_ref[1:2, :]).astype(BF)
    vt[...] = flip(v_ref[...])
    for block in range(rows // BLOCK):
        first = block * BLOCK
        count = first + BLOCK
        kept = self_mask(scal, count, first)
        for pair in range(part // PAIR):
            here = lanes(pair)
            queries = two_heads(q_ref[first : first + BLOCK, here])
            scores = jnp.where(kept, dot(k_ref[:count, here], queries, NT), NEG)
            largest = jnp.max(scores, axis=0, keepdims=True)
            chances = jnp.exp2((scores - largest) * (SCALE * LOG2E))
            totals = jnp.sum(chances, axis=0, keepdims=True)
            mixed = dot(vt[here, :count], chances.astype(BF)) * (1.0 / totals)
            o_ref[first : first + BLOCK, here] = pick_heads(mixed).astype(BF)
            lse_ref[pair, block] = largest * (SCALE * LOG2E) + jnp.log(totals) * LOG2E
    total[...] = dot(o_ref[...], wo_ref[...])
    split_out(scal, total, send_ref, keep_ref, rows // 2)


def self_forward(scal, x_win, gain, shift, w_in, bias, w_out):
    rows, width = x_win.shape
    part = w_out[0].shape[0]
    feats = 2 * part
    pairs = feats // PAIR
    blocks = rows // BLOCK
    return call(
        self_forward_kernel,
        (1,),
        [
            whole(rows, width),
            whole(1, width),
            whole(1, width),
            whole(3, part, width),
            whole(3, part, width),
            whole(2, feats),
            whole(part, width),
            whole(part, width),
        ],
        [whole(rows, width)]
        + [whole(rows, feats)] * 4
        + [whole(pairs, blocks, 1, 2 * BLOCK), whole(rows // 2, width), whole(rows // 2, width)],
        [shaped((rows, width), BF)]
        + [shaped((rows, feats), BF)] * 4
        + [
            shaped((pairs, blocks, 1, 2 * BLOCK), F32),
            shaped((rows // 2, width), BF),
            shaped((rows // 2, width), F32),
        ],
        [
            pltpu.VMEM((rows, width), F32),
            pltpu.VMEM((feats, rows), BF),
            pltpu.VMEM((3 * feats, width), BF),
            pltpu.VMEM((feats, width), BF),
        ],
        (8 * rows * width * feats + 4 * rows * rows * feats, rows * rows * 6, 12 << 20),
        "self_forward",
    )(scal, x_win, gain, shift, *w_in, bias, *w_out)


def self_backward_kernel(
    scal, own_ref, other_ref, wo_own, wo_peer, h_ref, q_ref, k_ref, v_ref, o_ref, lse_ref,
    w_own, w_peer, weights_ref, sum_ref, send_ref, keep_ref,
    dx_ref, grad_ref, total, kt, do, dks, dvs, w_ref, wo_ref,
):
    rows, feats = q_ref.shape
    join_halves(scal, own_ref, other_ref, dx_ref, rows // 2)
    join_stack(w_own, w_peer, w_ref)
    join_weights(wo_own, wo_peer, wo_ref)
    do[...] = dot(dx_ref[...], wo_ref[...], NT).astype(BF)
    kt[...] = flip(k_ref[...])
    for block in reversed(range(rows // BLOCK)):
        first = block * BLOCK
        count = first + BLOCK
        kept = self_mask(scal, count, first)
        for pair in range(feats // PAIR):
            here = lanes(pair)
            queries = two_heads(q_ref[first : first + BLOCK, here])
            grads = two_heads(do[first : first + BLOCK, here])
            scores = dot(k_ref[:count, here], queries, NT)
            chances = jnp.exp2(scores * (SCALE * LOG2E) - lse_ref[pair, block])
            chances = jnp.where(kept, chances, 0.0)
            prob_grad = dot(v_ref[:count, here], grads, NT)
            shared = jnp.sum(chances * prob_grad, axis=0, keepdims=True)
            score_grad = (chances * (prob_grad - shared)).astype(BF)
            dv = dot(chances.astype(BF), grads)
            dk = dot(score_grad, queries)
            if count == rows:
                dvs[:, here] = dv
                dks[:, here] = dk
            else:
                dvs[:count, here] += dv
                dks[:count, here] += dk
            turned = pick_heads(dot(kt[here, :count], score_grad)) * SCALE
            grad_ref[first : first + BLOCK, here] = turned.astype(BF)
    grad_ref[:, feats : 2 * feats] = (dks[...] * SCALE).astype(BF)
    grad_ref[:, 2 * feats :] = dvs[...].astype(BF)
    sum_ref[0:1, :] = jnp.sum(grad_ref[:, :feats].astype(F32), axis=0, keepdims=True)
    sum_ref[1:2, :] = jnp.sum(grad_ref[:, 2 * feats :].astype(F32), axis=0, keepdims=True)
    total[...] = dot(grad_ref[...], w_ref[...])
    split_out(scal, total, send_ref, keep_ref, rows // 2)
    hidden = h_ref[...]
    put_weights(weights_ref, 0, dot(grad_ref[:, : 2 * feats], hidden, TN))
    put_weights(
        weights_ref,
        1,
        jnp.concatenate(
            [dot(grad_ref[:, 2 * feats :], hidden, TN), dot(o_ref[...], dx_ref[...], TN)], axis=0
        ),
    )


def self_backward(scal, own, other, w_out, h, q, k, v, o, lse, w_in):
    rows, feats = q.shape
    width = own.shape[1]
    part = feats // 2
    pairs = feats // PAIR
    blocks = rows // BLOCK
    half = rows // 2
    return call(
        self_backward_kernel,
        (1,),
        [whole(half, width)] * 2
        + [whole(part, width)] * 2
        + [whole(rows, width)]
        + [whole(rows, feats)] * 4
        + [whole(pairs, blocks, 1, 2 * BLOCK)]
        + [whole(3, part, width)] * 2,
        [
            whole(2, 2, width, feats),
            whole(2, feats),
            whole(half, width),
            whole(half, width),
        ],
        [
            shaped((2, 2, width, feats), F32),
            shaped((2, feats), F32),
            shaped((half, width), BF),
            shaped((half, width), F32),
        ],
        [
            pltpu.VMEM((rows, width), BF),
            pltpu.VMEM((rows, 3 * feats), BF),
            pltpu.VMEM((rows, width), F32),
            pltpu.VMEM((feats, rows), BF),
            pltpu.VMEM((rows, feats), BF),
            pltpu.VMEM((rows, feats), F32),
            pltpu.VMEM((rows, feats), F32),
            pltpu.VMEM((3 * feats, width), BF),
            pltpu.VMEM((feats, width), BF),
        ],
        (8 * rows * width * feats + 10 * rows * rows * feats, rows * rows * 6, 14 << 20),
        "self_backward",
        SELF_VMEM,
    )(scal, own, other, *w_out, h, q, k, v, o, lse, *w_in)


def add_norm_kernel(scal, base_ref, keep_ref, got_ref, bias_ref, gain_ref, shift_ref, x_ref, h_ref):
    value = base_ref[...].astype(F32) + (keep_ref[...] + got_ref[...].astype(F32)) + bias_ref[...]
    x_ref[...] = value
    normed, _ = norm_parts(value)
    h_ref[...] = (normed * gain_ref[...] + shift_ref[...]).astype(BF)


def add_norm(scal, base, keep, got, bias, gain, shift, by_core):
    half, width = keep.shape
    steps = half // ROWS
    block = pl.BlockSpec((ROWS, width), lambda i, s: (i, 0))
    base_spec = pl.BlockSpec((ROWS, width), lambda i, s: (s[0] * steps + i, 0)) if by_core else block
    return call(
        add_norm_kernel,
        (steps,),
        [base_spec, block, block] + [whole(1, width)] * 3,
        [block] * 2,
        [shaped((half, width), F32), shaped((half, width), BF)],
        [],
        (0, 0, 0),
        "add_norm",
    )(scal, base, keep, got, bias, gain, shift)


def norm_back_kernel(scal, base_ref, keep_ref, got_ref, x_ref, gain_ref, dx_ref, low_ref, sum_ref):
    step, steps = pl.program_id(0), pl.num_programs(0)
    base = base_ref[...].astype(F32)
    grad = keep_ref[...] + got_ref[...].astype(F32)
    row = (scal[0] * steps + step) * ROWS + lax.broadcasted_iota(jnp.int32, (ROWS, 1), 0)
    valid = (row >= scal[5]) & (row < scal[8])
    grad = jnp.where(valid, grad, 0.0)
    base = jnp.where(valid, base, 0.0)
    normed, inverse = norm_parts(x_ref[...].astype(F32))
    scaled = grad * gain_ref[...]
    total = base + inverse * (
        scaled
        - jnp.mean(scaled, axis=-1, keepdims=True)
        - normed * jnp.mean(scaled * normed, axis=-1, keepdims=True)
    )
    dx_ref[...] = total
    low_ref[...] = total.astype(BF)

    @pl.when(step == 0)
    def _():
        sum_ref[...] = jnp.zeros_like(sum_ref)

    sum_ref[0:1, :] += jnp.sum(grad * normed, axis=0, keepdims=True)
    sum_ref[1:2, :] += jnp.sum(grad, axis=0, keepdims=True)
    sum_ref[2:3, :] += jnp.sum(total, axis=0, keepdims=True)
    sum_ref[3:4, :] += jnp.sum(base, axis=0, keepdims=True)


def norm_back(scal, base, keep, got, x, gain, base_by_core, x_by_core):
    half, width = keep.shape

    steps = half // ROWS
    block = pl.BlockSpec((ROWS, width), lambda i, s: (i, 0))
    cored = pl.BlockSpec((ROWS, width), lambda i, s: (s[0] * steps + i, 0))

    def spec(by_core):
        return cored if by_core else block

    return call(
        norm_back_kernel,
        (steps,),
        [spec(base_by_core), block, block, spec(x_by_core), whole(1, width)],
        [block, block, whole(4, width)],
        [shaped((half, width), F32), shaped((half, width), BF), shaped((4, width), F32)],
        [],
        (0, 0, 0),
        "norm_back",
    )(scal, base, keep, got, x, gain)


def pieces(total, size):
    return [(first, min(size, total - first)) for first in range(0, total, size)]


def memory_project_kernel(scal, mem_ref, w_own, w_peer, b_ref, k_ref, v_ref, w_ref):
    feats = k_ref.shape[2]

    @pl.when(pl.program_id(0) == 0)
    def _():
        for number in range(2):
            rows = slice(number * feats, (number + 1) * feats)
            join_weights(w_own.at[1 + number], w_peer.at[1 + number], w_ref.at[rows])

    frames = mem_ref.shape[1]
    padded = k_ref.shape[1]
    tail = padded - BLOCK
    k_ref[0, tail:padded, :] = jnp.zeros((BLOCK, k_ref.shape[2]), BF)
    v_ref[0, tail:padded, :] = jnp.zeros((BLOCK, k_ref.shape[2]), BF)
    for first, size in pieces(frames, PROJECT):
        both = dot(mem_ref[0, first : first + size, :], w_ref[...], NT)
        k_ref[0, first : first + size, :] = both[:, :feats].astype(BF)
        v_ref[0, first : first + size, :] = (both[:, feats:] + b_ref[...]).astype(BF)


def memory_project(scal, memory, w_kv, bias, padded):
    _, frames, width = memory.shape
    part = w_kv[0].shape[1]
    feats = 2 * part
    out = pl.BlockSpec((1, padded, feats), lambda j, s: (j, 0, 0))
    return call(
        memory_project_kernel,
        (2,),
        [
            pl.BlockSpec((1, frames, width), lambda j, s: (s[9 + j], 0, 0)),
            whole(3, part, width),
            whole(3, part, width),
            whole(1, feats),
        ],
        [out, out],
        [shaped((2, padded, feats), BF)] * 2,
        [pltpu.VMEM((2 * feats, width), BF)],
        (8 * frames * width * feats, 0, 12 << 20),
        "memory_project",
    )(scal, memory, *w_kv, bias)


def block_span(scal, doc):
    low, high = scal[5 + 2 * doc], scal[6 + 2 * doc]
    return low, high, low // BLOCK, (high + BLOCK - 1) // BLOCK


def lanes(pair):
    return slice(pair * PAIR, (pair + 1) * PAIR)


def cross_forward_kernel(
    scal, own_ref, other_ref, wq_own, wq_peer, bq_ref, k_ref, v_ref, wo_own, wo_peer,
    h_ref, q_ref, o_ref, lse_ref, send_ref, keep_ref, total, vt, s_ref, wq_ref, wo_ref, *, frames,
):
    doc = pl.program_id(0)
    rows, feats = q_ref.shape
    padded = k_ref.shape[1]

    @pl.when(doc == 0)
    def _():
        join_halves(scal, own_ref, other_ref, h_ref, rows // 2)
        join_weights(wq_own.at[0], wq_peer.at[0], wq_ref)
        join_weights(wo_own, wo_peer, wo_ref)
        q_ref[...] = (dot(h_ref[...], wq_ref[...], NT) + bq_ref[...]).astype(BF)
        o_ref[...] = jnp.zeros_like(o_ref)
        lse_ref[...] = jnp.zeros_like(lse_ref)

    vt[...] = flip(v_ref[0])
    low, high, start, stop = block_span(scal, doc)

    def one_block(block, carry):
        first = pl.multiple_of(block * BLOCK, BLOCK)
        number = row_lanes(first)
        inside = (number >= low) & (number < high)
        for pair in range(feats // PAIR):
            here = lanes(pair)
            queries = two_heads(q_ref[pl.ds(first, BLOCK), here])
            s_ref[pair] = dot(k_ref[0, :, here], queries, NT)
            s_ref[pair, frames:padded, :] = jnp.full((padded - frames, 2 * BLOCK), NEG, F32)
            scores = s_ref[pair]
            largest = jnp.max(scores, axis=0, keepdims=True)
            chances = jnp.exp2((scores - largest) * (SCALE * LOG2E))
            totals = jnp.sum(chances, axis=0, keepdims=True)
            mixed = dot(vt[here, :], chances.astype(BF)) * jnp.where(inside, 1.0 / totals, 0.0)
            o_ref[pl.ds(first, BLOCK), here] += pick_heads(mixed).astype(BF)
            log_total = largest * (SCALE * LOG2E) + jnp.log(totals) * LOG2E
            lse_ref[pair, block] = jnp.where(inside, log_total, lse_ref[pair, block])
        return carry

    lax.fori_loop(start, stop, one_block, 0)

    @pl.when(doc == 1)
    def _():
        total[...] = dot(o_ref[...], wo_ref[...])
        split_out(scal, total, send_ref, keep_ref, rows // 2)


def cross_forward(scal, own, other, wq, bq, k, v, w_out, frames):
    half, width = own.shape
    rows = 2 * half
    _, padded, feats = k.shape
    pairs = feats // PAIR
    blocks = rows // BLOCK
    keyed = pl.BlockSpec((1, padded, feats), lambda j, s: (j, 0, 0))

    def kernel(*refs):
        cross_forward_kernel(*refs, frames=frames)

    return call(
        kernel,
        (2,),
        [
            whole(half, width),
            whole(half, width),
            whole(1, feats // 2, width),
            whole(1, feats // 2, width),
            whole(1, feats),
            keyed,
            keyed,
            whole(feats // 2, width),
            whole(feats // 2, width),
        ],
        [
            whole(rows, width),
            whole(rows, feats),
            whole(rows, feats),
            whole(pairs, blocks, 1, 2 * BLOCK),
            whole(half, width),
            whole(half, width),
        ],
        [
            shaped((rows, width), BF),
            shaped((rows, feats), BF),
            shaped((rows, feats), BF),
            shaped((pairs, blocks, 1, 2 * BLOCK), F32),
            shaped((half, width), BF),
            shaped((half, width), F32),
        ],
        [
            pltpu.VMEM((rows, width), F32),
            pltpu.VMEM((feats, padded), BF),
            pltpu.VMEM((pairs, padded, 2 * BLOCK), F32),
            pltpu.VMEM((feats, width), BF),
            pltpu.VMEM((feats, width), BF),
        ],
        (4 * rows * width * feats + 4 * rows * padded * feats, rows * padded * 6, 14 << 20),
        "cross_forward",
        CROSS_VMEM,
    )(scal, own, other, *wq, bq, k, v, *w_out)


def cross_backward_kernel(
    scal, own_ref, other_ref, wo_own, wo_peer, q_ref, lse_ref, k_ref, v_ref, wq_own, wq_peer,
    dx_ref, dq_ref, dkv_ref, sum_ref, send_ref, keep_ref,
    total, kt, do, dks, dvs, wq_ref, wo_ref, *, frames,
):
    doc = pl.program_id(0)
    rows, feats = q_ref.shape
    padded = k_ref.shape[1]

    @pl.when(doc == 0)
    def _():
        join_halves(scal, own_ref, other_ref, dx_ref, rows // 2)
        join_weights(wq_own.at[0], wq_peer.at[0], wq_ref)
        join_weights(wo_own, wo_peer, wo_ref)
        do[...] = dot(dx_ref[...], wo_ref[...], NT).astype(BF)
        dq_ref[...] = jnp.zeros_like(dq_ref)

    kt[...] = flip(k_ref[0])
    dks[...] = jnp.zeros_like(dks)
    dvs[...] = jnp.zeros_like(dvs)
    low, high, start, stop = block_span(scal, doc)

    def one_block(block, carry):
        first = pl.multiple_of(block * BLOCK, BLOCK)
        number = row_lanes(first)
        inside = (number >= low) & (number < high)
        for pair in range(feats // PAIR):
            here = lanes(pair)
            queries = two_heads(q_ref[pl.ds(first, BLOCK), here])
            grads = two_heads(do[pl.ds(first, BLOCK), here])
            log_total = jnp.where(inside, lse_ref[pair, block], BIG)
            chances = jnp.exp2(dot(k_ref[0, :, here], queries, NT) * (SCALE * LOG2E) - log_total)
            prob_grad = dot(v_ref[0, :, here], grads, NT)
            shared = jnp.sum(chances * prob_grad, axis=0, keepdims=True)
            score_grad = (chances * (prob_grad - shared)).astype(BF)
            dvs[:, here] += dot(chances.astype(BF), grads)
            dks[:, here] += dot(score_grad, queries)
            turned = pick_heads(dot(kt[here, :], score_grad)) * SCALE
            dq_ref[pl.ds(first, BLOCK), here] += turned.astype(BF)
        return carry

    lax.fori_loop(start, stop, one_block, 0)
    tail = jnp.zeros((padded - frames, feats), F32)
    dks[frames:, :] = tail
    dvs[frames:, :] = tail
    dkv_ref[0, 0] = (dks[...] * SCALE).T.astype(BF)
    dkv_ref[0, 1] = dvs[...].T.astype(BF)

    @pl.when(doc == 1)
    def _():
        sum_ref[...] = jnp.sum(dq_ref[...].astype(F32), axis=0, keepdims=True)
        total[...] = dot(dq_ref[...], wq_ref[...])
        split_out(scal, total, send_ref, keep_ref, rows // 2)


def cross_backward(scal, own, other, w_out, q, lse, k, v, wq, frames):
    half, width = own.shape
    rows = 2 * half
    _, padded, feats = k.shape
    pairs = feats // PAIR
    blocks = rows // BLOCK
    keyed = pl.BlockSpec((1, padded, feats), lambda j, s: (j, 0, 0))

    def kernel(*refs):
        cross_backward_kernel(*refs, frames=frames)

    return call(
        kernel,
        (2,),
        [
            whole(half, width),
            whole(half, width),
            whole(feats // 2, width),
            whole(feats // 2, width),
            whole(rows, feats),
            whole(pairs, blocks, 1, 2 * BLOCK),
            keyed,
            keyed,
            whole(1, feats // 2, width),
            whole(1, feats // 2, width),
        ],
        [
            whole(rows, width),
            whole(rows, feats),
            pl.BlockSpec((1, 2, feats, padded), lambda j, s: (j, 0, 0, 0)),
            whole(1, feats),
            whole(half, width),
            whole(half, width),
        ],
        [
            shaped((rows, width), BF),
            shaped((rows, feats), BF),
            shaped((2, 2, feats, padded), BF),
            shaped((1, feats), F32),
            shaped((half, width), BF),
            shaped((half, width), F32),
        ],
        [
            pltpu.VMEM((rows, width), F32),
            pltpu.VMEM((feats, padded), BF),
            pltpu.VMEM((rows, feats), BF),
            pltpu.VMEM((padded, feats), F32),
            pltpu.VMEM((padded, feats), F32),
            pltpu.VMEM((feats, width), BF),
            pltpu.VMEM((feats, width), BF),
        ],
        (4 * rows * width * feats + 10 * rows * padded * feats, rows * padded * 6, 18 << 20),
        "cross_backward",
        CROSS_VMEM,
    )(scal, own, other, *w_out, q, lse, k, v, *wq)


def place_rows(scal, refs, full_ref):
    core, chip, edge = scal[0], scal[1], scal[2]
    half = refs[0].shape[0]
    shift = full_ref.shape[0] - 2 * half
    for number, ref in enumerate(refs):
        which_chip = chip if number < 2 else 1 - chip
        which_core = core if number % 2 == 0 else 1 - core
        first = pl.multiple_of(which_chip * shift + which_core * half, 64)
        row = first + lax.broadcasted_iota(jnp.int32, (half, 1), 0)
        valid = (row < edge) == (which_chip == 0)
        full_ref[pl.ds(first, half), :] = jnp.where(
            valid, ref[...].astype(full_ref.dtype), full_ref[pl.ds(first, half), :]
        )


def place_kernel(scal, a_ref, b_ref, c_ref, d_ref, out_ref):
    place_rows(scal, (a_ref, b_ref, c_ref, d_ref), out_ref)


def place(scal, parts, length, dtype):
    half, width = parts[0].shape
    return call(
        place_kernel,
        (1,),
        [whole(half, width)] * 4,
        whole(length, width),
        shaped((length, width), dtype),
        [],
        (0, 0, 0),
        "place_rows",
    )(scal, *parts)


def feed_forward_kernel(
    scal, a_ref, b_ref, c_ref, d_ref, dy_ref, wi_ref, bi_ref, wo_ref,
    h_ref, g_ref, du_ref, dh_ref, sum_ref,
):
    step = pl.program_id(0)
    size = dy_ref.shape[0]

    @pl.when(step == 0)
    def _():
        place_rows(scal, (a_ref, b_ref, c_ref, d_ref), h_ref)
        sum_ref[...] = jnp.zeros_like(sum_ref)

    rows = h_ref[pl.ds(pl.multiple_of(step * size, size), size), :]
    value = dot(rows, wi_ref[...]) + bi_ref[...]
    normal = 0.5 + 0.5 * lax.erf(value * (0.5**0.5))
    g_ref[...] = (value * normal).astype(BF)
    density = jnp.exp2(value * value * (-0.5 * LOG2E)) * 0.3989422804014327
    grad = dot(dy_ref[...], wo_ref[...], NT) * (normal + value * density)
    low = grad.astype(BF)
    du_ref[...] = low
    sum_ref[...] += jnp.sum(low.astype(F32), axis=0, keepdims=True)
    dh_ref[...] = dot(low, wi_ref[...], NT)


def feed_forward(scal, parts, dy, w_in, b_in, w_out):
    length, width = dy.shape
    hidden = w_in.shape[1]
    half = parts[0].shape[0]
    size = FEED
    return call(
        feed_forward_kernel,
        (length // size,),
        [whole(half, width)] * 4
        + [
            pl.BlockSpec((size, width), lambda i, s: (i, 0)),
            whole(width, hidden),
            whole(1, hidden),
            whole(hidden, width),
        ],
        [
            whole(length, width),
            pl.BlockSpec((size, hidden), lambda i, s: (i, 0)),
            pl.BlockSpec((size, hidden), lambda i, s: (i, 0)),
            pl.BlockSpec((size, width), lambda i, s: (i, 0)),
            whole(1, hidden),
        ],
        [
            shaped((length, width), BF),
            shaped((length, hidden), BF),
            shaped((length, hidden), BF),
            shaped((length, width), F32),
            shaped((1, hidden), F32),
        ],
        [],
        (6 * length * width * hidden, 2 * length * hidden, 14 << 20),
        "feed_forward",
    )(scal, *parts, dy, w_in, b_in, w_out)


def memory_back_kernel(scal, dkv_ref, w_own, w_peer, send_ref, keep_ref, w_ref, part_ref):
    core, chip = scal[0], scal[1]
    share = keep_ref.shape[2]
    frames = keep_ref.shape[3]
    part = w_own.shape[1]

    @pl.when(pl.program_id(0) == 0)
    def _():
        for number in range(2):
            for place, ref in enumerate((w_own, w_peer)):
                first = (2 * number + place) * part
                w_ref[:, first : first + part] = flip(ref[1 + number])

    dkv = dkv_ref[0].reshape(w_ref.shape[1], dkv_ref.shape[3])
    part_ref[...] = dot(w_ref[...], dkv)
    for slot in range(2):
        which = chip if slot == 0 else 1 - chip
        near = pl.ds(pl.multiple_of((2 * which + core) * share, 64), share)
        far = pl.ds(pl.multiple_of((2 * which + 1 - core) * share, 64), share)
        keep_ref[slot, 0] = part_ref[near, :frames]
        send_ref[slot, 0] = part_ref[far, :frames].astype(BF)


def memory_back(scal, dkv, w_in, frames):
    _, _, feats, padded = dkv.shape
    _, part, width = w_in[0].shape
    share = width // 4
    out = pl.BlockSpec((2, 1, share, frames), lambda j, s: (0, j, 0, 0))
    return call(
        memory_back_kernel,
        (2,),
        [
            pl.BlockSpec((1, 2, feats, padded), lambda j, s: (j, 0, 0, 0)),
            whole(3, part, width),
            whole(3, part, width),
        ],
        [out, out],
        [shaped((2, 2, share, frames), BF), shaped((2, 2, share, frames), F32)],
        [pltpu.VMEM((width, 2 * feats), BF), pltpu.VMEM((width, padded), F32)],
        (8 * frames * width * feats, 0, 14 << 20),
        "memory_back",
    )(scal, dkv, *w_in)


def memory_place_kernel(scal, keep_ref, got_ref, far_ref, out_ref):
    source = pl.program_id(0)

    @pl.when(source < 2)
    def _():
        out_ref[...] = (keep_ref[0] + got_ref[0].astype(F32)).astype(BF)

    @pl.when(source >= 2)
    def _():
        out_ref[...] = far_ref[...]


def memory_place(scal, keep, got, far):
    _, _, share, frames = keep.shape
    near = pl.BlockSpec((1, 1, share, frames), lambda i, s: (0, jnp.minimum(i, 1), 0, 0))
    return call(
        memory_place_kernel,
        (4,),
        [near, near, pl.BlockSpec((1, share, frames), lambda i, s: (jnp.maximum(i - 2, 0), 0, 0))],
        pl.BlockSpec((1, share, frames), lambda i, s: (s[9 + i], 0, 0)),
        shaped((4, share, frames), BF),
        [],
        (0, 0, 0),
        "memory_place",
    )(scal, keep, got, far)


def cross_weights_kernel(
    scal, mem_ref, dkv_ref, h_ref, dq_ref, dx_ref, o_ref, weights_ref, sum_ref, grads, tail_ref
):
    doc = pl.program_id(0)
    frames = mem_ref.shape[1]
    body = frames // BLOCK * BLOCK
    feats, padded = dkv_ref.shape[2:]

    @pl.when(doc == 0)
    def _():
        sum_ref[...] = jnp.zeros_like(sum_ref)
        tail_ref[...] = jnp.zeros_like(tail_ref)
        put_weights(
            weights_ref,
            1,
            jnp.concatenate([dot(dq_ref[...], h_ref[...], TN), dot(o_ref[...], dx_ref[...], TN)], axis=0),
        )

    tail_ref[: frames - body, :] = mem_ref[0, body:, :]
    rows = dkv_ref[0].reshape(2 * feats, padded)
    part = dot(rows[:, :body], mem_ref[0, :body, :]) + dot(rows[:, body:], tail_ref[...])
    sum_ref[...] += dot(jnp.ones((8, padded), BF), dkv_ref[0, 1], NT)[0:1]

    @pl.when(doc == 0)
    def _():
        grads[...] = part

    @pl.when(doc == 1)
    def _():
        put_weights(weights_ref, 0, grads[...] + part)


def cross_weights(scal, memory, dkv, h, dq, dx, o):
    _, frames, width = memory.shape
    _, _, feats, padded = dkv.shape
    rows = h.shape[0]
    return call(
        cross_weights_kernel,
        (2,),
        [
            pl.BlockSpec((1, frames, width), lambda j, s: (s[9 + j], 0, 0)),
            pl.BlockSpec((1, 2, feats, padded), lambda j, s: (j, 0, 0, 0)),
            whole(rows, width),
            whole(rows, feats),
            whole(rows, width),
            whole(rows, feats),
        ],
        [whole(2, 2, width, feats), whole(1, feats)],
        [shaped((2, 2, width, feats), F32), shaped((1, feats), F32)],
        [pltpu.VMEM((2 * feats, width), F32), pltpu.VMEM((BLOCK, width), BF)],
        (8 * frames * width * feats, 0, 14 << 20),
        "cross_weights",
        WEIGHTS_VMEM,
    )(scal, memory, dkv, h, dq, dx, o)


def per_device(
    inputs, memory, segments, documents, cotangent, norm_gain, norm_shift, attn_in, attn_bias,
    attn_out, cross_in, cross_bias, cross_out, fc_in, fc_in_bias, fc_out, out_bias, n_dp,
):
    length, width = inputs.shape
    docs, frames, _ = memory.shape
    padded = -(-frames // BLOCK) * BLOCK
    longest = length - 2 * (length // 5)
    rows = min(length, -(-longest // BLOCK) * BLOCK)
    half = rows // 2
    shift = length - rows
    slot = lax.axis_index("tensor")
    core, chip = slot % 2, slot // 2
    place_dp = lax.axis_index("dp")
    bits = n_dp.bit_length() - 1

    def swap(value, axis, bit):
        size = n_dp if axis == "dp" else 4
        return lax.ppermute(value, axis, [(i, i ^ bit) for i in range(size)])

    def to_core(value):
        return swap(value, "tensor", 1)

    def to_chip(value):
        return swap(value, "tensor", 2)

    numbers = jnp.arange(docs, dtype=jnp.int32)
    edges = jnp.sum((segments[None, :] < numbers[:, None]).astype(jnp.int32), axis=1)
    which = jnp.max(jnp.where(segments[None, :] == numbers[:, None], documents[None, :], 0), axis=1)
    which = which - place_dp * docs
    first_chip = chip == 0
    edge_one = jnp.where(first_chip, edges[1], edges[2] - shift)
    edge_two = jnp.where(first_chip, edges[2], edges[3] - shift)
    mine = jnp.where(first_chip, which, jnp.roll(which, 2))
    scal = jnp.concatenate(
        [
            jnp.stack(
                [
                    core,
                    chip,
                    edges[2],
                    edge_one,
                    edge_two,
                    jnp.where(first_chip, 0, edge_one),
                    jnp.where(first_chip, edge_one, edge_two),
                    jnp.where(first_chip, edge_one, edge_two),
                    jnp.where(first_chip, edge_two, rows),
                ]
            ),
            mine,
        ]
    ).astype(jnp.int32)

    def after(value, *earlier):
        return lax.optimization_barrier((value, earlier))[0]

    attn_in = jnp.swapaxes(attn_in, 1, 2)
    cross_in = jnp.swapaxes(cross_in, 1, 2)
    w_self = (attn_in, to_chip(attn_in))
    w_self_out = (attn_out, to_chip(attn_out))
    biases = jnp.concatenate([attn_bias, cross_bias], axis=0)
    biases = jnp.concatenate([biases, to_chip(biases)], axis=1)
    w_cross = (cross_in, to_chip(after(cross_in, w_self[1])))
    w_cross_out = (cross_out, to_chip(after(cross_out, w_self[1])))

    memory = with_layout_constraint(memory, Layout(major_to_minor=(0, 1, 2)))
    memory, peer_in = lax.optimization_barrier((memory, w_self[1]))
    w_self = (attn_in, peer_in)
    x_win = lax.dynamic_slice_in_dim(inputs, chip * shift, rows)
    dy_win = lax.dynamic_slice_in_dim(cotangent, chip * shift, rows)

    def row(matrix, index):
        return matrix[index : index + 1]

    h1, q1, k1, v1, o1, lse1, send, keep = self_forward(
        scal, x_win, row(norm_gain, 0), row(norm_shift, 0), w_self, biases[0:2], w_self_out
    )
    k2, v2 = memory_project(scal, memory, w_cross, biases[3:4], padded)
    x1, h2_own = add_norm(
        scal, x_win, keep, to_core(send), row(out_bias, 0), row(norm_gain, 1), row(norm_shift, 1), True
    )
    h2, q2, o2, lse2, send, keep = cross_forward(
        scal, h2_own, to_core(h2_own), w_cross, biases[2:3], k2, v2, w_cross_out, frames
    )
    x2, h3_own = add_norm(
        scal, x1, keep, to_core(send), row(out_bias, 1), row(norm_gain, 2), row(norm_shift, 2), False
    )

    def spread(value):
        far = to_chip(value)
        return (value, to_core(value), far, to_core(far))

    h3, g, du, dh3_part, fc_sum = feed_forward(
        scal, spread(h3_own), cotangent, fc_in, fc_in_bias[None], fc_out
    )

    def cut(value, which_chip, which_core):
        return lax.dynamic_slice_in_dim(value, which_chip * shift + which_core * half, half)

    def core_shares(value):
        send = jnp.stack([cut(value, chip, 1 - core), cut(value, 1 - chip, 1 - core)]).astype(BF)
        got = to_core(send).astype(F32)
        return cut(value, chip, core) + got[0], (cut(value, 1 - chip, core) + got[1]).astype(BF)

    near, far = core_shares(dh3_part)
    got = to_chip(far)
    near_out, far_out = core_shares(dot(g, fc_out))
    du, g_low = after((du, g), far)
    fc_in_grad, fc_out_grad = dot(h3, du, TN), dot(cotangent, g_low, TN)
    dx2, dx2_low, sums_three = norm_back(scal, dy_win, near, got, x2, row(norm_gain, 2), True, False)
    got_out = to_chip(after(far_out, got))

    def pick_bit(value, axis, bit):
        mine = (place_dp >> bit) & 1
        stay = lax.dynamic_index_in_dim(value, mine, axis, keepdims=False)
        return stay, lax.dynamic_index_in_dim(value, 1 - mine, axis, keepdims=False).astype(BF)

    others = list(range(2, bits))
    blocked = (2,) * bits + (width // n_dp,)

    def add(value, got):
        return value + got.astype(F32)

    def mlp_chain(matrices):
        value = jnp.stack(matrices).reshape(2, *blocked, -1)
        for number, bit in enumerate([0, 1] + others):
            axis = 1 + bits - 1 - bit if number == 0 else value.ndim - 3
            value, send = pick_bit(value, axis, bit)
            (got,) = yield [(send, "dp", 1 << bit)]
            value = add(value, got)
        return value

    def weights_chain(grads):
        grads = grads.reshape(2, 2, *blocked, -1)
        last = 1 + bits
        one, one_send = pick_bit(grads[0], last - 1, 0)
        two, two_send = pick_bit(grads[1], last - 2, 1)
        got = yield [(one_send, "dp", 1), (two_send, "dp", 2)]
        one, one_send = pick_bit(add(one, got[0]), last - 2, 1)
        two, two_send = pick_bit(add(two, got[1]), last - 2, 0)
        got = yield [(one_send, "dp", 2), (two_send, "dp", 1)]
        send = jnp.stack([one[1] + got[0][1].astype(F32), two[1] + got[1][1].astype(F32)]).astype(BF)
        stay = jnp.stack([add(one[0], got[0][0]), add(two[0], got[1][0])])
        (got,) = yield [(send, "tensor", 2)]
        value = add(stay, got)
        for bit in others:
            value, send = pick_bit(value, value.ndim - 3, bit)
            (got,) = yield [(send, "dp", 1 << bit)]
            value = add(value, got)
        return value

    def send_all(items):
        return [swap(*item) for item in items]

    mlp = mlp_chain([fc_in_grad, fc_out_grad])
    mlp_sent = next(mlp)
    mlp_got = send_all(mlp_sent)
    dx2_other = after(to_core(dx2_low), mlp_sent[0][0], far_out)
    dx2_full, dq2, dkv2, q2_sum, send, keep = cross_backward(
        scal, dx2_low, dx2_other, w_cross_out, q2, lse2, k2, v2, w_cross, frames
    )
    cross_grads, v2_sum = cross_weights(scal, memory, dkv2, h2, dq2, dx2_full, o2)
    cross = weights_chain(cross_grads)
    cross_sent = next(cross)
    cross_got = send_all(cross_sent)
    mlp_got, got_out = after((mlp_got, got_out), q2_sum)
    mlp_sent = mlp.send(mlp_got)
    mlp_got = send_all(mlp_sent)
    out_own = (x2 + (near_out + got_out.astype(F32)) + out_bias[2]).astype(BF)
    out_far = to_chip(out_own)

    dkv2 = after(dkv2, cross_sent[0][0], cross_sent[1][0], mlp_sent[0][0], out_own)
    mem_send, mem_keep = memory_back(scal, dkv2, w_cross, frames)
    mem_got = to_core(mem_send)
    keep = after(keep, mem_send)
    dx1, dx1_low, sums_two = norm_back(
        scal, dx2, keep, to_core(send), x1, row(norm_gain, 1), False, False
    )
    mem_far = (mem_keep[1] + mem_got[1].astype(F32)).astype(BF)
    cross_got = after(cross_got, mem_send)
    cross_sent = cross.send(cross_got)
    cross_got = send_all(cross_sent)
    dx1_other = after(to_core(dx1_low), mem_far, cross_sent[0][0], cross_sent[1][0])
    own_grads, self_sum, send, keep = self_backward(
        scal, dx1_low, dx1_other, w_self_out, h1, q1, k1, v1, o1, lse1, w_self
    )
    mem_far = to_chip(mem_far)
    cross_got, out_far = after((cross_got, out_far), self_sum)
    own = weights_chain(own_grads)
    own_sent = next(own)
    own_got = send_all(own_sent)
    keep = after(keep, own_sent[0][0], own_sent[1][0])
    input_own, input_low, sums_one = norm_back(
        scal, dx1, keep, to_core(send), x_win, row(norm_gain, 0), False, True
    )
    input_low = after(input_low, mem_far)
    out_own, out_far, mlp_got, cross_got = after((out_own, out_far, mlp_got, cross_got), sums_one)

    def input_chain(value):
        (far,) = yield [(value, "tensor", 2)]
        (got,) = yield [(jnp.stack([value, far]), "tensor", 1)]
        return value, got[0], far, got[1]

    def output_chain(value, far):
        (got,) = yield [(jnp.stack([value, far]), "tensor", 1)]
        return value, got[0], far, got[1]

    part = self_sum.shape[1] // 2

    def sums_chain():
        heads = jnp.concatenate([self_sum, q2_sum, v2_sum])
        sums = jnp.concatenate(
            [sums_one, sums_two, sums_three, jnp.pad(heads, ((0, 0), (0, width - 2 * part))), fc_sum]
        )
        number = jnp.arange(sums.shape[0])[:, None]
        (near,) = yield [(sums, "tensor", 1)]
        sums = sums + jnp.where(number < 12, near, 0.0)
        (far,) = yield [(sums, "tensor", 2)]
        turned = jnp.where(number < 16, jnp.roll(far, -part, axis=1), 0.0)
        sums = sums + jnp.where(number < 12, far, turned)
        start = bits % 2
        if start:
            (got,) = yield [(sums, "dp", 1)]
            sums = sums + got
        for bit in range(start, bits, 2):
            one, two, three = yield [(sums, "dp", which << bit) for which in (1, 2, 3)]
            sums = (sums + one) + (two + three)
        return sums

    chains = [
        (0, own, own_sent, own_got),
        (0, input_chain(input_low), None, None),
        (0, sums_chain(), None, None),
        (0, output_chain(out_own, out_far), None, None),
        (1, cross, None, cross_got),
        (2, mlp, None, mlp_got),
    ]
    results = [None] * len(chains)
    pending, came = {}, {}
    number = 0
    while number < 3 or pending:
        for i, (start, chain, sent, got) in enumerate(chains):
            if start == number:
                if sent is not None:
                    came[i] = got
                else:
                    pending[i] = next(chain) if got is None else chain.send(got)
        if number == 0:
            pending = {i: items for i, items in pending.items()}
        values = lax.optimization_barrier([[item[0] for item in items] for items in pending.values()])
        for i, held in zip(pending, values):
            came[i] = [swap(value, *item[1:]) for value, item in zip(held, pending[i])]
        came = lax.optimization_barrier(came)
        pending = {}
        for i, got in came.items():
            try:
                pending[i] = chains[i][1].send(got)
            except StopIteration as stop:
                results[i] = stop.value
        came = {}
        number += 1
    own_share, input_parts, sums, output_parts, cross_share, mlp_share = results
    input_grad = place(scal, input_parts, length, F32)
    output = place(scal, output_parts, length, BF)
    memory_grad = jnp.swapaxes(memory_place(scal, mem_keep, mem_got, mem_far), 1, 2)
    heads = sums[12:16, :part]

    def pick(*rows_of):
        return jnp.concatenate([sums[i : i + 1] for i in rows_of])

    return (
        output,
        input_grad,
        memory_grad,
        pick(0, 4, 8),
        pick(1, 5, 9),
        jnp.stack([own_share[0, :, :part], own_share[0, :, part:], own_share[1, :, :part]]),
        heads[0:2],
        own_share[1, :, part:].T,
        jnp.stack([cross_share[1, :, :part], cross_share[0, :, :part], cross_share[0, :, part:]]),
        heads[2:4],
        cross_share[1, :, part:].T,
        mlp_share[0],
        sums[16],
        mlp_share[1].T,
        pick(6, 10, 11),
    )


def solution(mesh):
    n_dp = mesh.shape["dp"]

    def run(*args):
        return per_device(*args, n_dp)

    return jax.shard_map(
        run,
        mesh=mesh,
        in_specs=(
            P("dp", None),
            P("dp", None, None),
            P("dp"),
            P("dp"),
            P("dp", None),
            P(),
            P(),
            P(None, None, "tensor"),
            P(None, "tensor"),
            P("tensor", None),
            P(None, None, "tensor"),
            P(None, "tensor"),
            P("tensor", None),
            P(None, "tensor"),
            P("tensor"),
            P("tensor", None),
            P(),
        ),
        out_specs=(
            P("dp", None),
            P("dp", None),
            P("dp", None, "tensor"),
            P(),
            P(),
            P(None, "dp", "tensor"),
            P(None, "tensor"),
            P("tensor", "dp"),
            P(None, "dp", "tensor"),
            P(None, "tensor"),
            P("tensor", "dp"),
            P("dp", "tensor"),
            P("tensor"),
            P("tensor", "dp"),
            P(),
        ),
        check_vma=False,
    )
```

```python
import jax
import jax.numpy as jnp
from jax import lax
from jax.experimental import pallas as pl
from jax.experimental.layout import Layout, with_layout_constraint
from jax.experimental.pallas import tpu as pltpu
from jax.sharding import PartitionSpec as P

HEAD = 64
PAIR = 2 * HEAD
BLOCK = 128
ROWS = 160
EPSILON = 1e-05
LOG2E = 1.4426950408889634
SCALE = HEAD ** (-0.5)
NEG = -1e30
BIG = 1e30
BF = jnp.bfloat16
F32 = jnp.float32
VMEM = 20 << 20
SMALL_VMEM = 12 << 20
OUT_ROUND = 2
CROSS_VMEM = 28 << 20
SELF_VMEM = 20 << 20
WEIGHTS_VMEM = 20 << 20
PROJECT = 512
FEED = 256
COST = 4

NT = (((1,), (1,)), ((), ()))
NN = (((1,), (0,)), ((), ()))
TN = (((0,), (0,)), ((), ()))


def dot(left, right, dims=NN):
    return lax.dot_general(left, right, dims, preferred_element_type=F32)


def norm_parts(values):
    centred = values - jnp.mean(values, axis=-1, keepdims=True)
    inverse = lax.rsqrt(jnp.mean(centred * centred, axis=-1, keepdims=True) + EPSILON)
    return centred * inverse, inverse


def call(kernel, grid, in_specs, out_specs, out_shape, scratch, cost, name, vmem=VMEM):
    flops, exps, moved = cost
    return pl.pallas_call(
        kernel,
        grid_spec=pltpu.PrefetchScalarGridSpec(
            num_scalar_prefetch=1,
            grid=grid,
            in_specs=in_specs,
            out_specs=out_specs,
            scratch_shapes=scratch,
        ),
        out_shape=out_shape,
        compiler_params=pltpu.CompilerParams(
            dimension_semantics=("arbitrary",) * len(grid), vmem_limit_bytes=vmem
        ),
        cost_estimate=pl.CostEstimate(
            flops=COST * flops + 1, transcendentals=COST * exps, bytes_accessed=COST * moved + 1
        ),
        name=name,
    )


def whole(*shape):
    zeros = (0,) * len(shape)
    return pl.BlockSpec(shape, lambda *_: zeros)


def shaped(shape, dtype):
    return jax.ShapeDtypeStruct(shape, dtype)


def two_heads(rows):
    lane = lax.broadcasted_iota(jnp.int32, rows.shape, 1)
    zero = jnp.zeros_like(rows)
    return jnp.concatenate(
        [jnp.where(lane < HEAD, rows, zero), jnp.where(lane < HEAD, zero, rows)], axis=0
    )


def pick_heads(both):
    row = lax.broadcasted_iota(jnp.int32, (PAIR, BLOCK), 0)
    return jnp.where(row < HEAD, both[:, :BLOCK], both[:, BLOCK:]).T


def row_lanes(first):
    lane = lax.broadcasted_iota(jnp.int32, (1, 2 * BLOCK), 1)
    return first + jnp.where(lane < BLOCK, lane, lane - BLOCK)


def flip(matrix):
    return matrix.astype(F32).T.astype(BF)


def split_out(scal, total, send_ref, keep_ref, half):
    core = scal[0]
    here = pl.multiple_of(core * half, half)
    there = pl.multiple_of((1 - core) * half, half)
    keep_ref[...] = total[pl.ds(here, half), :]
    send_ref[...] = total[pl.ds(there, half), :].astype(BF)


def join_halves(scal, own_ref, other_ref, full_ref, half):
    core = scal[0]
    full_ref[pl.ds(pl.multiple_of(core * half, half), half), :] = own_ref[...]
    full_ref[pl.ds(pl.multiple_of((1 - core) * half, half), half), :] = other_ref[...]


def join_weights(own_ref, peer_ref, full_ref):
    part = own_ref.shape[-2]
    full_ref[..., :part, :] = own_ref[...]
    full_ref[..., part:, :] = peer_ref[...]


def join_stack(own_ref, peer_ref, full_ref):
    count, part, _ = own_ref.shape
    for number in range(count):
        first = 2 * part * number
        full_ref[first : first + part, :] = own_ref[number]
        full_ref[first + part : first + 2 * part, :] = peer_ref[number]


def put_weights(scal, out_ref, send_ref, group, rows):
    part = rows.shape[0] // 4
    count, size = out_ref.shape[2:4]
    for side in range(2):
        one = rows[side * part : (side + 1) * part]
        two = rows[(2 + side) * part : (3 + side) * part]
        turned = jnp.concatenate([one, two], axis=0).T
        for block in range(count):
            out_ref[group, side, block] = turned[block * size : (block + 1) * size]
        for rest in range(count // 4):
            for other in range(2):
                where = 2 * other + 1 - scal[13] if group == 0 else 2 * (1 - scal[14]) + other
                send_ref[side, rest, other] = out_ref[group, side, 4 * rest + where].astype(BF)


def weights_specs(width, feats, n_dp):
    size = width // n_dp
    full = (2, 2, n_dp, size, feats)
    half = (2, n_dp // 4, 2, size, feats)
    return (
        [whole(*full), whole(*half), whole(*half)],
        [shaped(full, F32), shaped(half, BF), shaped(half, BF)],
    )


def shares_one_kernel(scal, full_ref, one_ref, two_ref, stay_ref, one_send, two_send):
    low, high = scal[13], scal[14]
    for side in range(2):
        for rest in range(one_ref.shape[1]):
            first = 4 * rest

            def one_sum(bit):
                return full_ref[0, side, first + 2 * bit + low] + one_ref[side, rest, bit].astype(F32)

            def two_sum(bit):
                return full_ref[1, side, first + 2 * high + bit] + two_ref[side, rest, bit].astype(F32)

            stay_ref[0, side, rest] = one_sum(high)
            one_send[side, rest] = one_sum(1 - high).astype(BF)
            stay_ref[1, side, rest] = two_sum(low)
            two_send[side, rest] = two_sum(1 - low).astype(BF)


def shares_one(scal, full, one, two):
    _, _, count, size, feats = full.shape
    stay = (2, 2, count // 4, size, feats)
    send = (2, count // 4, size, feats)
    return call(
        shares_one_kernel,
        (1,),
        [whole(*full.shape), whole(*one.shape), whole(*one.shape)],
        [whole(*stay), whole(*send), whole(*send)],
        [shaped(stay, F32), shaped(send, BF), shaped(send, BF)],
        [],
        (0, 0, 0),
        "shares_one",
        SMALL_VMEM,
    )(scal, full, one, two)


def shares_two_kernel(scal, stay_ref, one_ref, two_ref, near_ref, far_ref):
    for group, got in enumerate((one_ref, two_ref)):
        near_ref[group] = stay_ref[group, 0] + got[0].astype(F32)
        far_ref[group] = (stay_ref[group, 1] + got[1].astype(F32)).astype(BF)


def shares_two(scal, stay, one, two):
    out = (2, *stay.shape[2:])
    return call(
        shares_two_kernel,
        (1,),
        [whole(*stay.shape), whole(*one.shape), whole(*one.shape)],
        [whole(*out), whole(*out)],
        [shaped(out, F32), shaped(out, BF)],
        [],
        (0, 0, 0),
        "shares_two",
        SMALL_VMEM,
    )(scal, stay, one, two)


def self_mask(scal, count, first):
    rows = row_lanes(first)
    edge_one, edge_two = scal[3], scal[4]
    begin = jnp.where(rows >= edge_two, edge_two, jnp.where(rows >= edge_one, edge_one, 0))
    keys = lax.broadcasted_iota(jnp.int32, (count, 2 * BLOCK), 0)
    return (keys >= begin) & (keys <= rows)


def self_forward_kernel(
    scal, x_ref, gain_ref, shift_ref, w_own, w_peer, b_ref,
    h_ref, q_ref, k_ref, v_ref, o_ref, lse_ref, vt, w_ref,
):
    rows = x_ref.shape[0]
    join_stack(w_own, w_peer, w_ref)
    normed, _ = norm_parts(x_ref[...].astype(F32))
    h_ref[...] = (normed * gain_ref[...] + shift_ref[...]).astype(BF)
    part = q_ref.shape[1]
    projected = dot(h_ref[...], w_ref[...], NT)
    q_ref[...] = (projected[:, :part] + b_ref[0:1, :]).astype(BF)
    k_ref[...] = projected[:, part : 2 * part].astype(BF)
    v_ref[...] = (projected[:, 2 * part :] + b_ref[1:2, :]).astype(BF)
    vt[...] = flip(v_ref[...])
    for block in range(rows // BLOCK):
        first = block * BLOCK
        count = first + BLOCK
        kept = self_mask(scal, count, first)
        for pair in range(part // PAIR):
            here = lanes(pair)
            queries = two_heads(q_ref[first : first + BLOCK, here])
            scores = jnp.where(kept, dot(k_ref[:count, here], queries, NT), NEG)
            largest = jnp.max(scores, axis=0, keepdims=True)
            chances = jnp.exp2((scores - largest) * (SCALE * LOG2E))
            totals = jnp.sum(chances, axis=0, keepdims=True)
            mixed = dot(vt[here, :count], chances.astype(BF)) * (1.0 / totals)
            o_ref[first : first + BLOCK, here] = pick_heads(mixed).astype(BF)
            lse_ref[pair, block] = largest * (SCALE * LOG2E) + jnp.log(totals) * LOG2E


def project_out_kernel(scal, o_ref, wo_own, wo_peer, send_ref, keep_ref, total):
    part = wo_own.shape[0]
    wo = jnp.concatenate([wo_own[...], wo_peer[...]], axis=0)
    total[...] = dot(o_ref[...], wo)
    split_out(scal, total, send_ref, keep_ref, o_ref.shape[0] // 2)


def project_out(scal, mixed, w_out):
    rows, feats = mixed.shape
    part, width = w_out[0].shape
    half = rows // 2
    return call(
        project_out_kernel,
        (1,),
        [whole(rows, feats), whole(part, width), whole(part, width)],
        [whole(half, width)] * 2,
        [shaped((half, width), BF), shaped((half, width), F32)],
        [pltpu.VMEM((rows, width), F32)],
        (0, 0, 0),
        "project_out",
        SMALL_VMEM,
    )(scal, mixed, *w_out)


def self_forward(scal, x_win, gain, shift, w_in, bias):
    rows, width = x_win.shape
    part = w_in[0].shape[1]
    feats = 2 * part
    pairs = feats // PAIR
    blocks = rows // BLOCK
    return call(
        self_forward_kernel,
        (1,),
        [
            whole(rows, width),
            whole(1, width),
            whole(1, width),
            whole(3, part, width),
            whole(3, part, width),
            whole(2, feats),
        ],
        [whole(rows, width)]
        + [whole(rows, feats)] * 4
        + [whole(pairs, blocks, 1, 2 * BLOCK)],
        [shaped((rows, width), BF)]
        + [shaped((rows, feats), BF)] * 4
        + [shaped((pairs, blocks, 1, 2 * BLOCK), F32)],
        [
            pltpu.VMEM((feats, rows), BF),
            pltpu.VMEM((3 * feats, width), BF),
        ],
        (8 * rows * width * feats + 4 * rows * rows * feats, rows * rows * 6, 12 << 20),
        "self_forward",
    )(scal, x_win, gain, shift, *w_in, bias)


def self_backward_kernel(
    scal, own_ref, other_ref, wo_own, wo_peer, h_ref, q_ref, k_ref, v_ref, o_ref, lse_ref,
    w_own, w_peer, weights_ref, one_ref, two_ref, sum_ref, send_ref, keep_ref,
    dx_ref, grad_ref, total, kt, do, dks, dvs, w_ref, wo_ref,
):
    rows, feats = q_ref.shape
    join_halves(scal, own_ref, other_ref, dx_ref, rows // 2)
    join_stack(w_own, w_peer, w_ref)
    join_weights(wo_own, wo_peer, wo_ref)
    do[...] = dot(dx_ref[...], wo_ref[...], NT).astype(BF)
    kt[...] = flip(k_ref[...])
    for block in reversed(range(rows // BLOCK)):
        first = block * BLOCK
        count = first + BLOCK
        kept = self_mask(scal, count, first)
        for pair in range(feats // PAIR):
            here = lanes(pair)
            queries = two_heads(q_ref[first : first + BLOCK, here])
            grads = two_heads(do[first : first + BLOCK, here])
            scores = dot(k_ref[:count, here], queries, NT)
            chances = jnp.exp2(scores * (SCALE * LOG2E) - lse_ref[pair, block])
            chances = jnp.where(kept, chances, 0.0)
            prob_grad = dot(v_ref[:count, here], grads, NT)
            shared = jnp.sum(chances * prob_grad, axis=0, keepdims=True)
            score_grad = (chances * (prob_grad - shared)).astype(BF)
            dv = dot(chances.astype(BF), grads)
            dk = dot(score_grad, queries)
            if count == rows:
                dvs[:, here] = dv
                dks[:, here] = dk
            else:
                dvs[:count, here] += dv
                dks[:count, here] += dk
            turned = pick_heads(dot(kt[here, :count], score_grad)) * SCALE
            grad_ref[first : first + BLOCK, here] = turned.astype(BF)
    grad_ref[:, feats : 2 * feats] = (dks[...] * SCALE).astype(BF)
    grad_ref[:, 2 * feats :] = dvs[...].astype(BF)
    sum_ref[0:1, :] = jnp.sum(grad_ref[:, :feats].astype(F32), axis=0, keepdims=True)
    sum_ref[1:2, :] = jnp.sum(grad_ref[:, 2 * feats :].astype(F32), axis=0, keepdims=True)
    total[...] = dot(grad_ref[...], w_ref[...])
    split_out(scal, total, send_ref, keep_ref, rows // 2)
    hidden = h_ref[...]
    put_weights(scal, weights_ref, one_ref, 0, dot(grad_ref[:, : 2 * feats], hidden, TN))
    put_weights(
        scal,
        weights_ref,
        two_ref,
        1,
        jnp.concatenate(
            [dot(grad_ref[:, 2 * feats :], hidden, TN), dot(o_ref[...], dx_ref[...], TN)], axis=0
        ),
    )


def self_backward(scal, own, other, w_out, h, q, k, v, o, lse, w_in, n_dp):
    rows, feats = q.shape
    width = own.shape[1]
    part = feats // 2
    pairs = feats // PAIR
    blocks = rows // BLOCK
    half = rows // 2
    specs, shapes = weights_specs(width, feats, n_dp)
    return call(
        self_backward_kernel,
        (1,),
        [whole(half, width)] * 2
        + [whole(part, width)] * 2
        + [whole(rows, width)]
        + [whole(rows, feats)] * 4
        + [whole(pairs, blocks, 1, 2 * BLOCK)]
        + [whole(3, part, width)] * 2,
        specs
        + [
            whole(2, feats),
            whole(half, width),
            whole(half, width),
        ],
        shapes
        + [
            shaped((2, feats), F32),
            shaped((half, width), BF),
            shaped((half, width), F32),
        ],
        [
            pltpu.VMEM((rows, width), BF),
            pltpu.VMEM((rows, 3 * feats), BF),
            pltpu.VMEM((rows, width), F32),
            pltpu.VMEM((feats, rows), BF),
            pltpu.VMEM((rows, feats), BF),
            pltpu.VMEM((rows, feats), F32),
            pltpu.VMEM((rows, feats), F32),
            pltpu.VMEM((3 * feats, width), BF),
            pltpu.VMEM((feats, width), BF),
        ],
        (8 * rows * width * feats + 10 * rows * rows * feats, rows * rows * 6, 14 << 20),
        "self_backward",
        SELF_VMEM,
    )(scal, own, other, *w_out, h, q, k, v, o, lse, *w_in)


def add_norm_kernel(scal, base_ref, keep_ref, got_ref, bias_ref, gain_ref, shift_ref, x_ref, h_ref):
    value = base_ref[...].astype(F32) + (keep_ref[...] + got_ref[...].astype(F32)) + bias_ref[...]
    x_ref[...] = value
    normed, _ = norm_parts(value)
    h_ref[...] = (normed * gain_ref[...] + shift_ref[...]).astype(BF)


def add_norm(scal, base, keep, got, bias, gain, shift, by_core):
    half, width = keep.shape
    steps = half // ROWS
    block = pl.BlockSpec((ROWS, width), lambda i, s: (i, 0))
    base_spec = pl.BlockSpec((ROWS, width), lambda i, s: (s[0] * steps + i, 0)) if by_core else block
    return call(
        add_norm_kernel,
        (steps,),
        [base_spec, block, block] + [whole(1, width)] * 3,
        [block] * 2,
        [shaped((half, width), F32), shaped((half, width), BF)],
        [],
        (0, 0, 0),
        "add_norm",
        SMALL_VMEM,
    )(scal, base, keep, got, bias, gain, shift)


def norm_back_more_kernel(
    scal, base_ref, keep_ref, got_ref, x_ref, gain_ref, more_ref, dx_ref, low_ref, sum_ref
):
    norm_back_body(
        scal, base_ref, keep_ref[0] + more_ref[0].astype(F32), got_ref, x_ref, gain_ref,
        dx_ref, low_ref, sum_ref,
    )


def norm_back_kernel(scal, base_ref, keep_ref, got_ref, x_ref, gain_ref, dx_ref, low_ref, sum_ref):
    norm_back_body(
        scal, base_ref, keep_ref[...], got_ref, x_ref, gain_ref, dx_ref, low_ref, sum_ref
    )


def norm_back_body(scal, base_ref, keep, got_ref, x_ref, gain_ref, dx_ref, low_ref, sum_ref):
    step, steps = pl.program_id(0), pl.num_programs(0)
    base = base_ref[...].astype(F32)
    grad = keep + got_ref[...].astype(F32)
    row = (scal[0] * steps + step) * ROWS + lax.broadcasted_iota(jnp.int32, (ROWS, 1), 0)
    valid = (row >= scal[5]) & (row < scal[8])
    grad = jnp.where(valid, grad, 0.0)
    base = jnp.where(valid, base, 0.0)
    normed, inverse = norm_parts(x_ref[...].astype(F32))
    scaled = grad * gain_ref[...]
    total = base + inverse * (
        scaled
        - jnp.mean(scaled, axis=-1, keepdims=True)
        - normed * jnp.mean(scaled * normed, axis=-1, keepdims=True)
    )
    dx_ref[...] = total
    low_ref[...] = total.astype(BF)

    @pl.when(step == 0)
    def _():
        sum_ref[...] = jnp.zeros_like(sum_ref)

    sum_ref[0:1, :] += jnp.sum(grad * normed, axis=0, keepdims=True)
    sum_ref[1:2, :] += jnp.sum(grad, axis=0, keepdims=True)
    sum_ref[2:3, :] += jnp.sum(total, axis=0, keepdims=True)
    sum_ref[3:4, :] += jnp.sum(base, axis=0, keepdims=True)


def norm_back(scal, base, keep, got, x, gain, base_by_core, x_by_core, more=None, cost=0):
    half, width = got.shape

    steps = half // ROWS
    block = pl.BlockSpec((ROWS, width), lambda i, s: (i, 0))
    cored = pl.BlockSpec((ROWS, width), lambda i, s: (s[0] * steps + i, 0))

    stacked = pl.BlockSpec((1, ROWS, width), lambda i, s: (0, i, 0))

    def spec(by_core):
        return cored if by_core else block

    return call(
        norm_back_kernel if more is None else norm_back_more_kernel,
        (steps,),
        [
            spec(base_by_core),
            block if more is None else stacked,
            block,
            spec(x_by_core),
            whole(1, width),
        ]
        + [stacked] * (more is not None),
        [block, block, whole(4, width)],
        [shaped((half, width), F32), shaped((half, width), BF), shaped((4, width), F32)],
        [],
        (0, 0, cost),
        "norm_back",
        SMALL_VMEM,
    )(scal, base, keep, got, x, gain, *([] if more is None else [more]))


def pieces(total, size):
    return [(first, min(size, total - first)) for first in range(0, total, size)]


def memory_project_kernel(scal, mem_ref, w_own, w_peer, b_ref, k_ref, v_ref, w_ref):
    feats = k_ref.shape[2]

    @pl.when(pl.program_id(0) == 0)
    def _():
        for number in range(2):
            rows = slice(number * feats, (number + 1) * feats)
            join_weights(w_own.at[1 + number], w_peer.at[1 + number], w_ref.at[rows])

    frames = mem_ref.shape[1]
    padded = k_ref.shape[1]
    tail = padded - BLOCK
    k_ref[0, tail:padded, :] = jnp.zeros((BLOCK, k_ref.shape[2]), BF)
    v_ref[0, tail:padded, :] = jnp.zeros((BLOCK, k_ref.shape[2]), BF)
    for first, size in pieces(frames, PROJECT):
        both = dot(mem_ref[0, first : first + size, :], w_ref[...], NT)
        k_ref[0, first : first + size, :] = both[:, :feats].astype(BF)
        v_ref[0, first : first + size, :] = (both[:, feats:] + b_ref[...]).astype(BF)


def memory_project(scal, memory, w_kv, bias, padded):
    _, frames, width = memory.shape
    part = w_kv[0].shape[1]
    feats = 2 * part
    out = pl.BlockSpec((1, padded, feats), lambda j, s: (j, 0, 0))
    return call(
        memory_project_kernel,
        (2,),
        [
            pl.BlockSpec((1, frames, width), lambda j, s: (s[9 + j], 0, 0)),
            whole(3, part, width),
            whole(3, part, width),
            whole(1, feats),
        ],
        [out, out],
        [shaped((2, padded, feats), BF)] * 2,
        [pltpu.VMEM((2 * feats, width), BF)],
        (8 * frames * width * feats, 0, 12 << 20),
        "memory_project",
    )(scal, memory, *w_kv, bias)


def block_span(scal, doc):
    low, high = scal[5 + 2 * doc], scal[6 + 2 * doc]
    return low, high, low // BLOCK, (high + BLOCK - 1) // BLOCK


def lanes(pair):
    return slice(pair * PAIR, (pair + 1) * PAIR)


def cross_forward_kernel(
    scal, own_ref, other_ref, wq_own, wq_peer, bq_ref, k_ref, v_ref, wo_own, wo_peer,
    h_ref, q_ref, o_ref, lse_ref, send_ref, keep_ref, total, vt, s_ref, wq_ref, wo_ref, *, frames,
):
    doc = pl.program_id(0)
    rows, feats = q_ref.shape
    padded = k_ref.shape[1]

    @pl.when(doc == 0)
    def _():
        join_halves(scal, own_ref, other_ref, h_ref, rows // 2)
        join_weights(wq_own.at[0], wq_peer.at[0], wq_ref)
        join_weights(wo_own, wo_peer, wo_ref)
        q_ref[...] = (dot(h_ref[...], wq_ref[...], NT) + bq_ref[...]).astype(BF)
        o_ref[...] = jnp.zeros_like(o_ref)
        lse_ref[...] = jnp.zeros_like(lse_ref)

    vt[...] = flip(v_ref[0])
    low, high, start, stop = block_span(scal, doc)

    def one_block(block, carry):
        first = pl.multiple_of(block * BLOCK, BLOCK)
        number = row_lanes(first)
        inside = (number >= low) & (number < high)
        for pair in range(feats // PAIR):
            here = lanes(pair)
            queries = two_heads(q_ref[pl.ds(first, BLOCK), here])
            s_ref[pair] = dot(k_ref[0, :, here], queries, NT)
            s_ref[pair, frames:padded, :] = jnp.full((padded - frames, 2 * BLOCK), NEG, F32)
            scores = s_ref[pair]
            largest = jnp.max(scores, axis=0, keepdims=True)
            chances = jnp.exp2((scores - largest) * (SCALE * LOG2E))
            totals = jnp.sum(chances, axis=0, keepdims=True)
            mixed = dot(vt[here, :], chances.astype(BF)) * jnp.where(inside, 1.0 / totals, 0.0)
            o_ref[pl.ds(first, BLOCK), here] += pick_heads(mixed).astype(BF)
            log_total = largest * (SCALE * LOG2E) + jnp.log(totals) * LOG2E
            lse_ref[pair, block] = jnp.where(inside, log_total, lse_ref[pair, block])
        return carry

    lax.fori_loop(start, stop, one_block, 0)

    @pl.when(doc == 1)
    def _():
        total[...] = dot(o_ref[...], wo_ref[...])
        split_out(scal, total, send_ref, keep_ref, rows // 2)


def cross_forward(scal, own, other, wq, bq, k, v, w_out, frames):
    half, width = own.shape
    rows = 2 * half
    _, padded, feats = k.shape
    pairs = feats // PAIR
    blocks = rows // BLOCK
    keyed = pl.BlockSpec((1, padded, feats), lambda j, s: (j, 0, 0))

    def kernel(*refs):
        cross_forward_kernel(*refs, frames=frames)

    return call(
        kernel,
        (2,),
        [
            whole(half, width),
            whole(half, width),
            whole(1, feats // 2, width),
            whole(1, feats // 2, width),
            whole(1, feats),
            keyed,
            keyed,
            whole(feats // 2, width),
            whole(feats // 2, width),
        ],
        [
            whole(rows, width),
            whole(rows, feats),
            whole(rows, feats),
            whole(pairs, blocks, 1, 2 * BLOCK),
            whole(half, width),
            whole(half, width),
        ],
        [
            shaped((rows, width), BF),
            shaped((rows, feats), BF),
            shaped((rows, feats), BF),
            shaped((pairs, blocks, 1, 2 * BLOCK), F32),
            shaped((half, width), BF),
            shaped((half, width), F32),
        ],
        [
            pltpu.VMEM((rows, width), F32),
            pltpu.VMEM((feats, padded), BF),
            pltpu.VMEM((pairs, padded, 2 * BLOCK), F32),
            pltpu.VMEM((feats, width), BF),
            pltpu.VMEM((feats, width), BF),
        ],
        (4 * rows * width * feats + 4 * rows * padded * feats, rows * padded * 6, 14 << 20),
        "cross_forward",
        CROSS_VMEM,
    )(scal, own, other, *wq, bq, k, v, *w_out)


def cross_backward_kernel(
    scal, own_ref, other_ref, wo_own, wo_peer, q_ref, lse_ref, k_ref, v_ref, wq_own, wq_peer,
    dx_ref, dq_ref, dkv_ref, sum_ref, send_ref, keep_ref,
    total, kt, do, dks, dvs, wq_ref, wo_ref, *, frames,
):
    doc = pl.program_id(0)
    rows, feats = q_ref.shape
    padded = k_ref.shape[1]

    @pl.when(doc == 0)
    def _():
        join_halves(scal, own_ref, other_ref, dx_ref, rows // 2)
        join_weights(wq_own.at[0], wq_peer.at[0], wq_ref)
        join_weights(wo_own, wo_peer, wo_ref)
        do[...] = dot(dx_ref[...], wo_ref[...], NT).astype(BF)
        dq_ref[...] = jnp.zeros_like(dq_ref)

    kt[...] = flip(k_ref[0])
    dks[...] = jnp.zeros_like(dks)
    dvs[...] = jnp.zeros_like(dvs)
    low, high, start, stop = block_span(scal, doc)

    def one_block(block, carry):
        first = pl.multiple_of(block * BLOCK, BLOCK)
        number = row_lanes(first)
        inside = (number >= low) & (number < high)
        for pair in range(feats // PAIR):
            here = lanes(pair)
            queries = two_heads(q_ref[pl.ds(first, BLOCK), here])
            grads = two_heads(do[pl.ds(first, BLOCK), here])
            log_total = jnp.where(inside, lse_ref[pair, block], BIG)
            chances = jnp.exp2(dot(k_ref[0, :, here], queries, NT) * (SCALE * LOG2E) - log_total)
            prob_grad = dot(v_ref[0, :, here], grads, NT)
            shared = jnp.sum(chances * prob_grad, axis=0, keepdims=True)
            score_grad = (chances * (prob_grad - shared)).astype(BF)
            dvs[:, here] += dot(chances.astype(BF), grads)
            dks[:, here] += dot(score_grad, queries)
            turned = pick_heads(dot(kt[here, :], score_grad)) * SCALE
            dq_ref[pl.ds(first, BLOCK), here] += turned.astype(BF)
        return carry

    lax.fori_loop(start, stop, one_block, 0)
    tail = jnp.zeros((padded - frames, feats), F32)
    dks[frames:, :] = tail
    dvs[frames:, :] = tail
    dkv_ref[0, 0] = (dks[...] * SCALE).T.astype(BF)
    dkv_ref[0, 1] = dvs[...].T.astype(BF)

    @pl.when(doc == 1)
    def _():
        sum_ref[...] = jnp.sum(dq_ref[...].astype(F32), axis=0, keepdims=True)
        total[...] = dot(dq_ref[...], wq_ref[...])
        split_out(scal, total, send_ref, keep_ref, rows // 2)


def cross_backward(scal, own, other, w_out, q, lse, k, v, wq, frames):
    half, width = own.shape
    rows = 2 * half
    _, padded, feats = k.shape
    pairs = feats // PAIR
    blocks = rows // BLOCK
    keyed = pl.BlockSpec((1, padded, feats), lambda j, s: (j, 0, 0))

    def kernel(*refs):
        cross_backward_kernel(*refs, frames=frames)

    return call(
        kernel,
        (2,),
        [
            whole(half, width),
            whole(half, width),
            whole(feats // 2, width),
            whole(feats // 2, width),
            whole(rows, feats),
            whole(pairs, blocks, 1, 2 * BLOCK),
            keyed,
            keyed,
            whole(1, feats // 2, width),
            whole(1, feats // 2, width),
        ],
        [
            whole(rows, width),
            whole(rows, feats),
            pl.BlockSpec((1, 2, feats, padded), lambda j, s: (j, 0, 0, 0)),
            whole(1, feats),
            whole(half, width),
            whole(half, width),
        ],
        [
            shaped((rows, width), BF),
            shaped((rows, feats), BF),
            shaped((2, 2, feats, padded), BF),
            shaped((1, feats), F32),
            shaped((half, width), BF),
            shaped((half, width), F32),
        ],
        [
            pltpu.VMEM((rows, width), F32),
            pltpu.VMEM((feats, padded), BF),
            pltpu.VMEM((rows, feats), BF),
            pltpu.VMEM((padded, feats), F32),
            pltpu.VMEM((padded, feats), F32),
            pltpu.VMEM((feats, width), BF),
            pltpu.VMEM((feats, width), BF),
        ],
        (4 * rows * width * feats + 10 * rows * padded * feats, rows * padded * 6, 18 << 20),
        "cross_backward",
        CROSS_VMEM,
    )(scal, own, other, *w_out, q, lse, k, v, *wq)


def place_rows(scal, refs, full_ref):
    core, chip, edge = scal[0], scal[1], scal[2]
    half = refs[0].shape[-2]
    shift = full_ref.shape[0] - 2 * half
    for number, ref in enumerate(refs):
        which_chip = chip if number < 2 else 1 - chip
        which_core = core if number % 2 == 0 else 1 - core
        first = pl.multiple_of(which_chip * shift + which_core * half, 64)
        row = first + lax.broadcasted_iota(jnp.int32, (half, 1), 0)
        valid = (row < edge) == (which_chip == 0)
        part = (ref[...] if ref.ndim == 2 else ref[0]).astype(full_ref.dtype)
        full_ref[pl.ds(first, half), :] = jnp.where(valid, part, full_ref[pl.ds(first, half), :])


def place_kernel(scal, a_ref, b_ref, c_ref, d_ref, out_ref):
    place_rows(scal, (a_ref, b_ref, c_ref, d_ref), out_ref)


def place(scal, own, far, got, length, dtype):
    half, width = own.shape
    near_half = pl.BlockSpec((1, half, width), lambda *_: (0, 0, 0))
    far_half = pl.BlockSpec((1, half, width), lambda *_: (1, 0, 0))
    return call(
        place_kernel,
        (1,),
        [whole(half, width), near_half, whole(half, width), far_half],
        whole(length, width),
        shaped((length, width), dtype),
        [],
        (0, 0, 0),
        "place_rows",
        SMALL_VMEM,
    )(scal, own, got, far, got)


def window_shares(scal, full_ref, send_ref, keep_ref):
    core, chip = scal[0], scal[1]
    half = keep_ref.shape[1]
    shift = full_ref.shape[0] - 2 * half
    for slot in range(2):
        first = (chip if slot == 0 else 1 - chip) * shift
        near = pl.multiple_of(first + core * half, 64)
        far = pl.multiple_of(first + (1 - core) * half, 64)
        keep_ref[slot] = full_ref[pl.ds(near, half), :]
        send_ref[slot] = full_ref[pl.ds(far, half), :].astype(BF)


def second_product_kernel(scal, g_ref, w_ref, send_ref, keep_ref, full_ref):
    full_ref[...] = dot(g_ref[...], w_ref[...])
    window_shares(scal, full_ref, send_ref, keep_ref)


def second_product(scal, g, w_out, half):
    length, hidden = g.shape
    width = w_out.shape[1]
    return call(
        second_product_kernel,
        (1,),
        [whole(length, hidden), whole(hidden, width)],
        [whole(2, half, width)] * 2,
        [shaped((2, half, width), BF), shaped((2, half, width), F32)],
        [pltpu.VMEM((length, width), F32)],
        (0, 0, 0),
        "second_product",
    )(scal, g, w_out)


def fold_kernel(scal, keep_ref, got_ref, out_ref):
    out_ref[...] = (keep_ref[0] + got_ref[0].astype(F32)).astype(BF)


def fold(scal, keep, got):
    second = pl.BlockSpec((1, *keep.shape[1:]), lambda i, s: (1, *(0,) * (keep.ndim - 1)))
    return call(
        fold_kernel,
        (1,),
        [second, second],
        whole(*keep.shape[1:]),
        shaped(keep.shape[1:], BF),
        [],
        (0, 0, 0),
        "fold",
        SMALL_VMEM,
    )(scal, keep, got)


def output_rows_kernel(scal, x_ref, keep_ref, near_ref, far_ref, bias_ref, out_ref):
    value = keep_ref[0] + near_ref[0].astype(F32) + far_ref[...].astype(F32)
    out_ref[...] = (x_ref[...] + value + bias_ref[...]).astype(BF)


def output_rows(scal, x, keep, near, far, bias):
    half, width = x.shape
    first = pl.BlockSpec((1, half, width), lambda i, s: (0, 0, 0))
    return call(
        output_rows_kernel,
        (1,),
        [whole(half, width), first, first, whole(half, width), whole(1, width)],
        whole(half, width),
        shaped((half, width), BF),
        [],
        (0, 0, 0),
        "output_rows",
        SMALL_VMEM,
    )(scal, x, keep, near, far, bias)


def feed_forward_kernel(
    scal, a_ref, b_ref, c_ref, d_ref, dy_ref, wi_ref, bi_ref, wo_ref,
    h_ref, g_ref, du_ref, send_ref, keep_ref, sum_ref, dh_ref,
):
    step = pl.program_id(0)
    size = dy_ref.shape[0]

    @pl.when(step == 0)
    def _():
        place_rows(scal, (a_ref, b_ref, c_ref, d_ref), h_ref)
        sum_ref[...] = jnp.zeros_like(sum_ref)

    rows = h_ref[pl.ds(pl.multiple_of(step * size, size), size), :]
    value = dot(rows, wi_ref[...]) + bi_ref[...]
    normal = 0.5 + 0.5 * lax.erf(value * (0.5**0.5))
    g_ref[...] = (value * normal).astype(BF)
    density = jnp.exp2(value * value * (-0.5 * LOG2E)) * 0.3989422804014327
    grad = dot(dy_ref[...], wo_ref[...], NT) * (normal + value * density)
    low = grad.astype(BF)
    du_ref[...] = low
    sum_ref[...] += jnp.sum(low.astype(F32), axis=0, keepdims=True)
    dh_ref[pl.ds(pl.multiple_of(step * size, size), size), :] = dot(low, wi_ref[...], NT)

    @pl.when(step == pl.num_programs(0) - 1)
    def _():
        window_shares(scal, dh_ref, send_ref, keep_ref)


def feed_forward(scal, parts, dy, w_in, b_in, w_out):
    length, width = dy.shape
    hidden = w_in.shape[1]
    half = parts[0].shape[0]
    size = FEED
    return call(
        feed_forward_kernel,
        (length // size,),
        [whole(half, width)] * 4
        + [
            pl.BlockSpec((size, width), lambda i, s: (i, 0)),
            whole(width, hidden),
            whole(1, hidden),
            whole(hidden, width),
        ],
        [
            whole(length, width),
            pl.BlockSpec((size, hidden), lambda i, s: (i, 0)),
            pl.BlockSpec((size, hidden), lambda i, s: (i, 0)),
            whole(2, half, width),
            whole(2, half, width),
            whole(1, hidden),
        ],
        [
            shaped((length, width), BF),
            shaped((length, hidden), BF),
            shaped((length, hidden), BF),
            shaped((2, half, width), BF),
            shaped((2, half, width), F32),
            shaped((1, hidden), F32),
        ],
        [pltpu.VMEM((length, width), F32)],
        (6 * length * width * hidden, 2 * length * hidden, 14 << 20),
        "feed_forward",
    )(scal, *parts, dy, w_in, b_in, w_out)


def memory_back_kernel(scal, dkv_ref, w_own, w_peer, send_ref, keep_ref, w_ref, part_ref):
    core, chip = scal[0], scal[1]
    share = keep_ref.shape[2]
    frames = keep_ref.shape[3]
    part = w_own.shape[1]

    @pl.when(pl.program_id(0) == 0)
    def _():
        for number in range(2):
            for place, ref in enumerate((w_own, w_peer)):
                first = (2 * number + place) * part
                w_ref[:, first : first + part] = flip(ref[1 + number])

    dkv = dkv_ref[0].reshape(w_ref.shape[1], dkv_ref.shape[3])
    part_ref[...] = dot(w_ref[...], dkv)
    for slot in range(2):
        which = chip if slot == 0 else 1 - chip
        near = pl.ds(pl.multiple_of((2 * which + core) * share, 64), share)
        far = pl.ds(pl.multiple_of((2 * which + 1 - core) * share, 64), share)
        keep_ref[slot, 0] = part_ref[near, :frames]
        send_ref[slot, 0] = part_ref[far, :frames].astype(BF)


def memory_back(scal, dkv, w_in, frames):
    _, _, feats, padded = dkv.shape
    _, part, width = w_in[0].shape
    share = width // 4
    out = pl.BlockSpec((2, 1, share, frames), lambda j, s: (0, j, 0, 0))
    return call(
        memory_back_kernel,
        (2,),
        [
            pl.BlockSpec((1, 2, feats, padded), lambda j, s: (j, 0, 0, 0)),
            whole(3, part, width),
            whole(3, part, width),
        ],
        [out, out],
        [shaped((2, 2, share, frames), BF), shaped((2, 2, share, frames), F32)],
        [pltpu.VMEM((width, 2 * feats), BF), pltpu.VMEM((width, padded), F32)],
        (8 * frames * width * feats, 0, 14 << 20),
        "memory_back",
    )(scal, dkv, *w_in)


def memory_place_kernel(scal, keep_ref, got_ref, far_ref, out_ref):
    source = pl.program_id(0)

    @pl.when(source < 2)
    def _():
        out_ref[...] = (keep_ref[0] + got_ref[0].astype(F32)).astype(BF)

    @pl.when(source >= 2)
    def _():
        out_ref[...] = far_ref[...]


def memory_place(scal, keep, got, far):
    _, _, share, frames = keep.shape
    near = pl.BlockSpec((1, 1, share, frames), lambda i, s: (0, jnp.minimum(i, 1), 0, 0))
    return call(
        memory_place_kernel,
        (4,),
        [near, near, pl.BlockSpec((1, share, frames), lambda i, s: (jnp.maximum(i - 2, 0), 0, 0))],
        pl.BlockSpec((1, share, frames), lambda i, s: (s[9 + i], 0, 0)),
        shaped((4, share, frames), BF),
        [],
        (0, 0, 0),
        "memory_place",
    )(scal, keep, got, far)


def cross_weights_kernel(
    scal, mem_ref, dkv_ref, h_ref, dq_ref, dx_ref, o_ref,
    weights_ref, one_ref, two_ref, sum_ref, grads, tail_ref,
):
    doc = pl.program_id(0)
    frames = mem_ref.shape[1]
    body = frames // BLOCK * BLOCK
    feats, padded = dkv_ref.shape[2:]

    @pl.when(doc == 0)
    def _():
        sum_ref[...] = jnp.zeros_like(sum_ref)
        tail_ref[...] = jnp.zeros_like(tail_ref)
        put_weights(
            scal,
            weights_ref,
            two_ref,
            1,
            jnp.concatenate([dot(dq_ref[...], h_ref[...], TN), dot(o_ref[...], dx_ref[...], TN)], axis=0),
        )

    tail_ref[: frames - body, :] = mem_ref[0, body:, :]
    rows = dkv_ref[0].reshape(2 * feats, padded)
    part = dot(rows[:, :body], mem_ref[0, :body, :]) + dot(rows[:, body:], tail_ref[...])
    sum_ref[...] += dot(jnp.ones((8, padded), BF), dkv_ref[0, 1], NT)[0:1]

    @pl.when(doc == 0)
    def _():
        grads[...] = part

    @pl.when(doc == 1)
    def _():
        put_weights(scal, weights_ref, one_ref, 0, grads[...] + part)


def cross_weights(scal, memory, dkv, h, dq, dx, o, n_dp):
    _, frames, width = memory.shape
    _, _, feats, padded = dkv.shape
    rows = h.shape[0]
    specs, shapes = weights_specs(width, feats, n_dp)
    return call(
        cross_weights_kernel,
        (2,),
        [
            pl.BlockSpec((1, frames, width), lambda j, s: (s[9 + j], 0, 0)),
            pl.BlockSpec((1, 2, feats, padded), lambda j, s: (j, 0, 0, 0)),
            whole(rows, width),
            whole(rows, feats),
            whole(rows, width),
            whole(rows, feats),
        ],
        specs + [whole(1, feats)],
        shapes + [shaped((1, feats), F32)],
        [pltpu.VMEM((2 * feats, width), F32), pltpu.VMEM((BLOCK, width), BF)],
        (8 * frames * width * feats, 0, 14 << 20),
        "cross_weights",
        WEIGHTS_VMEM,
    )(scal, memory, dkv, h, dq, dx, o)


def per_device(
    inputs, memory, segments, documents, cotangent, norm_gain, norm_shift, attn_in, attn_bias,
    attn_out, cross_in, cross_bias, cross_out, fc_in, fc_in_bias, fc_out, out_bias, n_dp,
):
    length, width = inputs.shape
    docs, frames, _ = memory.shape
    padded = -(-frames // BLOCK) * BLOCK
    longest = length - 2 * (length // 5)
    rows = min(length, -(-longest // BLOCK) * BLOCK)
    half = rows // 2
    shift = length - rows
    slot = lax.axis_index("tensor")
    core, chip = slot % 2, slot // 2
    place_dp = lax.axis_index("dp")
    bits = n_dp.bit_length() - 1

    def swap(value, axis, bit):
        size = n_dp if axis == "dp" else 4
        return lax.ppermute(value, axis, [(i, i ^ bit) for i in range(size)])

    def to_core(value):
        return swap(value, "tensor", 1)

    def to_chip(value):
        return swap(value, "tensor", 2)

    numbers = jnp.arange(docs, dtype=jnp.int32)
    edges = jnp.sum((segments[None, :] < numbers[:, None]).astype(jnp.int32), axis=1)
    which = jnp.max(jnp.where(segments[None, :] == numbers[:, None], documents[None, :], 0), axis=1)
    which = which - place_dp * docs
    first_chip = chip == 0
    edge_one = jnp.where(first_chip, edges[1], edges[2] - shift)
    edge_two = jnp.where(first_chip, edges[2], edges[3] - shift)
    mine = jnp.where(first_chip, which, jnp.roll(which, 2))
    scal = jnp.concatenate(
        [
            jnp.stack(
                [
                    core,
                    chip,
                    edges[2],
                    edge_one,
                    edge_two,
                    jnp.where(first_chip, 0, edge_one),
                    jnp.where(first_chip, edge_one, edge_two),
                    jnp.where(first_chip, edge_one, edge_two),
                    jnp.where(first_chip, edge_two, rows),
                ]
            ),
            mine,
            jnp.stack([place_dp & 1, (place_dp >> 1) & 1]),
        ]
    ).astype(jnp.int32)

    def after(value, *earlier):
        return lax.optimization_barrier((value, earlier))[0]

    attn_in = jnp.swapaxes(attn_in, 1, 2)
    cross_in = jnp.swapaxes(cross_in, 1, 2)
    w_self = (attn_in, to_chip(attn_in))
    w_self_out = (attn_out, to_chip(attn_out))
    biases = jnp.concatenate([attn_bias, cross_bias], axis=0)
    biases = jnp.concatenate([biases, to_chip(biases)], axis=1)
    w_cross = (cross_in, to_chip(after(cross_in, w_self[1])))
    w_cross_out = (cross_out, to_chip(after(cross_out, w_self[1])))

    memory = with_layout_constraint(memory, Layout(major_to_minor=(0, 1, 2)))
    memory, peer_in = lax.optimization_barrier((memory, w_self[1]))
    w_self = (attn_in, peer_in)
    x_win = lax.dynamic_slice_in_dim(inputs, chip * shift, rows)
    dy_win = lax.dynamic_slice_in_dim(cotangent, chip * shift, rows)

    def row(matrix, index):
        return matrix[index : index + 1]

    h1, q1, k1, v1, o1, lse1 = self_forward(
        scal, x_win, row(norm_gain, 0), row(norm_shift, 0), w_self, biases[0:2]
    )
    send, keep = project_out(scal, o1, w_self_out)
    k2, v2 = memory_project(scal, memory, w_cross, biases[3:4], padded)
    x1, h2_own = add_norm(
        scal, x_win, keep, to_core(send), row(out_bias, 0), row(norm_gain, 1), row(norm_shift, 1), True
    )
    h2, q2, o2, lse2, send, keep = cross_forward(
        scal, h2_own, to_core(h2_own), w_cross, biases[2:3], k2, v2, w_cross_out, frames
    )
    x2, h3_own = add_norm(
        scal, x1, keep, to_core(send), row(out_bias, 1), row(norm_gain, 2), row(norm_shift, 2), False
    )

    def spread(value):
        far = to_chip(value)
        return (value, to_core(value), far, to_core(far))

    h3, g, du, send, keep, fc_sum = feed_forward(
        scal, spread(h3_own), cotangent, fc_in, fc_in_bias[None], fc_out
    )
    more = to_core(send)
    far = fold(scal, keep, more)
    got = to_chip(far)
    du, g_low = after((du, g), far)
    out_send, out_keep = second_product(scal, g_low, fc_out, half)
    out_near = to_core(out_send)
    fc_in_grad, fc_out_grad = dot(h3, du, TN), dot(cotangent, g_low, TN)
    far_out = fold(scal, out_keep, out_near)
    got_out = to_chip(after(far_out, got))

    def pick_bit(value, axis, bit):
        mine = (place_dp >> bit) & 1
        stay = lax.dynamic_index_in_dim(value, mine, axis, keepdims=False)
        return stay, lax.dynamic_index_in_dim(value, 1 - mine, axis, keepdims=False).astype(BF)

    others = list(range(2, bits))
    blocked = (2,) * bits + (width // n_dp,)

    def add(value, got):
        return value + got.astype(F32)

    def mlp_chain(matrices):
        value = jnp.stack(matrices).reshape(2, *blocked, -1)
        for number, bit in enumerate([0, 1] + others):
            axis = 1 + bits - 1 - bit if number == 0 else value.ndim - 3
            value, send = pick_bit(value, axis, bit)
            (got,) = yield [(send, "dp", 1 << bit)]
            value = add(value, got)
        return value

    def weights_chain(full, one_send, two_send):
        got = yield [(one_send, "dp", 1), (two_send, "dp", 2)]
        stay, one_send, two_send = shares_one(scal, full, *got)
        got = yield [(one_send, "dp", 2), (two_send, "dp", 1)]
        near, far = shares_two(scal, stay, *got)
        (got,) = yield [(far, "tensor", 2)]
        value = add(near, got)
        value = value.reshape(2, *(2,) * (bits - 2), *value.shape[2:])
        for bit in others:
            value, send = pick_bit(value, value.ndim - 3, bit)
            (got,) = yield [(send, "dp", 1 << bit)]
            value = add(value, got)
        return value

    def send_all(items):
        return [swap(*item) for item in items]

    mlp = mlp_chain([fc_in_grad, fc_out_grad])
    mlp_sent = next(mlp)
    mlp_got = send_all(mlp_sent)
    got = after(got, mlp_sent[0][0], far_out)
    dx2, dx2_low, sums_three = norm_back(
        scal, dy_win, keep, got, x2, row(norm_gain, 2), True, False, more
    )
    dx2_other = to_core(dx2_low)
    dx2_full, dq2, dkv2, q2_sum, send, keep = cross_backward(
        scal, dx2_low, dx2_other, w_cross_out, q2, lse2, k2, v2, w_cross, frames
    )
    mlp_got, got_out = after((mlp_got, got_out), q2_sum)
    mlp_sent = mlp.send(mlp_got)
    mlp_got = send_all(mlp_sent)
    dkv2 = after(dkv2, mlp_sent[0][0])
    *cross_grads, v2_sum = cross_weights(scal, memory, dkv2, h2, dq2, dx2_full, o2, n_dp)
    cross = weights_chain(*cross_grads)
    cross_sent = next(cross)
    cross_got = send_all(cross_sent)
    out_own = output_rows(scal, x2, out_keep, out_near, got_out, row(out_bias, 2))
    out_far = to_chip(out_own)
    mlp_sent = mlp.send(after(mlp_got, v2_sum, out_own))
    mlp_got = send_all(mlp_sent)

    dkv2 = after(dkv2, cross_sent[0][0], cross_sent[1][0], mlp_sent[0][0], out_own)
    mem_send, mem_keep = memory_back(scal, dkv2, w_cross, frames)
    mem_got = to_core(mem_send)
    keep = after(keep, mem_send)
    dx1, dx1_low, sums_two = norm_back(
        scal, dx2, keep, to_core(send), x1, row(norm_gain, 1), False, False, cost=1 << 26
    )
    mem_far = fold(scal, mem_keep, mem_got)
    dx1_other = after(to_core(dx1_low), mem_far)
    *own_grads, self_sum, send, keep = self_backward(
        scal, dx1_low, dx1_other, w_self_out, h1, q1, k1, v1, o1, lse1, w_self, n_dp
    )
    mem_far = to_chip(mem_far)
    out_far = after(out_far, self_sum)
    own = weights_chain(*own_grads)
    own_sent = next(own)
    own_got = send_all(own_sent)
    input_own, input_low, sums_one = norm_back(
        scal, dx1, keep, to_core(send), x_win, row(norm_gain, 0), False, True
    )
    cross_sent = cross.send(after(cross_got, sums_one))
    mlp_got = after(mlp_got, sums_one)
    mem_far = after(mem_far, cross_sent[0][0])
    input_low = after(input_low, mem_far)
    out_own, out_far, mlp_got = after((out_own, out_far, mlp_got), sums_one)

    def input_chain(value):
        (far,) = yield [(value, "tensor", 2)]
        (got,) = yield [(jnp.stack([value, far]), "tensor", 1)]
        return value, far, got

    def output_chain(value, far):
        (got,) = yield [(jnp.stack([value, far]), "tensor", 1)]
        return value, far, got

    part = self_sum.shape[1] // 2

    def sums_chain():
        heads = jnp.concatenate([self_sum, q2_sum, v2_sum])
        sums = jnp.concatenate(
            [sums_one, sums_two, sums_three, jnp.pad(heads, ((0, 0), (0, width - 2 * part))), fc_sum]
        )
        number = jnp.arange(sums.shape[0])[:, None]
        (near,) = yield [(sums, "tensor", 1)]
        sums = sums + jnp.where(number < 12, near, 0.0)
        (far,) = yield [(sums, "tensor", 2)]
        turned = jnp.where(number < 16, jnp.roll(far, -part, axis=1), 0.0)
        sums = sums + jnp.where(number < 12, far, turned)
        start = bits % 2
        if start:
            (got,) = yield [(sums, "dp", 1)]
            sums = sums + got
        for bit in range(start, bits, 2):
            one, two, three = yield [(sums, "dp", which << bit) for which in (1, 2, 3)]
            sums = (sums + one) + (two + three)
        return sums

    chains = [
        (0, own, own_sent, own_got),
        (0, input_chain(input_low), None, None),
        (0, sums_chain(), None, None),
        (OUT_ROUND, output_chain(out_own, out_far), None, None),
        (0, cross, cross_sent, None),
        (0, mlp, mlp_sent, mlp_got),
    ]
    results = [None] * len(chains)
    pending, came = {}, {}
    number = 0
    while number < 3 or pending:
        for i, (start, chain, sent, got) in enumerate(chains):
            if start == number:
                if sent is not None and got is not None:
                    came[i] = got
                elif sent is not None:
                    pending[i] = sent
                else:
                    pending[i] = next(chain) if got is None else chain.send(got)
        values = lax.optimization_barrier([[item[0] for item in items] for items in pending.values()])
        for i, held in zip(pending, values):
            came[i] = [swap(value, *item[1:]) for value, item in zip(held, pending[i])]
        came = lax.optimization_barrier(came)
        pending = {}
        for i, got in came.items():
            try:
                pending[i] = chains[i][1].send(got)
            except StopIteration as stop:
                results[i] = stop.value
        came = {}
        number += 1
    own_share, input_parts, sums, output_parts, cross_share, mlp_share = results
    input_grad = place(scal, *input_parts, length, F32)
    output = place(scal, *output_parts, length, BF)
    memory_grad = jnp.swapaxes(memory_place(scal, mem_keep, mem_got, mem_far), 1, 2)
    heads = sums[12:16, :part]

    def pick(*rows_of):
        return jnp.concatenate([sums[i : i + 1] for i in rows_of])

    return (
        output,
        input_grad,
        memory_grad,
        pick(0, 4, 8),
        pick(1, 5, 9),
        jnp.stack([own_share[0, :, :part], own_share[0, :, part:], own_share[1, :, :part]]),
        heads[0:2],
        own_share[1, :, part:].T,
        jnp.stack([cross_share[1, :, :part], cross_share[0, :, :part], cross_share[0, :, part:]]),
        heads[2:4],
        cross_share[1, :, part:].T,
        mlp_share[0],
        sums[16],
        mlp_share[1].T,
        pick(6, 10, 11),
    )


def solution(mesh):
    n_dp = mesh.shape["dp"]

    def run(*args):
        return per_device(*args, n_dp)

    return jax.shard_map(
        run,
        mesh=mesh,
        in_specs=(
            P("dp", None),
            P("dp", None, None),
            P("dp"),
            P("dp"),
            P("dp", None),
            P(),
            P(),
            P(None, None, "tensor"),
            P(None, "tensor"),
            P("tensor", None),
            P(None, None, "tensor"),
            P(None, "tensor"),
            P("tensor", None),
            P(None, "tensor"),
            P("tensor"),
            P("tensor", None),
            P(),
        ),
        out_specs=(
            P("dp", None),
            P("dp", None),
            P("dp", None, "tensor"),
            P(),
            P(),
            P(None, "dp", "tensor"),
            P(None, "tensor"),
            P("tensor", "dp"),
            P(None, "dp", "tensor"),
            P(None, "tensor"),
            P("tensor", "dp"),
            P("dp", "tensor"),
            P("tensor"),
            P("tensor", "dp"),
            P(),
        ),
        check_vma=False,
    )
```

```python
import jax
import jax.numpy as jnp
from jax import lax
from jax.experimental import pallas as pl
from jax.experimental.layout import Layout, with_layout_constraint
from jax.experimental.pallas import tpu as pltpu
from jax.sharding import PartitionSpec as P

HEAD = 64
PAIR = 2 * HEAD
BLOCK = 128
ROWS = 160
EPSILON = 1e-05
LOG2E = 1.4426950408889634
SCALE = HEAD ** (-0.5)
NEG = -1e30
BIG = 1e30
BF = jnp.bfloat16
F32 = jnp.float32
VMEM = 20 << 20
SMALL_VMEM = 12 << 20
OUT_ROUND = 2
CROSS_VMEM = 34 << 20
SELF_VMEM = 20 << 20
WEIGHTS_VMEM = 20 << 20
PROJECT = 512
FEED = 256
COST = 4

NT = (((1,), (1,)), ((), ()))
NN = (((1,), (0,)), ((), ()))
TN = (((0,), (0,)), ((), ()))


def dot(left, right, dims=NN):
    return lax.dot_general(left, right, dims, preferred_element_type=F32)


def norm_parts(values):
    centred = values - jnp.mean(values, axis=-1, keepdims=True)
    inverse = lax.rsqrt(jnp.mean(centred * centred, axis=-1, keepdims=True) + EPSILON)
    return centred * inverse, inverse


def call(kernel, grid, in_specs, out_specs, out_shape, scratch, cost, name, vmem=VMEM):
    flops, exps, moved = cost
    return pl.pallas_call(
        kernel,
        grid_spec=pltpu.PrefetchScalarGridSpec(
            num_scalar_prefetch=1,
            grid=grid,
            in_specs=in_specs,
            out_specs=out_specs,
            scratch_shapes=scratch,
        ),
        out_shape=out_shape,
        compiler_params=pltpu.CompilerParams(
            dimension_semantics=("arbitrary",) * len(grid), vmem_limit_bytes=vmem
        ),
        cost_estimate=pl.CostEstimate(
            flops=COST * flops + 1, transcendentals=COST * exps, bytes_accessed=COST * moved + 1
        ),
        name=name,
    )


def whole(*shape):
    zeros = (0,) * len(shape)
    return pl.BlockSpec(shape, lambda *_: zeros)


def shaped(shape, dtype):
    return jax.ShapeDtypeStruct(shape, dtype)


def two_heads(rows):
    lane = lax.broadcasted_iota(jnp.int32, rows.shape, 1)
    zero = jnp.zeros_like(rows)
    return jnp.concatenate(
        [jnp.where(lane < HEAD, rows, zero), jnp.where(lane < HEAD, zero, rows)], axis=0
    )


def pick_heads(both):
    row = lax.broadcasted_iota(jnp.int32, (PAIR, BLOCK), 0)
    return jnp.where(row < HEAD, both[:, :BLOCK], both[:, BLOCK:]).T


def row_lanes(first):
    lane = lax.broadcasted_iota(jnp.int32, (1, 2 * BLOCK), 1)
    return first + jnp.where(lane < BLOCK, lane, lane - BLOCK)


def flip(matrix):
    return matrix.astype(F32).T.astype(BF)


def split_out(scal, total, send_ref, keep_ref, half):
    core = scal[0]
    here = pl.multiple_of(core * half, half)
    there = pl.multiple_of((1 - core) * half, half)
    keep_ref[...] = total[pl.ds(here, half), :]
    send_ref[...] = total[pl.ds(there, half), :].astype(BF)


def join_halves(scal, own_ref, other_ref, full_ref, half):
    core = scal[0]
    full_ref[pl.ds(pl.multiple_of(core * half, half), half), :] = own_ref[...]
    full_ref[pl.ds(pl.multiple_of((1 - core) * half, half), half), :] = other_ref[...]


def join_weights(own_ref, peer_ref, full_ref):
    part = own_ref.shape[-2]
    full_ref[..., :part, :] = own_ref[...]
    full_ref[..., part:, :] = peer_ref[...]


def join_stack(own_ref, peer_ref, full_ref):
    count, part, _ = own_ref.shape
    for number in range(count):
        first = 2 * part * number
        full_ref[first : first + part, :] = own_ref[number]
        full_ref[first + part : first + 2 * part, :] = peer_ref[number]


def put_weights(scal, full_ref, stay_ref, send_ref, group, rows):
    part = rows.shape[0] // 4
    count, size = full_ref.shape[:2]
    for side in range(2):
        one = rows[side * part : (side + 1) * part]
        two = rows[(2 + side) * part : (3 + side) * part]
        turned = jnp.concatenate([one, two], axis=0).T
        for block in range(count):
            full_ref[block] = turned[block * size : (block + 1) * size]
        for rest in range(count // 4):
            for other in range(2):
                stay = 2 * other + scal[13] if group == 0 else 2 * scal[14] + other
                send = 2 * other + 1 - scal[13] if group == 0 else 2 * (1 - scal[14]) + other
                stay_ref[group, side, rest, other] = full_ref[4 * rest + stay]
                send_ref[side, rest, other] = full_ref[4 * rest + send].astype(BF)


def weights_specs(width, feats, n_dp):
    size = width // n_dp
    half = (2, n_dp // 4, 2, size, feats)
    return (
        [whole(2, *half), whole(*half), whole(*half)],
        [shaped((2, *half), F32), shaped(half, BF), shaped(half, BF)],
        pltpu.VMEM((n_dp, size, feats), F32),
    )


def shares_one_kernel(scal, full_ref, one_ref, two_ref, stay_ref, one_send, two_send):
    low, high = scal[13], scal[14]
    for side in range(2):
        for rest in range(one_ref.shape[1]):

            def one_sum(bit):
                return full_ref[0, side, rest, bit] + one_ref[side, rest, bit].astype(F32)

            def two_sum(bit):
                return full_ref[1, side, rest, bit] + two_ref[side, rest, bit].astype(F32)

            stay_ref[0, side, rest] = one_sum(high)
            one_send[side, rest] = one_sum(1 - high).astype(BF)
            stay_ref[1, side, rest] = two_sum(low)
            two_send[side, rest] = two_sum(1 - low).astype(BF)


def shares_one(scal, full, one, two):
    _, _, count, _, size, feats = full.shape
    stay = (2, 2, count, size, feats)
    send = (2, count, size, feats)
    return call(
        shares_one_kernel,
        (1,),
        [whole(*full.shape), whole(*one.shape), whole(*one.shape)],
        [whole(*stay), whole(*send), whole(*send)],
        [shaped(stay, F32), shaped(send, BF), shaped(send, BF)],
        [],
        (0, 0, 0),
        "shares_one",
        SMALL_VMEM,
    )(scal, full, one, two)


def shares_two_kernel(scal, stay_ref, one_ref, two_ref, near_ref, far_ref):
    for group, got in enumerate((one_ref, two_ref)):
        near_ref[group] = stay_ref[group, 0] + got[0].astype(F32)
        far_ref[group] = (stay_ref[group, 1] + got[1].astype(F32)).astype(BF)


def shares_two(scal, stay, one, two):
    out = (2, *stay.shape[2:])
    return call(
        shares_two_kernel,
        (1,),
        [whole(*stay.shape), whole(*one.shape), whole(*one.shape)],
        [whole(*out), whole(*out)],
        [shaped(out, F32), shaped(out, BF)],
        [],
        (0, 0, 0),
        "shares_two",
        SMALL_VMEM,
    )(scal, stay, one, two)


def self_mask(scal, count, first):
    rows = row_lanes(first)
    edge_one, edge_two = scal[3], scal[4]
    begin = jnp.where(rows >= edge_two, edge_two, jnp.where(rows >= edge_one, edge_one, 0))
    keys = lax.broadcasted_iota(jnp.int32, (count, 2 * BLOCK), 0)
    return (keys >= begin) & (keys <= rows)


def self_forward_kernel(
    scal, x_ref, gain_ref, shift_ref, w_own, w_peer, b_ref,
    h_ref, q_ref, k_ref, v_ref, o_ref, lse_ref, vt, w_ref,
):
    rows = x_ref.shape[0]
    join_stack(w_own, w_peer, w_ref)
    normed, _ = norm_parts(x_ref[...].astype(F32))
    h_ref[...] = (normed * gain_ref[...] + shift_ref[...]).astype(BF)
    part = q_ref.shape[1]
    projected = dot(h_ref[...], w_ref[...], NT)
    q_ref[...] = (projected[:, :part] + b_ref[0:1, :]).astype(BF)
    k_ref[...] = projected[:, part : 2 * part].astype(BF)
    v_ref[...] = (projected[:, 2 * part :] + b_ref[1:2, :]).astype(BF)
    vt[...] = flip(v_ref[...])
    for block in range(rows // BLOCK):
        first = block * BLOCK
        count = first + BLOCK
        kept = self_mask(scal, count, first)
        for pair in range(part // PAIR):
            here = lanes(pair)
            queries = two_heads(q_ref[first : first + BLOCK, here])
            scores = jnp.where(kept, dot(k_ref[:count, here], queries, NT), NEG)
            largest = jnp.max(scores, axis=0, keepdims=True)
            chances = jnp.exp2((scores - largest) * (SCALE * LOG2E))
            totals = jnp.sum(chances, axis=0, keepdims=True)
            mixed = dot(vt[here, :count], chances.astype(BF)) * (1.0 / totals)
            o_ref[first : first + BLOCK, here] = pick_heads(mixed).astype(BF)
            lse_ref[pair, block] = largest * (SCALE * LOG2E) + jnp.log(totals) * LOG2E


def project_out_kernel(scal, o_ref, wo_own, wo_peer, send_ref, keep_ref, total):
    part = wo_own.shape[0]
    wo = jnp.concatenate([wo_own[...], wo_peer[...]], axis=0)
    total[...] = dot(o_ref[...], wo)
    split_out(scal, total, send_ref, keep_ref, o_ref.shape[0] // 2)


def project_out(scal, mixed, w_out):
    rows, feats = mixed.shape
    part, width = w_out[0].shape
    half = rows // 2
    return call(
        project_out_kernel,
        (1,),
        [whole(rows, feats), whole(part, width), whole(part, width)],
        [whole(half, width)] * 2,
        [shaped((half, width), BF), shaped((half, width), F32)],
        [pltpu.VMEM((rows, width), F32)],
        (0, 0, 0),
        "project_out",
        SMALL_VMEM,
    )(scal, mixed, *w_out)


def self_forward(scal, x_win, gain, shift, w_in, bias):
    rows, width = x_win.shape
    part = w_in[0].shape[1]
    feats = 2 * part
    pairs = feats // PAIR
    blocks = rows // BLOCK
    return call(
        self_forward_kernel,
        (1,),
        [
            whole(rows, width),
            whole(1, width),
            whole(1, width),
            whole(3, part, width),
            whole(3, part, width),
            whole(2, feats),
        ],
        [whole(rows, width)]
        + [whole(rows, feats)] * 4
        + [whole(pairs, blocks, 1, 2 * BLOCK)],
        [shaped((rows, width), BF)]
        + [shaped((rows, feats), BF)] * 4
        + [shaped((pairs, blocks, 1, 2 * BLOCK), F32)],
        [
            pltpu.VMEM((feats, rows), BF),
            pltpu.VMEM((3 * feats, width), BF),
        ],
        (8 * rows * width * feats + 4 * rows * rows * feats, rows * rows * 6, 12 << 20),
        "self_forward",
    )(scal, x_win, gain, shift, *w_in, bias)


def self_backward_kernel(
    scal, own_ref, other_ref, wo_own, wo_peer, h_ref, q_ref, k_ref, v_ref, o_ref, lse_ref,
    w_own, w_peer, weights_ref, one_ref, two_ref, sum_ref, send_ref, keep_ref,
    full_ref, dx_ref, grad_ref, total, kt, do, dks, dvs, w_ref, wo_ref,
):
    rows, feats = q_ref.shape
    join_halves(scal, own_ref, other_ref, dx_ref, rows // 2)
    join_stack(w_own, w_peer, w_ref)
    join_weights(wo_own, wo_peer, wo_ref)
    do[...] = dot(dx_ref[...], wo_ref[...], NT).astype(BF)
    kt[...] = flip(k_ref[...])
    for block in reversed(range(rows // BLOCK)):
        first = block * BLOCK
        count = first + BLOCK
        kept = self_mask(scal, count, first)
        for pair in range(feats // PAIR):
            here = lanes(pair)
            queries = two_heads(q_ref[first : first + BLOCK, here])
            grads = two_heads(do[first : first + BLOCK, here])
            scores = dot(k_ref[:count, here], queries, NT)
            chances = jnp.exp2(scores * (SCALE * LOG2E) - lse_ref[pair, block])
            chances = jnp.where(kept, chances, 0.0)
            prob_grad = dot(v_ref[:count, here], grads, NT)
            shared = jnp.sum(chances * prob_grad, axis=0, keepdims=True)
            score_grad = (chances * (prob_grad - shared)).astype(BF)
            dv = dot(chances.astype(BF), grads)
            dk = dot(score_grad, queries)
            if count == rows:
                dvs[:, here] = dv
                dks[:, here] = dk
            else:
                dvs[:count, here] += dv
                dks[:count, here] += dk
            turned = pick_heads(dot(kt[here, :count], score_grad)) * SCALE
            grad_ref[first : first + BLOCK, here] = turned.astype(BF)
    grad_ref[:, feats : 2 * feats] = (dks[...] * SCALE).astype(BF)
    grad_ref[:, 2 * feats :] = dvs[...].astype(BF)
    sum_ref[0:1, :] = jnp.sum(grad_ref[:, :feats].astype(F32), axis=0, keepdims=True)
    sum_ref[1:2, :] = jnp.sum(grad_ref[:, 2 * feats :].astype(F32), axis=0, keepdims=True)
    total[...] = dot(grad_ref[...], w_ref[...])
    split_out(scal, total, send_ref, keep_ref, rows // 2)
    hidden = h_ref[...]
    put_weights(scal, full_ref, weights_ref, one_ref, 0, dot(grad_ref[:, : 2 * feats], hidden, TN))
    put_weights(
        scal,
        full_ref,
        weights_ref,
        two_ref,
        1,
        jnp.concatenate(
            [dot(grad_ref[:, 2 * feats :], hidden, TN), dot(o_ref[...], dx_ref[...], TN)], axis=0
        ),
    )


def self_backward(scal, own, other, w_out, h, q, k, v, o, lse, w_in, n_dp):
    rows, feats = q.shape
    width = own.shape[1]
    part = feats // 2
    pairs = feats // PAIR
    blocks = rows // BLOCK
    half = rows // 2
    specs, shapes, blocked = weights_specs(width, feats, n_dp)
    return call(
        self_backward_kernel,
        (1,),
        [whole(half, width)] * 2
        + [whole(part, width)] * 2
        + [whole(rows, width)]
        + [whole(rows, feats)] * 4
        + [whole(pairs, blocks, 1, 2 * BLOCK)]
        + [whole(3, part, width)] * 2,
        specs
        + [
            whole(2, feats),
            whole(half, width),
            whole(half, width),
        ],
        shapes
        + [
            shaped((2, feats), F32),
            shaped((half, width), BF),
            shaped((half, width), F32),
        ],
        [
            blocked,
            pltpu.VMEM((rows, width), BF),
            pltpu.VMEM((rows, 3 * feats), BF),
            pltpu.VMEM((rows, width), F32),
            pltpu.VMEM((feats, rows), BF),
            pltpu.VMEM((rows, feats), BF),
            pltpu.VMEM((rows, feats), F32),
            pltpu.VMEM((rows, feats), F32),
            pltpu.VMEM((3 * feats, width), BF),
            pltpu.VMEM((feats, width), BF),
        ],
        (8 * rows * width * feats + 10 * rows * rows * feats, rows * rows * 6, 14 << 20),
        "self_backward",
        SELF_VMEM,
    )(scal, own, other, *w_out, h, q, k, v, o, lse, *w_in)


def add_norm_kernel(scal, base_ref, keep_ref, got_ref, bias_ref, gain_ref, shift_ref, x_ref, h_ref):
    value = base_ref[...].astype(F32) + (keep_ref[...] + got_ref[...].astype(F32)) + bias_ref[...]
    x_ref[...] = value
    normed, _ = norm_parts(value)
    h_ref[...] = (normed * gain_ref[...] + shift_ref[...]).astype(BF)


def add_norm(scal, base, keep, got, bias, gain, shift, by_core):
    half, width = keep.shape
    steps = half // ROWS
    block = pl.BlockSpec((ROWS, width), lambda i, s: (i, 0))
    base_spec = pl.BlockSpec((ROWS, width), lambda i, s: (s[0] * steps + i, 0)) if by_core else block
    return call(
        add_norm_kernel,
        (steps,),
        [base_spec, block, block] + [whole(1, width)] * 3,
        [block] * 2,
        [shaped((half, width), F32), shaped((half, width), BF)],
        [],
        (0, 0, 0),
        "add_norm",
        SMALL_VMEM,
    )(scal, base, keep, got, bias, gain, shift)


def norm_back_more_kernel(
    scal, base_ref, keep_ref, got_ref, x_ref, gain_ref, more_ref, dx_ref, low_ref, sum_ref
):
    norm_back_body(
        scal, base_ref, keep_ref[0] + more_ref[0].astype(F32), got_ref, x_ref, gain_ref,
        dx_ref, low_ref, sum_ref,
    )


def norm_back_kernel(scal, base_ref, keep_ref, got_ref, x_ref, gain_ref, dx_ref, low_ref, sum_ref):
    norm_back_body(
        scal, base_ref, keep_ref[...], got_ref, x_ref, gain_ref, dx_ref, low_ref, sum_ref
    )


def norm_back_body(scal, base_ref, keep, got_ref, x_ref, gain_ref, dx_ref, low_ref, sum_ref):
    step, steps = pl.program_id(0), pl.num_programs(0)
    base = base_ref[...].astype(F32)
    grad = keep + got_ref[...].astype(F32)
    row = (scal[0] * steps + step) * ROWS + lax.broadcasted_iota(jnp.int32, (ROWS, 1), 0)
    valid = (row >= scal[5]) & (row < scal[8])
    grad = jnp.where(valid, grad, 0.0)
    base = jnp.where(valid, base, 0.0)
    normed, inverse = norm_parts(x_ref[...].astype(F32))
    scaled = grad * gain_ref[...]
    total = base + inverse * (
        scaled
        - jnp.mean(scaled, axis=-1, keepdims=True)
        - normed * jnp.mean(scaled * normed, axis=-1, keepdims=True)
    )
    dx_ref[...] = total
    low_ref[...] = total.astype(BF)

    @pl.when(step == 0)
    def _():
        sum_ref[...] = jnp.zeros_like(sum_ref)

    sum_ref[0:1, :] += jnp.sum(grad * normed, axis=0, keepdims=True)
    sum_ref[1:2, :] += jnp.sum(grad, axis=0, keepdims=True)
    sum_ref[2:3, :] += jnp.sum(total, axis=0, keepdims=True)
    sum_ref[3:4, :] += jnp.sum(base, axis=0, keepdims=True)


def norm_back(scal, base, keep, got, x, gain, base_by_core, x_by_core, more=None, cost=0):
    half, width = got.shape

    steps = half // ROWS
    block = pl.BlockSpec((ROWS, width), lambda i, s: (i, 0))
    cored = pl.BlockSpec((ROWS, width), lambda i, s: (s[0] * steps + i, 0))

    stacked = pl.BlockSpec((1, ROWS, width), lambda i, s: (0, i, 0))

    def spec(by_core):
        return cored if by_core else block

    return call(
        norm_back_kernel if more is None else norm_back_more_kernel,
        (steps,),
        [
            spec(base_by_core),
            block if more is None else stacked,
            block,
            spec(x_by_core),
            whole(1, width),
        ]
        + [stacked] * (more is not None),
        [block, block, whole(4, width)],
        [shaped((half, width), F32), shaped((half, width), BF), shaped((4, width), F32)],
        [],
        (0, 0, cost),
        "norm_back",
        SMALL_VMEM,
    )(scal, base, keep, got, x, gain, *([] if more is None else [more]))


def pieces(total, size):
    return [(first, min(size, total - first)) for first in range(0, total, size)]


def memory_project_kernel(scal, mem_ref, w_own, w_peer, b_ref, k_ref, v_ref, w_ref):
    feats = k_ref.shape[2]

    @pl.when(pl.program_id(0) == 0)
    def _():
        for number in range(2):
            rows = slice(number * feats, (number + 1) * feats)
            join_weights(w_own.at[1 + number], w_peer.at[1 + number], w_ref.at[rows])

    frames = mem_ref.shape[1]
    padded = k_ref.shape[1]
    tail = padded - BLOCK
    k_ref[0, tail:padded, :] = jnp.zeros((BLOCK, k_ref.shape[2]), BF)
    v_ref[0, tail:padded, :] = jnp.zeros((BLOCK, k_ref.shape[2]), BF)
    for first, size in pieces(frames, PROJECT):
        both = dot(mem_ref[0, first : first + size, :], w_ref[...], NT)
        k_ref[0, first : first + size, :] = both[:, :feats].astype(BF)
        v_ref[0, first : first + size, :] = (both[:, feats:] + b_ref[...]).astype(BF)


def memory_project(scal, memory, w_kv, bias, padded):
    _, frames, width = memory.shape
    part = w_kv[0].shape[1]
    feats = 2 * part
    out = pl.BlockSpec((1, padded, feats), lambda j, s: (j, 0, 0))
    return call(
        memory_project_kernel,
        (2,),
        [
            pl.BlockSpec((1, frames, width), lambda j, s: (s[9 + j], 0, 0)),
            whole(3, part, width),
            whole(3, part, width),
            whole(1, feats),
        ],
        [out, out],
        [shaped((2, padded, feats), BF)] * 2,
        [pltpu.VMEM((2 * feats, width), BF)],
        (8 * frames * width * feats, 0, 12 << 20),
        "memory_project",
    )(scal, memory, *w_kv, bias)


def block_span(scal, doc):
    low, high = scal[5 + 2 * doc], scal[6 + 2 * doc]
    return low, high, low // BLOCK, (high + BLOCK - 1) // BLOCK


def lanes(pair):
    return slice(pair * PAIR, (pair + 1) * PAIR)


def cross_forward_kernel(
    scal, own_ref, other_ref, wq_own, wq_peer, bq_ref, k_ref, v_ref, wo_own, wo_peer,
    h_ref, q_ref, o_ref, lse_ref, send_ref, keep_ref, total, vt, s_ref, wq_ref, wo_ref, *, frames,
):
    doc = pl.program_id(0)
    rows, feats = q_ref.shape
    padded = k_ref.shape[1]

    @pl.when(doc == 0)
    def _():
        join_halves(scal, own_ref, other_ref, h_ref, rows // 2)
        join_weights(wq_own.at[0], wq_peer.at[0], wq_ref)
        join_weights(wo_own, wo_peer, wo_ref)
        q_ref[...] = (dot(h_ref[...], wq_ref[...], NT) + bq_ref[...]).astype(BF)
        o_ref[...] = jnp.zeros_like(o_ref)
        lse_ref[...] = jnp.zeros_like(lse_ref)

    vt[...] = flip(v_ref[0])
    low, high, start, stop = block_span(scal, doc)

    def one_block(block, carry):
        first = pl.multiple_of(block * BLOCK, BLOCK)
        number = row_lanes(first)
        inside = (number >= low) & (number < high)
        for pair in range(feats // PAIR):
            here = lanes(pair)
            queries = two_heads(q_ref[pl.ds(first, BLOCK), here])
            s_ref[pair] = dot(k_ref[0, :, here], queries, NT)
            s_ref[pair, frames:padded, :] = jnp.full((padded - frames, 2 * BLOCK), NEG, F32)
            scores = s_ref[pair]
            largest = jnp.max(scores, axis=0, keepdims=True)
            chances = jnp.exp2((scores - largest) * (SCALE * LOG2E))
            totals = jnp.sum(chances, axis=0, keepdims=True)
            mixed = dot(vt[here, :], chances.astype(BF)) * jnp.where(inside, 1.0 / totals, 0.0)
            o_ref[pl.ds(first, BLOCK), here] += pick_heads(mixed).astype(BF)
            log_total = largest * (SCALE * LOG2E) + jnp.log(totals) * LOG2E
            lse_ref[pair, block] = jnp.where(inside, log_total, lse_ref[pair, block])
        return carry

    lax.fori_loop(start, stop, one_block, 0)

    @pl.when(doc == 1)
    def _():
        total[...] = dot(o_ref[...], wo_ref[...])
        split_out(scal, total, send_ref, keep_ref, rows // 2)


def cross_forward(scal, own, other, wq, bq, k, v, w_out, frames):
    half, width = own.shape
    rows = 2 * half
    _, padded, feats = k.shape
    pairs = feats // PAIR
    blocks = rows // BLOCK
    keyed = pl.BlockSpec((1, padded, feats), lambda j, s: (j, 0, 0))

    def kernel(*refs):
        cross_forward_kernel(*refs, frames=frames)

    return call(
        kernel,
        (2,),
        [
            whole(half, width),
            whole(half, width),
            whole(1, feats // 2, width),
            whole(1, feats // 2, width),
            whole(1, feats),
            keyed,
            keyed,
            whole(feats // 2, width),
            whole(feats // 2, width),
        ],
        [
            whole(rows, width),
            whole(rows, feats),
            whole(rows, feats),
            whole(pairs, blocks, 1, 2 * BLOCK),
            whole(half, width),
            whole(half, width),
        ],
        [
            shaped((rows, width), BF),
            shaped((rows, feats), BF),
            shaped((rows, feats), BF),
            shaped((pairs, blocks, 1, 2 * BLOCK), F32),
            shaped((half, width), BF),
            shaped((half, width), F32),
        ],
        [
            pltpu.VMEM((rows, width), F32),
            pltpu.VMEM((feats, padded), BF),
            pltpu.VMEM((pairs, padded, 2 * BLOCK), F32),
            pltpu.VMEM((feats, width), BF),
            pltpu.VMEM((feats, width), BF),
        ],
        (4 * rows * width * feats + 4 * rows * padded * feats, rows * padded * 6, 14 << 20),
        "cross_forward",
        CROSS_VMEM,
    )(scal, own, other, *wq, bq, k, v, *w_out)


def cross_backward_kernel(
    scal, own_ref, other_ref, wo_own, wo_peer, q_ref, lse_ref, k_ref, v_ref, wq_own, wq_peer,
    dx_ref, dq_ref, dkv_ref, sum_ref, send_ref, keep_ref,
    total, kt, do, dks, dvs, wq_ref, wo_ref, *, frames,
):
    doc = pl.program_id(0)
    rows, feats = q_ref.shape
    padded = k_ref.shape[1]

    @pl.when(doc == 0)
    def _():
        join_halves(scal, own_ref, other_ref, dx_ref, rows // 2)
        join_weights(wq_own.at[0], wq_peer.at[0], wq_ref)
        join_weights(wo_own, wo_peer, wo_ref)
        do[...] = dot(dx_ref[...], wo_ref[...], NT).astype(BF)
        dq_ref[...] = jnp.zeros_like(dq_ref)

    kt[...] = flip(k_ref[0])
    dks[...] = jnp.zeros_like(dks)
    dvs[...] = jnp.zeros_like(dvs)
    low, high, start, stop = block_span(scal, doc)

    def one_block(block, carry):
        first = pl.multiple_of(block * BLOCK, BLOCK)
        number = row_lanes(first)
        inside = (number >= low) & (number < high)
        for pair in range(feats // PAIR):
            here = lanes(pair)
            queries = two_heads(q_ref[pl.ds(first, BLOCK), here])
            grads = two_heads(do[pl.ds(first, BLOCK), here])
            log_total = jnp.where(inside, lse_ref[pair, block], BIG)
            chances = jnp.exp2(dot(k_ref[0, :, here], queries, NT) * (SCALE * LOG2E) - log_total)
            prob_grad = dot(v_ref[0, :, here], grads, NT)
            shared = jnp.sum(chances * prob_grad, axis=0, keepdims=True)
            score_grad = (chances * (prob_grad - shared)).astype(BF)
            dvs[:, here] += dot(chances.astype(BF), grads)
            dks[:, here] += dot(score_grad, queries)
            turned = pick_heads(dot(kt[here, :], score_grad)) * SCALE
            dq_ref[pl.ds(first, BLOCK), here] += turned.astype(BF)
        return carry

    lax.fori_loop(start, stop, one_block, 0)
    tail = jnp.zeros((padded - frames, feats), F32)
    dks[frames:, :] = tail
    dvs[frames:, :] = tail
    dkv_ref[0, 0] = (dks[...] * SCALE).T.astype(BF)
    dkv_ref[0, 1] = dvs[...].T.astype(BF)

    @pl.when(doc == 1)
    def _():
        sum_ref[...] = jnp.sum(dq_ref[...].astype(F32), axis=0, keepdims=True)
        total[...] = dot(dq_ref[...], wq_ref[...])
        split_out(scal, total, send_ref, keep_ref, rows // 2)


def cross_backward(scal, own, other, w_out, q, lse, k, v, wq, frames):
    half, width = own.shape
    rows = 2 * half
    _, padded, feats = k.shape
    pairs = feats // PAIR
    blocks = rows // BLOCK
    keyed = pl.BlockSpec((1, padded, feats), lambda j, s: (j, 0, 0))

    def kernel(*refs):
        cross_backward_kernel(*refs, frames=frames)

    return call(
        kernel,
        (2,),
        [
            whole(half, width),
            whole(half, width),
            whole(feats // 2, width),
            whole(feats // 2, width),
            whole(rows, feats),
            whole(pairs, blocks, 1, 2 * BLOCK),
            keyed,
            keyed,
            whole(1, feats // 2, width),
            whole(1, feats // 2, width),
        ],
        [
            whole(rows, width),
            whole(rows, feats),
            pl.BlockSpec((1, 2, feats, padded), lambda j, s: (j, 0, 0, 0)),
            whole(1, feats),
            whole(half, width),
            whole(half, width),
        ],
        [
            shaped((rows, width), BF),
            shaped((rows, feats), BF),
            shaped((2, 2, feats, padded), BF),
            shaped((1, feats), F32),
            shaped((half, width), BF),
            shaped((half, width), F32),
        ],
        [
            pltpu.VMEM((rows, width), F32),
            pltpu.VMEM((feats, padded), BF),
            pltpu.VMEM((rows, feats), BF),
            pltpu.VMEM((padded, feats), F32),
            pltpu.VMEM((padded, feats), F32),
            pltpu.VMEM((feats, width), BF),
            pltpu.VMEM((feats, width), BF),
        ],
        (4 * rows * width * feats + 10 * rows * padded * feats, rows * padded * 6, 18 << 20),
        "cross_backward",
        CROSS_VMEM,
    )(scal, own, other, *w_out, q, lse, k, v, *wq)


def finish_sums_kernel(scal, sum_ref, gain_ref, shift_ref, bias_ref, self_ref, cross_ref, fc_ref):
    part = self_ref.shape[1]
    for norm in range(3):
        gain_ref[norm : norm + 1, :] = sum_ref[4 * norm : 4 * norm + 1, :]
        shift_ref[norm : norm + 1, :] = sum_ref[4 * norm + 1 : 4 * norm + 2, :]
    for number, line in enumerate((6, 10, 11)):
        bias_ref[number : number + 1, :] = sum_ref[line : line + 1, :]
    self_ref[...] = sum_ref[12:14, :part]
    cross_ref[...] = sum_ref[14:16, :part]
    fc_ref[...] = sum_ref[16:17, :]


def finish_sums(scal, sums, part):
    rows, width = sums.shape
    shapes = [(3, width)] * 3 + [(2, part)] * 2 + [(1, width)]
    return call(
        finish_sums_kernel,
        (1,),
        [whole(rows, width)],
        [whole(*shape) for shape in shapes],
        [shaped(shape, F32) for shape in shapes],
        [],
        (0, 0, 0),
        "finish_sums",
        SMALL_VMEM,
    )(scal, sums)


def place_rows(scal, refs, full_ref):
    core, chip, edge = scal[0], scal[1], scal[2]
    half = refs[0].shape[-2]
    shift = full_ref.shape[0] - 2 * half
    for number, ref in enumerate(refs):
        which_chip = chip if number < 2 else 1 - chip
        which_core = core if number % 2 == 0 else 1 - core
        first = pl.multiple_of(which_chip * shift + which_core * half, 64)
        row = first + lax.broadcasted_iota(jnp.int32, (half, 1), 0)
        valid = (row < edge) == (which_chip == 0)
        part = (ref[...] if ref.ndim == 2 else ref[0]).astype(full_ref.dtype)
        full_ref[pl.ds(first, half), :] = jnp.where(valid, part, full_ref[pl.ds(first, half), :])


def place_kernel(scal, a_ref, b_ref, c_ref, d_ref, out_ref):
    place_rows(scal, (a_ref, b_ref, c_ref, d_ref), out_ref)


def place(scal, own, far, got, length, dtype):
    half, width = own.shape
    near_half = pl.BlockSpec((1, half, width), lambda *_: (0, 0, 0))
    far_half = pl.BlockSpec((1, half, width), lambda *_: (1, 0, 0))
    return call(
        place_kernel,
        (1,),
        [whole(half, width), near_half, whole(half, width), far_half],
        whole(length, width),
        shaped((length, width), dtype),
        [],
        (0, 0, 0),
        "place_rows",
        SMALL_VMEM,
    )(scal, own, got, far, got)


def window_shares(scal, full_ref, send_ref, keep_ref):
    core, chip = scal[0], scal[1]
    half = keep_ref.shape[1]
    shift = full_ref.shape[0] - 2 * half
    for slot in range(2):
        first = (chip if slot == 0 else 1 - chip) * shift
        near = pl.multiple_of(first + core * half, 64)
        far = pl.multiple_of(first + (1 - core) * half, 64)
        keep_ref[slot] = full_ref[pl.ds(near, half), :]
        send_ref[slot] = full_ref[pl.ds(far, half), :].astype(BF)


def second_product_kernel(scal, g_ref, w_ref, send_ref, keep_ref, full_ref):
    full_ref[...] = dot(g_ref[...], w_ref[...])
    window_shares(scal, full_ref, send_ref, keep_ref)


def second_product(scal, g, w_out, half):
    length, hidden = g.shape
    width = w_out.shape[1]
    return call(
        second_product_kernel,
        (1,),
        [whole(length, hidden), whole(hidden, width)],
        [whole(2, half, width)] * 2,
        [shaped((2, half, width), BF), shaped((2, half, width), F32)],
        [pltpu.VMEM((length, width), F32)],
        (0, 0, 0),
        "second_product",
    )(scal, g, w_out)


def fold_kernel(scal, keep_ref, got_ref, out_ref):
    keep = keep_ref[0] if keep_ref.ndim > out_ref.ndim else keep_ref[...]
    out_ref[...] = (keep + got_ref[0].astype(F32)).astype(BF)


def fold(scal, keep, got):
    shape = got.shape[1:]
    second = pl.BlockSpec((1, *shape), lambda i, s: (1, *(0,) * len(shape)))
    return call(
        fold_kernel,
        (1,),
        [second if keep.ndim == got.ndim else whole(*shape), second],
        whole(*shape),
        shaped(shape, BF),
        [],
        (0, 0, 0),
        "fold",
        SMALL_VMEM,
    )(scal, keep, got)


def output_rows_kernel(scal, x_ref, keep_ref, near_ref, far_ref, bias_ref, out_ref):
    value = keep_ref[0] + near_ref[0].astype(F32) + far_ref[...].astype(F32)
    out_ref[...] = (x_ref[...] + value + bias_ref[...]).astype(BF)


def output_rows(scal, x, keep, near, far, bias):
    half, width = x.shape
    first = pl.BlockSpec((1, half, width), lambda i, s: (0, 0, 0))
    return call(
        output_rows_kernel,
        (1,),
        [whole(half, width), first, first, whole(half, width), whole(1, width)],
        whole(half, width),
        shaped((half, width), BF),
        [],
        (0, 0, 0),
        "output_rows",
        SMALL_VMEM,
    )(scal, x, keep, near, far, bias)


def feed_forward_kernel(
    scal, a_ref, b_ref, c_ref, d_ref, dy_ref, wi_ref, bi_ref, wo_ref,
    h_ref, g_ref, du_ref, send_ref, keep_ref, sum_ref, dh_ref,
):
    step = pl.program_id(0)
    size = dy_ref.shape[0]

    @pl.when(step == 0)
    def _():
        place_rows(scal, (a_ref, b_ref, c_ref, d_ref), h_ref)
        sum_ref[...] = jnp.zeros_like(sum_ref)

    rows = h_ref[pl.ds(pl.multiple_of(step * size, size), size), :]
    value = dot(rows, wi_ref[...]) + bi_ref[...]
    normal = 0.5 + 0.5 * lax.erf(value * (0.5**0.5))
    g_ref[...] = (value * normal).astype(BF)
    density = jnp.exp2(value * value * (-0.5 * LOG2E)) * 0.3989422804014327
    grad = dot(dy_ref[...], wo_ref[...], NT) * (normal + value * density)
    low = grad.astype(BF)
    du_ref[...] = low
    sum_ref[...] += jnp.sum(low.astype(F32), axis=0, keepdims=True)
    dh_ref[pl.ds(pl.multiple_of(step * size, size), size), :] = dot(low, wi_ref[...], NT)

    @pl.when(step == pl.num_programs(0) - 1)
    def _():
        window_shares(scal, dh_ref, send_ref, keep_ref)


def feed_forward(scal, parts, dy, w_in, b_in, w_out):
    length, width = dy.shape
    hidden = w_in.shape[1]
    half = parts[0].shape[0]
    size = FEED
    return call(
        feed_forward_kernel,
        (length // size,),
        [whole(half, width)] * 4
        + [
            pl.BlockSpec((size, width), lambda i, s: (i, 0)),
            whole(width, hidden),
            whole(1, hidden),
            whole(hidden, width),
        ],
        [
            whole(length, width),
            pl.BlockSpec((size, hidden), lambda i, s: (i, 0)),
            pl.BlockSpec((size, hidden), lambda i, s: (i, 0)),
            whole(2, half, width),
            whole(2, half, width),
            whole(1, hidden),
        ],
        [
            shaped((length, width), BF),
            shaped((length, hidden), BF),
            shaped((length, hidden), BF),
            shaped((2, half, width), BF),
            shaped((2, half, width), F32),
            shaped((1, hidden), F32),
        ],
        [pltpu.VMEM((length, width), F32)],
        (6 * length * width * hidden, 2 * length * hidden, 14 << 20),
        "feed_forward",
    )(scal, *parts, dy, w_in, b_in, w_out)


def memory_back_kernel(
    scal, dkv_ref, w_own, w_peer, send_ref, near_ref, far_ref, w_ref, part_ref
):
    core, chip = scal[0], scal[1]
    share, frames = near_ref.shape[1:]
    part = w_own.shape[1]

    @pl.when(pl.program_id(0) == 0)
    def _():
        for number in range(2):
            for place, ref in enumerate((w_own, w_peer)):
                first = (2 * number + place) * part
                w_ref[:, first : first + part] = flip(ref[1 + number])

    dkv = dkv_ref[0].reshape(w_ref.shape[1], dkv_ref.shape[3])
    part_ref[...] = dot(w_ref[...], dkv)
    for slot, keep_ref in enumerate((near_ref, far_ref)):
        which = chip if slot == 0 else 1 - chip
        near = pl.ds(pl.multiple_of((2 * which + core) * share, 64), share)
        far = pl.ds(pl.multiple_of((2 * which + 1 - core) * share, 64), share)
        keep_ref[0] = part_ref[near, :frames]
        send_ref[slot, 0] = part_ref[far, :frames].astype(BF)


def memory_back(scal, dkv, w_in, frames):
    _, _, feats, padded = dkv.shape
    _, part, width = w_in[0].shape
    share = width // 4
    out = pl.BlockSpec((2, 1, share, frames), lambda j, s: (0, j, 0, 0))
    return call(
        memory_back_kernel,
        (2,),
        [
            pl.BlockSpec((1, 2, feats, padded), lambda j, s: (j, 0, 0, 0)),
            whole(3, part, width),
            whole(3, part, width),
        ],
        [out] + [pl.BlockSpec((1, share, frames), lambda j, s: (j, 0, 0))] * 2,
        [shaped((2, 2, share, frames), BF)] + [shaped((2, share, frames), F32)] * 2,
        [pltpu.VMEM((width, 2 * feats), BF), pltpu.VMEM((width, padded), F32)],
        (8 * frames * width * feats, 0, 14 << 20),
        "memory_back",
    )(scal, dkv, *w_in)


def memory_place_kernel(scal, keep_ref, got_ref, far_ref, out_ref):
    source = pl.program_id(0)

    @pl.when(source < 2)
    def _():
        out_ref[...] = (keep_ref[...] + got_ref[0].astype(F32)).astype(BF)

    @pl.when(source >= 2)
    def _():
        out_ref[...] = far_ref[...]


def memory_place(scal, keep, got, far):
    _, share, frames = keep.shape
    kept = pl.BlockSpec((1, share, frames), lambda i, s: (jnp.minimum(i, 1), 0, 0))
    near = pl.BlockSpec((1, 1, share, frames), lambda i, s: (0, jnp.minimum(i, 1), 0, 0))
    return call(
        memory_place_kernel,
        (4,),
        [kept, near, pl.BlockSpec((1, share, frames), lambda i, s: (jnp.maximum(i - 2, 0), 0, 0))],
        pl.BlockSpec((1, share, frames), lambda i, s: (s[9 + i], 0, 0)),
        shaped((4, share, frames), BF),
        [],
        (0, 0, 0),
        "memory_place",
    )(scal, keep, got, far)


def cross_weights_kernel(
    scal, mem_ref, dkv_ref, h_ref, dq_ref, dx_ref, o_ref,
    weights_ref, one_ref, two_ref, sum_ref, full_ref, grads, tail_ref,
):
    doc = pl.program_id(0)
    frames = mem_ref.shape[1]
    body = frames // BLOCK * BLOCK
    feats, padded = dkv_ref.shape[2:]

    @pl.when(doc == 0)
    def _():
        sum_ref[...] = jnp.zeros_like(sum_ref)
        tail_ref[...] = jnp.zeros_like(tail_ref)
        put_weights(
            scal,
            full_ref,
            weights_ref,
            two_ref,
            1,
            jnp.concatenate([dot(dq_ref[...], h_ref[...], TN), dot(o_ref[...], dx_ref[...], TN)], axis=0),
        )

    tail_ref[: frames - body, :] = mem_ref[0, body:, :]
    rows = dkv_ref[0].reshape(2 * feats, padded)
    part = dot(rows[:, :body], mem_ref[0, :body, :]) + dot(rows[:, body:], tail_ref[...])
    sum_ref[...] += dot(jnp.ones((8, padded), BF), dkv_ref[0, 1], NT)[0:1]

    @pl.when(doc == 0)
    def _():
        grads[...] = part

    @pl.when(doc == 1)
    def _():
        put_weights(scal, full_ref, weights_ref, one_ref, 0, grads[...] + part)


def cross_weights(scal, memory, dkv, h, dq, dx, o, n_dp):
    _, frames, width = memory.shape
    _, _, feats, padded = dkv.shape
    rows = h.shape[0]
    specs, shapes, blocked = weights_specs(width, feats, n_dp)
    return call(
        cross_weights_kernel,
        (2,),
        [
            pl.BlockSpec((1, frames, width), lambda j, s: (s[9 + j], 0, 0)),
            pl.BlockSpec((1, 2, feats, padded), lambda j, s: (j, 0, 0, 0)),
            whole(rows, width),
            whole(rows, feats),
            whole(rows, width),
            whole(rows, feats),
        ],
        specs + [whole(1, feats)],
        shapes + [shaped((1, feats), F32)],
        [blocked, pltpu.VMEM((2 * feats, width), F32), pltpu.VMEM((BLOCK, width), BF)],
        (8 * frames * width * feats, 0, 14 << 20),
        "cross_weights",
        WEIGHTS_VMEM,
    )(scal, memory, dkv, h, dq, dx, o)


def per_device(
    inputs, memory, segments, documents, cotangent, norm_gain, norm_shift, attn_in, attn_bias,
    attn_out, cross_in, cross_bias, cross_out, fc_in, fc_in_bias, fc_out, out_bias, n_dp,
):
    length, width = inputs.shape
    docs, frames, _ = memory.shape
    padded = -(-frames // BLOCK) * BLOCK
    longest = length - 2 * (length // 5)
    rows = min(length, -(-longest // BLOCK) * BLOCK)
    half = rows // 2
    shift = length - rows
    slot = lax.axis_index("tensor")
    core, chip = slot % 2, slot // 2
    place_dp = lax.axis_index("dp")
    bits = n_dp.bit_length() - 1

    def swap(value, axis, bit):
        size = n_dp if axis == "dp" else 4
        return lax.ppermute(value, axis, [(i, i ^ bit) for i in range(size)])

    def to_core(value):
        return swap(value, "tensor", 1)

    def to_chip(value):
        return swap(value, "tensor", 2)

    numbers = jnp.arange(docs, dtype=jnp.int32)
    edges = jnp.sum((segments[None, :] < numbers[:, None]).astype(jnp.int32), axis=1)
    which = jnp.max(jnp.where(segments[None, :] == numbers[:, None], documents[None, :], 0), axis=1)
    which = which - place_dp * docs
    first_chip = chip == 0
    edge_one = jnp.where(first_chip, edges[1], edges[2] - shift)
    edge_two = jnp.where(first_chip, edges[2], edges[3] - shift)
    mine = jnp.where(first_chip, which, jnp.roll(which, 2))
    scal = jnp.concatenate(
        [
            jnp.stack(
                [
                    core,
                    chip,
                    edges[2],
                    edge_one,
                    edge_two,
                    jnp.where(first_chip, 0, edge_one),
                    jnp.where(first_chip, edge_one, edge_two),
                    jnp.where(first_chip, edge_one, edge_two),
                    jnp.where(first_chip, edge_two, rows),
                ]
            ),
            mine,
            jnp.stack([place_dp & 1, (place_dp >> 1) & 1]),
        ]
    ).astype(jnp.int32)

    def after(value, *earlier):
        return lax.optimization_barrier((value, earlier))[0]

    attn_in = jnp.swapaxes(attn_in, 1, 2)
    cross_in = jnp.swapaxes(cross_in, 1, 2)
    w_self = (attn_in, to_chip(attn_in))
    w_self_out = (attn_out, to_chip(attn_out))
    biases = jnp.concatenate([attn_bias, cross_bias], axis=0)
    biases = jnp.concatenate([biases, to_chip(biases)], axis=1)
    w_cross = (cross_in, to_chip(after(cross_in, w_self[1])))
    w_cross_out = (cross_out, to_chip(after(cross_out, w_self[1])))

    memory = with_layout_constraint(memory, Layout(major_to_minor=(0, 1, 2)))
    memory, peer_in = lax.optimization_barrier((memory, w_self[1]))
    w_self = (attn_in, peer_in)
    x_win = lax.dynamic_slice_in_dim(inputs, chip * shift, rows)
    dy_win = lax.dynamic_slice_in_dim(cotangent, chip * shift, rows)

    def row(matrix, index):
        return matrix[index : index + 1]

    h1, q1, k1, v1, o1, lse1 = self_forward(
        scal, x_win, row(norm_gain, 0), row(norm_shift, 0), w_self, biases[0:2]
    )
    send, keep = project_out(scal, o1, w_self_out)
    k2, v2 = memory_project(scal, memory, w_cross, biases[3:4], padded)
    x1, h2_own = add_norm(
        scal, x_win, keep, to_core(send), row(out_bias, 0), row(norm_gain, 1), row(norm_shift, 1), True
    )
    h2, q2, o2, lse2, send, keep = cross_forward(
        scal, h2_own, to_core(h2_own), w_cross, biases[2:3], k2, v2, w_cross_out, frames
    )
    x2, h3_own = add_norm(
        scal, x1, keep, to_core(send), row(out_bias, 1), row(norm_gain, 2), row(norm_shift, 2), False
    )

    def spread(value):
        far = to_chip(value)
        return (value, to_core(value), far, to_core(far))

    h3, g, du, send, keep, fc_sum = feed_forward(
        scal, spread(h3_own), cotangent, fc_in, fc_in_bias[None], fc_out
    )
    more = to_core(send)
    far = fold(scal, keep, more)
    got = to_chip(far)
    du, g_low = after((du, g), far)
    out_send, out_keep = second_product(scal, g_low, fc_out, half)
    out_near = to_core(out_send)
    fc_in_grad, fc_out_grad = dot(h3, du, TN), dot(cotangent, g_low, TN)
    far_out = fold(scal, out_keep, out_near)
    got_out = to_chip(after(far_out, got))

    def pick_bit(value, axis, bit):
        mine = (place_dp >> bit) & 1
        stay = lax.dynamic_index_in_dim(value, mine, axis, keepdims=False)
        return stay, lax.dynamic_index_in_dim(value, 1 - mine, axis, keepdims=False).astype(BF)

    others = list(range(2, bits))
    blocked = (2,) * bits + (width // n_dp,)

    def add(value, got):
        return value + got.astype(F32)

    def mlp_chain(matrices):
        value = jnp.stack(matrices).reshape(2, *blocked, -1)
        for number, bit in enumerate([0, 1] + others):
            axis = 1 + bits - 1 - bit if number == 0 else value.ndim - 3
            value, send = pick_bit(value, axis, bit)
            (got,) = yield [(send, "dp", 1 << bit)]
            value = add(value, got)
        return value

    def weights_chain(full, one_send, two_send):
        got = yield [(one_send, "dp", 1), (two_send, "dp", 2)]
        stay, one_send, two_send = shares_one(scal, full, *got)
        got = yield [(one_send, "dp", 2), (two_send, "dp", 1)]
        near, far = shares_two(scal, stay, *got)
        (got,) = yield [(far, "tensor", 2)]
        value = add(near, got)
        value = value.reshape(2, *(2,) * (bits - 2), *value.shape[2:])
        for bit in others:
            value, send = pick_bit(value, value.ndim - 3, bit)
            (got,) = yield [(send, "dp", 1 << bit)]
            value = add(value, got)
        return value

    def send_all(items):
        return [swap(*item) for item in items]

    mlp = mlp_chain([fc_in_grad, fc_out_grad])
    mlp_sent = next(mlp)
    mlp_got = send_all(mlp_sent)
    got = after(got, mlp_sent[0][0], far_out)
    dx2, dx2_low, sums_three = norm_back(
        scal, dy_win, keep, got, x2, row(norm_gain, 2), True, False, more
    )
    dx2_other = to_core(dx2_low)
    dx2_full, dq2, dkv2, q2_sum, send, keep = cross_backward(
        scal, dx2_low, dx2_other, w_cross_out, q2, lse2, k2, v2, w_cross, frames
    )
    mlp_got, got_out = after((mlp_got, got_out), q2_sum)
    mlp_sent = mlp.send(mlp_got)
    mlp_got = send_all(mlp_sent)
    dkv2 = after(dkv2, mlp_sent[0][0])
    *cross_grads, v2_sum = cross_weights(scal, memory, dkv2, h2, dq2, dx2_full, o2, n_dp)
    cross = weights_chain(*cross_grads)
    cross_sent = next(cross)
    cross_got = send_all(cross_sent)
    out_own = output_rows(scal, x2, out_keep, out_near, got_out, row(out_bias, 2))
    out_far = to_chip(out_own)
    got = to_core(send)
    mlp_sent = mlp.send(after(mlp_got, v2_sum, out_own))
    mlp_got = send_all(mlp_sent)

    dkv2 = after(dkv2, cross_sent[0][0], cross_sent[1][0], mlp_sent[0][0], out_own, got)
    mem_send, mem_near, mem_keep = memory_back(scal, dkv2, w_cross, frames)
    mem_got = to_core(mem_send)
    keep = after(keep, mem_send)
    dx1, dx1_low, sums_two = norm_back(
        scal, dx2, keep, got, x1, row(norm_gain, 1), False, False, cost=1 << 26
    )
    mem_far = fold(scal, mem_keep, mem_got)
    dx1_other = after(to_core(dx1_low), mem_far)
    *own_grads, self_sum, send, keep = self_backward(
        scal, dx1_low, dx1_other, w_self_out, h1, q1, k1, v1, o1, lse1, w_self, n_dp
    )
    mem_far = to_chip(mem_far)
    out_far = after(out_far, self_sum)
    own = weights_chain(*own_grads)
    own_sent = next(own)
    own_got = send_all(own_sent)
    input_own, input_low, sums_one = norm_back(
        scal, dx1, keep, to_core(send), x_win, row(norm_gain, 0), False, True
    )
    cross_sent = cross.send(after(cross_got, sums_one))
    mlp_got = after(mlp_got, sums_one)
    mem_far = after(mem_far, cross_sent[0][0])
    input_low = after(input_low, mem_far)
    out_own, out_far, mlp_got = after((out_own, out_far, mlp_got), sums_one)

    def input_chain(value):
        (far,) = yield [(value, "tensor", 2)]
        (got,) = yield [(jnp.stack([value, far]), "tensor", 1)]
        return value, far, got

    def output_chain(value, far):
        (got,) = yield [(jnp.stack([value, far]), "tensor", 1)]
        return value, far, got

    part = self_sum.shape[1] // 2

    def sums_chain():
        heads = jnp.concatenate([self_sum, q2_sum, v2_sum])
        sums = jnp.concatenate(
            [sums_one, sums_two, sums_three, jnp.pad(heads, ((0, 0), (0, width - 2 * part))), fc_sum]
        )
        number = jnp.arange(sums.shape[0])[:, None]
        (near,) = yield [(sums, "tensor", 1)]
        sums = sums + jnp.where(number < 12, near, 0.0)
        (far,) = yield [(sums, "tensor", 2)]
        turned = jnp.where(number < 16, jnp.roll(far, -part, axis=1), 0.0)
        sums = sums + jnp.where(number < 12, far, turned)
        start = bits % 2
        if start:
            (got,) = yield [(sums, "dp", 1)]
            sums = sums + got
        for bit in range(start, bits, 2):
            one, two, three = yield [(sums, "dp", which << bit) for which in (1, 2, 3)]
            sums = (sums + one) + (two + three)
        return sums

    chains = [
        (0, own, own_sent, own_got),
        (0, input_chain(input_low), None, None),
        (0, sums_chain(), None, None),
        (OUT_ROUND, output_chain(out_own, out_far), None, None),
        (0, cross, cross_sent, None),
        (0, mlp, mlp_sent, mlp_got),
    ]
    results = [None] * len(chains)
    pending, came = {}, {}
    number = 0
    while number < 3 or pending:
        for i, (start, chain, sent, got) in enumerate(chains):
            if start == number:
                if sent is not None and got is not None:
                    came[i] = got
                elif sent is not None:
                    pending[i] = sent
                else:
                    pending[i] = next(chain) if got is None else chain.send(got)
        values = lax.optimization_barrier([[item[0] for item in items] for items in pending.values()])
        for i, held in zip(pending, values):
            came[i] = [swap(value, *item[1:]) for value, item in zip(held, pending[i])]
        if number == 1:
            mem_far, *_ = lax.optimization_barrier((mem_far, values))
            memory_grad = memory_place(scal, mem_near, mem_got, mem_far)
            came, memory_grad = lax.optimization_barrier((came, memory_grad))
        else:
            came = lax.optimization_barrier(came)
        pending = {}
        for i, got in came.items():
            try:
                pending[i] = chains[i][1].send(got)
            except StopIteration as stop:
                results[i] = stop.value
        came = {}
        number += 1
    own_share, input_parts, sums, output_parts, cross_share, mlp_share = results
    input_grad = place(scal, *input_parts, length, F32)
    output = place(scal, *output_parts, length, BF)
    memory_grad = jnp.swapaxes(memory_grad, 1, 2)
    gain_sum, shift_sum, out_sum, self_total, cross_total, fc_total = finish_sums(scal, sums, part)
    return (
        output,
        input_grad,
        memory_grad,
        gain_sum,
        shift_sum,
        jnp.stack([own_share[0, :, :part], own_share[0, :, part:], own_share[1, :, :part]]),
        self_total,
        own_share[1, :, part:].T,
        jnp.stack([cross_share[1, :, :part], cross_share[0, :, :part], cross_share[0, :, part:]]),
        cross_total,
        cross_share[1, :, part:].T,
        mlp_share[0],
        fc_total[0],
        mlp_share[1].T,
        out_sum,
    )


def solution(mesh):
    n_dp = mesh.shape["dp"]

    def run(*args):
        return per_device(*args, n_dp)

    return jax.shard_map(
        run,
        mesh=mesh,
        in_specs=(
            P("dp", None),
            P("dp", None, None),
            P("dp"),
            P("dp"),
            P("dp", None),
            P(),
            P(),
            P(None, None, "tensor"),
            P(None, "tensor"),
            P("tensor", None),
            P(None, None, "tensor"),
            P(None, "tensor"),
            P("tensor", None),
            P(None, "tensor"),
            P("tensor"),
            P("tensor", None),
            P(),
        ),
        out_specs=(
            P("dp", None),
            P("dp", None),
            P("dp", None, "tensor"),
            P(),
            P(),
            P(None, "dp", "tensor"),
            P(None, "tensor"),
            P("tensor", "dp"),
            P(None, "dp", "tensor"),
            P(None, "tensor"),
            P("tensor", "dp"),
            P("dp", "tensor"),
            P("tensor"),
            P("tensor", "dp"),
            P(),
        ),
        check_vma=False,
    )
```

```python
import jax
import jax.numpy as jnp
from jax import lax
from jax.experimental import pallas as pl
from jax.experimental.layout import Layout, with_layout_constraint
from jax.experimental.pallas import tpu as pltpu
from jax.sharding import PartitionSpec as P

HEAD = 64
PAIR = 2 * HEAD
BLOCK = 128
ROWS = 160
EPSILON = 1e-05
LOG2E = 1.4426950408889634
SCALE = HEAD ** (-0.5)
NEG = -1e30
BIG = 1e30
BF = jnp.bfloat16
F32 = jnp.float32
VMEM = 20 << 20
SMALL_VMEM = 12 << 20
OUT_ROUND = 2
CROSS_VMEM = 34 << 20
BACK_VMEM = 46 << 20
SELF_VMEM = 20 << 20
WEIGHTS_VMEM = 20 << 20
PROJECT = 512
FEED = 256
COST = 4

NT = (((1,), (1,)), ((), ()))
NN = (((1,), (0,)), ((), ()))
TN = (((0,), (0,)), ((), ()))


def dot(left, right, dims=NN):
    return lax.dot_general(left, right, dims, preferred_element_type=F32)


def norm_parts(values):
    centred = values - jnp.mean(values, axis=-1, keepdims=True)
    inverse = lax.rsqrt(jnp.mean(centred * centred, axis=-1, keepdims=True) + EPSILON)
    return centred * inverse, inverse


def call(kernel, grid, in_specs, out_specs, out_shape, scratch, cost, name, vmem=VMEM):
    flops, exps, moved = cost
    return pl.pallas_call(
        kernel,
        grid_spec=pltpu.PrefetchScalarGridSpec(
            num_scalar_prefetch=1,
            grid=grid,
            in_specs=in_specs,
            out_specs=out_specs,
            scratch_shapes=scratch,
        ),
        out_shape=out_shape,
        compiler_params=pltpu.CompilerParams(
            dimension_semantics=("arbitrary",) * len(grid), vmem_limit_bytes=vmem
        ),
        cost_estimate=pl.CostEstimate(
            flops=COST * flops + 1, transcendentals=COST * exps, bytes_accessed=COST * moved + 1
        ),
        name=name,
    )


def whole(*shape):
    zeros = (0,) * len(shape)
    return pl.BlockSpec(shape, lambda *_: zeros)


def shaped(shape, dtype):
    return jax.ShapeDtypeStruct(shape, dtype)


def two_heads(rows):
    lane = lax.broadcasted_iota(jnp.int32, rows.shape, 1)
    zero = jnp.zeros_like(rows)
    return jnp.concatenate(
        [jnp.where(lane < HEAD, rows, zero), jnp.where(lane < HEAD, zero, rows)], axis=0
    )


def pick_heads(both):
    row = lax.broadcasted_iota(jnp.int32, (PAIR, BLOCK), 0)
    return jnp.where(row < HEAD, both[:, :BLOCK], both[:, BLOCK:]).T


def row_lanes(first):
    lane = lax.broadcasted_iota(jnp.int32, (1, 2 * BLOCK), 1)
    return first + jnp.where(lane < BLOCK, lane, lane - BLOCK)


def flip(matrix):
    return matrix.astype(F32).T.astype(BF)


def split_out(scal, total, send_ref, keep_ref, half):
    core = scal[0]
    here = pl.multiple_of(core * half, half)
    there = pl.multiple_of((1 - core) * half, half)
    keep_ref[...] = total[pl.ds(here, half), :]
    send_ref[...] = total[pl.ds(there, half), :].astype(BF)


def join_halves(scal, own_ref, other_ref, full_ref, half):
    core = scal[0]
    full_ref[pl.ds(pl.multiple_of(core * half, half), half), :] = own_ref[...]
    full_ref[pl.ds(pl.multiple_of((1 - core) * half, half), half), :] = other_ref[...]


def join_weights(own_ref, peer_ref, full_ref):
    part = own_ref.shape[-2]
    full_ref[..., :part, :] = own_ref[...]
    full_ref[..., part:, :] = peer_ref[...]


def join_stack(own_ref, peer_ref, full_ref):
    count, part, _ = own_ref.shape
    for number in range(count):
        first = 2 * part * number
        full_ref[first : first + part, :] = own_ref[number]
        full_ref[first + part : first + 2 * part, :] = peer_ref[number]


def put_weights(scal, full_ref, stay_ref, send_ref, group, rows):
    part = rows.shape[0] // 4
    count, size = full_ref.shape[:2]
    for side in range(2):
        one = rows[side * part : (side + 1) * part]
        two = rows[(2 + side) * part : (3 + side) * part]
        turned = jnp.concatenate([one, two], axis=0).T
        for block in range(count):
            full_ref[block] = turned[block * size : (block + 1) * size]
        for rest in range(count // 4):
            for other in range(2):
                stay = 2 * other + scal[13] if group == 0 else 2 * scal[14] + other
                send = 2 * other + 1 - scal[13] if group == 0 else 2 * (1 - scal[14]) + other
                stay_ref[group, side, rest, other] = full_ref[4 * rest + stay]
                send_ref[side, rest, other] = full_ref[4 * rest + send].astype(BF)


def weights_specs(width, feats, n_dp):
    size = width // n_dp
    half = (2, n_dp // 4, 2, size, feats)
    return (
        [whole(2, *half), whole(*half), whole(*half)],
        [shaped((2, *half), F32), shaped(half, BF), shaped(half, BF)],
        pltpu.VMEM((n_dp, size, feats), F32),
    )


def shares_one_kernel(scal, full_ref, one_ref, two_ref, stay_ref, one_send, two_send):
    low, high = scal[13], scal[14]
    for side in range(2):
        for rest in range(one_ref.shape[1]):

            def one_sum(bit):
                return full_ref[0, side, rest, bit] + one_ref[side, rest, bit].astype(F32)

            def two_sum(bit):
                return full_ref[1, side, rest, bit] + two_ref[side, rest, bit].astype(F32)

            stay_ref[0, side, rest] = one_sum(high)
            one_send[side, rest] = one_sum(1 - high).astype(BF)
            stay_ref[1, side, rest] = two_sum(low)
            two_send[side, rest] = two_sum(1 - low).astype(BF)


def shares_one(scal, full, one, two):
    _, _, count, _, size, feats = full.shape
    stay = (2, 2, count, size, feats)
    send = (2, count, size, feats)
    return call(
        shares_one_kernel,
        (1,),
        [whole(*full.shape), whole(*one.shape), whole(*one.shape)],
        [whole(*stay), whole(*send), whole(*send)],
        [shaped(stay, F32), shaped(send, BF), shaped(send, BF)],
        [],
        (0, 0, 0),
        "shares_one",
        SMALL_VMEM,
    )(scal, full, one, two)


def shares_two_kernel(scal, stay_ref, one_ref, two_ref, near_ref, far_ref):
    for group, got in enumerate((one_ref, two_ref)):
        near_ref[group] = stay_ref[group, 0] + got[0].astype(F32)
        far_ref[group] = (stay_ref[group, 1] + got[1].astype(F32)).astype(BF)


def shares_two(scal, stay, one, two):
    out = (2, *stay.shape[2:])
    return call(
        shares_two_kernel,
        (1,),
        [whole(*stay.shape), whole(*one.shape), whole(*one.shape)],
        [whole(*out), whole(*out)],
        [shaped(out, F32), shaped(out, BF)],
        [],
        (0, 0, 0),
        "shares_two",
        SMALL_VMEM,
    )(scal, stay, one, two)


def self_mask(scal, count, first):
    rows = row_lanes(first)
    edge_one, edge_two = scal[3], scal[4]
    begin = jnp.where(rows >= edge_two, edge_two, jnp.where(rows >= edge_one, edge_one, 0))
    keys = lax.broadcasted_iota(jnp.int32, (count, 2 * BLOCK), 0)
    return (keys >= begin) & (keys <= rows)


def self_forward_kernel(
    scal, x_ref, gain_ref, shift_ref, w_own, w_peer, b_ref,
    h_ref, q_ref, k_ref, v_ref, o_ref, lse_ref, vt, w_ref,
):
    rows = x_ref.shape[0]
    join_stack(w_own, w_peer, w_ref)
    normed, _ = norm_parts(x_ref[...].astype(F32))
    h_ref[...] = (normed * gain_ref[...] + shift_ref[...]).astype(BF)
    part = q_ref.shape[1]
    projected = dot(h_ref[...], w_ref[...], NT)
    q_ref[...] = (projected[:, :part] + b_ref[0:1, :]).astype(BF)
    k_ref[...] = projected[:, part : 2 * part].astype(BF)
    v_ref[...] = (projected[:, 2 * part :] + b_ref[1:2, :]).astype(BF)
    vt[...] = flip(v_ref[...])
    for block in range(rows // BLOCK):
        first = block * BLOCK
        count = first + BLOCK
        kept = self_mask(scal, count, first)
        for pair in range(part // PAIR):
            here = lanes(pair)
            queries = two_heads(q_ref[first : first + BLOCK, here])
            scores = jnp.where(kept, dot(k_ref[:count, here], queries, NT), NEG)
            largest = jnp.max(scores, axis=0, keepdims=True)
            chances = jnp.exp2((scores - largest) * (SCALE * LOG2E))
            totals = jnp.sum(chances, axis=0, keepdims=True)
            mixed = dot(vt[here, :count], chances.astype(BF)) * (1.0 / totals)
            o_ref[first : first + BLOCK, here] = pick_heads(mixed).astype(BF)
            lse_ref[pair, block] = largest * (SCALE * LOG2E) + jnp.log(totals) * LOG2E


def project_out_kernel(scal, o_ref, wo_own, wo_peer, send_ref, keep_ref, total):
    part = wo_own.shape[0]
    wo = jnp.concatenate([wo_own[...], wo_peer[...]], axis=0)
    total[...] = dot(o_ref[...], wo)
    split_out(scal, total, send_ref, keep_ref, o_ref.shape[0] // 2)


def project_out(scal, mixed, w_out):
    rows, feats = mixed.shape
    part, width = w_out[0].shape
    half = rows // 2
    return call(
        project_out_kernel,
        (1,),
        [whole(rows, feats), whole(part, width), whole(part, width)],
        [whole(half, width)] * 2,
        [shaped((half, width), BF), shaped((half, width), F32)],
        [pltpu.VMEM((rows, width), F32)],
        (0, 0, 0),
        "project_out",
        SMALL_VMEM,
    )(scal, mixed, *w_out)


def self_forward(scal, x_win, gain, shift, w_in, bias):
    rows, width = x_win.shape
    part = w_in[0].shape[1]
    feats = 2 * part
    pairs = feats // PAIR
    blocks = rows // BLOCK
    return call(
        self_forward_kernel,
        (1,),
        [
            whole(rows, width),
            whole(1, width),
            whole(1, width),
            whole(3, part, width),
            whole(3, part, width),
            whole(2, feats),
        ],
        [whole(rows, width)]
        + [whole(rows, feats)] * 4
        + [whole(pairs, blocks, 1, 2 * BLOCK)],
        [shaped((rows, width), BF)]
        + [shaped((rows, feats), BF)] * 4
        + [shaped((pairs, blocks, 1, 2 * BLOCK), F32)],
        [
            pltpu.VMEM((feats, rows), BF),
            pltpu.VMEM((3 * feats, width), BF),
        ],
        (8 * rows * width * feats + 4 * rows * rows * feats, rows * rows * 6, 12 << 20),
        "self_forward",
    )(scal, x_win, gain, shift, *w_in, bias)


def self_backward_kernel(
    scal, own_ref, other_ref, wo_own, wo_peer, h_ref, q_ref, k_ref, v_ref, o_ref, lse_ref,
    w_own, w_peer, weights_ref, one_ref, two_ref, sum_ref, send_ref, keep_ref,
    full_ref, dx_ref, grad_ref, total, kt, do, dks, dvs, w_ref, wo_ref,
):
    rows, feats = q_ref.shape
    join_halves(scal, own_ref, other_ref, dx_ref, rows // 2)
    join_stack(w_own, w_peer, w_ref)
    join_weights(wo_own, wo_peer, wo_ref)
    do[...] = dot(dx_ref[...], wo_ref[...], NT).astype(BF)
    kt[...] = flip(k_ref[...])
    for block in reversed(range(rows // BLOCK)):
        first = block * BLOCK
        count = first + BLOCK
        kept = self_mask(scal, count, first)
        for pair in range(feats // PAIR):
            here = lanes(pair)
            queries = two_heads(q_ref[first : first + BLOCK, here])
            grads = two_heads(do[first : first + BLOCK, here])
            scores = dot(k_ref[:count, here], queries, NT)
            chances = jnp.exp2(scores * (SCALE * LOG2E) - lse_ref[pair, block])
            chances = jnp.where(kept, chances, 0.0)
            prob_grad = dot(v_ref[:count, here], grads, NT)
            shared = jnp.sum(chances * prob_grad, axis=0, keepdims=True)
            score_grad = (chances * (prob_grad - shared)).astype(BF)
            dv = dot(chances.astype(BF), grads)
            dk = dot(score_grad, queries)
            if count == rows:
                dvs[:, here] = dv
                dks[:, here] = dk
            else:
                dvs[:count, here] += dv
                dks[:count, here] += dk
            turned = pick_heads(dot(kt[here, :count], score_grad)) * SCALE
            grad_ref[first : first + BLOCK, here] = turned.astype(BF)
    grad_ref[:, feats : 2 * feats] = (dks[...] * SCALE).astype(BF)
    grad_ref[:, 2 * feats :] = dvs[...].astype(BF)
    sum_ref[0:1, :] = jnp.sum(grad_ref[:, :feats].astype(F32), axis=0, keepdims=True)
    sum_ref[1:2, :] = jnp.sum(grad_ref[:, 2 * feats :].astype(F32), axis=0, keepdims=True)
    total[...] = dot(grad_ref[...], w_ref[...])
    split_out(scal, total, send_ref, keep_ref, rows // 2)
    hidden = h_ref[...]
    put_weights(scal, full_ref, weights_ref, one_ref, 0, dot(grad_ref[:, : 2 * feats], hidden, TN))
    put_weights(
        scal,
        full_ref,
        weights_ref,
        two_ref,
        1,
        jnp.concatenate(
            [dot(grad_ref[:, 2 * feats :], hidden, TN), dot(o_ref[...], dx_ref[...], TN)], axis=0
        ),
    )


def self_backward(scal, own, other, w_out, h, q, k, v, o, lse, w_in, n_dp):
    rows, feats = q.shape
    width = own.shape[1]
    part = feats // 2
    pairs = feats // PAIR
    blocks = rows // BLOCK
    half = rows // 2
    specs, shapes, blocked = weights_specs(width, feats, n_dp)
    return call(
        self_backward_kernel,
        (1,),
        [whole(half, width)] * 2
        + [whole(part, width)] * 2
        + [whole(rows, width)]
        + [whole(rows, feats)] * 4
        + [whole(pairs, blocks, 1, 2 * BLOCK)]
        + [whole(3, part, width)] * 2,
        specs
        + [
            whole(2, feats),
            whole(half, width),
            whole(half, width),
        ],
        shapes
        + [
            shaped((2, feats), F32),
            shaped((half, width), BF),
            shaped((half, width), F32),
        ],
        [
            blocked,
            pltpu.VMEM((rows, width), BF),
            pltpu.VMEM((rows, 3 * feats), BF),
            pltpu.VMEM((rows, width), F32),
            pltpu.VMEM((feats, rows), BF),
            pltpu.VMEM((rows, feats), BF),
            pltpu.VMEM((rows, feats), F32),
            pltpu.VMEM((rows, feats), F32),
            pltpu.VMEM((3 * feats, width), BF),
            pltpu.VMEM((feats, width), BF),
        ],
        (8 * rows * width * feats + 10 * rows * rows * feats, rows * rows * 6, 14 << 20),
        "self_backward",
        SELF_VMEM,
    )(scal, own, other, *w_out, h, q, k, v, o, lse, *w_in)


def add_norm_kernel(scal, base_ref, keep_ref, got_ref, bias_ref, gain_ref, shift_ref, x_ref, h_ref):
    value = base_ref[...].astype(F32) + (keep_ref[...] + got_ref[...].astype(F32)) + bias_ref[...]
    x_ref[...] = value
    normed, _ = norm_parts(value)
    h_ref[...] = (normed * gain_ref[...] + shift_ref[...]).astype(BF)


def add_norm(scal, base, keep, got, bias, gain, shift, by_core):
    half, width = keep.shape
    steps = half // ROWS
    block = pl.BlockSpec((ROWS, width), lambda i, s: (i, 0))
    base_spec = pl.BlockSpec((ROWS, width), lambda i, s: (s[0] * steps + i, 0)) if by_core else block
    return call(
        add_norm_kernel,
        (steps,),
        [base_spec, block, block] + [whole(1, width)] * 3,
        [block] * 2,
        [shaped((half, width), F32), shaped((half, width), BF)],
        [],
        (0, 0, 0),
        "add_norm",
        SMALL_VMEM,
    )(scal, base, keep, got, bias, gain, shift)


def norm_back_more_kernel(
    scal, base_ref, keep_ref, got_ref, x_ref, gain_ref, more_ref, dx_ref, low_ref, sum_ref
):
    norm_back_body(
        scal, base_ref, keep_ref[0] + more_ref[0].astype(F32), got_ref, x_ref, gain_ref,
        dx_ref, low_ref, sum_ref,
    )


def norm_back_kernel(scal, base_ref, keep_ref, got_ref, x_ref, gain_ref, dx_ref, low_ref, sum_ref):
    norm_back_body(
        scal, base_ref, keep_ref[...], got_ref, x_ref, gain_ref, dx_ref, low_ref, sum_ref
    )


def norm_back_body(scal, base_ref, keep, got_ref, x_ref, gain_ref, dx_ref, low_ref, sum_ref):
    step, steps = pl.program_id(0), pl.num_programs(0)
    base = base_ref[...].astype(F32)
    grad = keep + got_ref[...].astype(F32)
    row = (scal[0] * steps + step) * ROWS + lax.broadcasted_iota(jnp.int32, (ROWS, 1), 0)
    valid = (row >= scal[5]) & (row < scal[8])
    grad = jnp.where(valid, grad, 0.0)
    base = jnp.where(valid, base, 0.0)
    normed, inverse = norm_parts(x_ref[...].astype(F32))
    scaled = grad * gain_ref[...]
    total = base + inverse * (
        scaled
        - jnp.mean(scaled, axis=-1, keepdims=True)
        - normed * jnp.mean(scaled * normed, axis=-1, keepdims=True)
    )
    dx_ref[...] = total
    low_ref[...] = total.astype(BF)

    @pl.when(step == 0)
    def _():
        sum_ref[...] = jnp.zeros_like(sum_ref)

    sum_ref[0:1, :] += jnp.sum(grad * normed, axis=0, keepdims=True)
    sum_ref[1:2, :] += jnp.sum(grad, axis=0, keepdims=True)
    sum_ref[2:3, :] += jnp.sum(total, axis=0, keepdims=True)
    sum_ref[3:4, :] += jnp.sum(base, axis=0, keepdims=True)


def norm_back(scal, base, keep, got, x, gain, base_by_core, x_by_core, more=None, cost=0):
    half, width = got.shape

    steps = half // ROWS
    block = pl.BlockSpec((ROWS, width), lambda i, s: (i, 0))
    cored = pl.BlockSpec((ROWS, width), lambda i, s: (s[0] * steps + i, 0))

    stacked = pl.BlockSpec((1, ROWS, width), lambda i, s: (0, i, 0))

    def spec(by_core):
        return cored if by_core else block

    return call(
        norm_back_kernel if more is None else norm_back_more_kernel,
        (steps,),
        [
            spec(base_by_core),
            block if more is None else stacked,
            block,
            spec(x_by_core),
            whole(1, width),
        ]
        + [stacked] * (more is not None),
        [block, block, whole(4, width)],
        [shaped((half, width), F32), shaped((half, width), BF), shaped((4, width), F32)],
        [],
        (0, 0, cost),
        "norm_back",
        SMALL_VMEM,
    )(scal, base, keep, got, x, gain, *([] if more is None else [more]))


def pieces(total, size):
    return [(first, min(size, total - first)) for first in range(0, total, size)]


def memory_project_kernel(scal, mem_ref, w_own, w_peer, b_ref, k_ref, v_ref, w_ref):
    feats = k_ref.shape[2]

    @pl.when(pl.program_id(0) == 0)
    def _():
        for number in range(2):
            rows = slice(number * feats, (number + 1) * feats)
            join_weights(w_own.at[1 + number], w_peer.at[1 + number], w_ref.at[rows])

    frames = mem_ref.shape[1]
    padded = k_ref.shape[1]
    tail = padded - BLOCK
    k_ref[0, tail:padded, :] = jnp.zeros((BLOCK, k_ref.shape[2]), BF)
    v_ref[0, tail:padded, :] = jnp.zeros((BLOCK, k_ref.shape[2]), BF)
    for first, size in pieces(frames, PROJECT):
        both = dot(mem_ref[0, first : first + size, :], w_ref[...], NT)
        k_ref[0, first : first + size, :] = both[:, :feats].astype(BF)
        v_ref[0, first : first + size, :] = (both[:, feats:] + b_ref[...]).astype(BF)


def memory_project(scal, memory, w_kv, bias, padded):
    _, frames, width = memory.shape
    part = w_kv[0].shape[1]
    feats = 2 * part
    out = pl.BlockSpec((1, padded, feats), lambda j, s: (j, 0, 0))
    return call(
        memory_project_kernel,
        (2,),
        [
            pl.BlockSpec((1, frames, width), lambda j, s: (s[9 + j], 0, 0)),
            whole(3, part, width),
            whole(3, part, width),
            whole(1, feats),
        ],
        [out, out],
        [shaped((2, padded, feats), BF)] * 2,
        [pltpu.VMEM((2 * feats, width), BF)],
        (8 * frames * width * feats, 0, 12 << 20),
        "memory_project",
    )(scal, memory, *w_kv, bias)


def block_span(scal, doc):
    low, high = scal[5 + 2 * doc], scal[6 + 2 * doc]
    return low, high, low // BLOCK, (high + BLOCK - 1) // BLOCK


def lanes(pair):
    return slice(pair * PAIR, (pair + 1) * PAIR)


def cross_forward_kernel(
    scal, own_ref, other_ref, wq_own, wq_peer, bq_ref, k_ref, v_ref, wo_own, wo_peer,
    h_ref, q_ref, o_ref, lse_ref, send_ref, keep_ref, total, vt, s_ref, wq_ref, wo_ref, *, frames,
):
    doc = pl.program_id(0)
    rows, feats = q_ref.shape
    padded = k_ref.shape[1]

    @pl.when(doc == 0)
    def _():
        join_halves(scal, own_ref, other_ref, h_ref, rows // 2)
        join_weights(wq_own.at[0], wq_peer.at[0], wq_ref)
        join_weights(wo_own, wo_peer, wo_ref)
        q_ref[...] = (dot(h_ref[...], wq_ref[...], NT) + bq_ref[...]).astype(BF)
        o_ref[...] = jnp.zeros_like(o_ref)
        lse_ref[...] = jnp.zeros_like(lse_ref)

    vt[...] = flip(v_ref[0])
    low, high, start, stop = block_span(scal, doc)

    def one_block(block, carry):
        first = pl.multiple_of(block * BLOCK, BLOCK)
        number = row_lanes(first)
        inside = (number >= low) & (number < high)
        for pair in range(feats // PAIR):
            here = lanes(pair)
            queries = two_heads(q_ref[pl.ds(first, BLOCK), here])
            s_ref[pair] = dot(k_ref[0, :, here], queries, NT)
            s_ref[pair, frames:padded, :] = jnp.full((padded - frames, 2 * BLOCK), NEG, F32)
            scores = s_ref[pair]
            largest = jnp.max(scores, axis=0, keepdims=True)
            chances = jnp.exp2((scores - largest) * (SCALE * LOG2E))
            totals = jnp.sum(chances, axis=0, keepdims=True)
            mixed = dot(vt[here, :], chances.astype(BF)) * jnp.where(inside, 1.0 / totals, 0.0)
            o_ref[pl.ds(first, BLOCK), here] += pick_heads(mixed).astype(BF)
            log_total = largest * (SCALE * LOG2E) + jnp.log(totals) * LOG2E
            lse_ref[pair, block] = jnp.where(inside, log_total, lse_ref[pair, block])
        return carry

    lax.fori_loop(start, stop, one_block, 0)

    @pl.when(doc == 1)
    def _():
        total[...] = dot(o_ref[...], wo_ref[...])
        split_out(scal, total, send_ref, keep_ref, rows // 2)


def cross_forward(scal, own, other, wq, bq, k, v, w_out, frames):
    half, width = own.shape
    rows = 2 * half
    _, padded, feats = k.shape
    pairs = feats // PAIR
    blocks = rows // BLOCK
    keyed = pl.BlockSpec((1, padded, feats), lambda j, s: (j, 0, 0))

    def kernel(*refs):
        cross_forward_kernel(*refs, frames=frames)

    return call(
        kernel,
        (2,),
        [
            whole(half, width),
            whole(half, width),
            whole(1, feats // 2, width),
            whole(1, feats // 2, width),
            whole(1, feats),
            keyed,
            keyed,
            whole(feats // 2, width),
            whole(feats // 2, width),
        ],
        [
            whole(rows, width),
            whole(rows, feats),
            whole(rows, feats),
            whole(pairs, blocks, 1, 2 * BLOCK),
            whole(half, width),
            whole(half, width),
        ],
        [
            shaped((rows, width), BF),
            shaped((rows, feats), BF),
            shaped((rows, feats), BF),
            shaped((pairs, blocks, 1, 2 * BLOCK), F32),
            shaped((half, width), BF),
            shaped((half, width), F32),
        ],
        [
            pltpu.VMEM((rows, width), F32),
            pltpu.VMEM((feats, padded), BF),
            pltpu.VMEM((pairs, padded, 2 * BLOCK), F32),
            pltpu.VMEM((feats, width), BF),
            pltpu.VMEM((feats, width), BF),
        ],
        (4 * rows * width * feats + 4 * rows * padded * feats, rows * padded * 6, 14 << 20),
        "cross_forward",
        CROSS_VMEM,
    )(scal, own, other, *wq, bq, k, v, *w_out)


def cross_backward_kernel(
    scal, own_ref, other_ref, wo_own, wo_peer, q_ref, lse_ref, k_ref, v_ref, wq_own, wq_peer,
    dx_ref, dq_ref, dkv_ref, sum_ref, send_ref, keep_ref,
    total, kt, do, dks, dvs, wq_ref, wo_ref, *, frames,
):
    doc = pl.program_id(0)
    rows, feats = q_ref.shape
    padded = k_ref.shape[1]

    @pl.when(doc == 0)
    def _():
        join_halves(scal, own_ref, other_ref, dx_ref, rows // 2)
        join_weights(wq_own.at[0], wq_peer.at[0], wq_ref)
        join_weights(wo_own, wo_peer, wo_ref)
        do[...] = dot(dx_ref[...], wo_ref[...], NT).astype(BF)
        dq_ref[...] = jnp.zeros_like(dq_ref)

    kt[...] = flip(k_ref[0])
    dks[...] = jnp.zeros_like(dks)
    dvs[...] = jnp.zeros_like(dvs)
    low, high, start, stop = block_span(scal, doc)

    def one_block(block, carry):
        first = pl.multiple_of(block * BLOCK, BLOCK)
        number = row_lanes(first)
        inside = (number >= low) & (number < high)
        for pair in range(feats // PAIR):
            here = lanes(pair)
            queries = two_heads(q_ref[pl.ds(first, BLOCK), here])
            grads = two_heads(do[pl.ds(first, BLOCK), here])
            log_total = jnp.where(inside, lse_ref[pair, block], BIG)
            chances = jnp.exp2(dot(k_ref[0, :, here], queries, NT) * (SCALE * LOG2E) - log_total)
            prob_grad = dot(v_ref[0, :, here], grads, NT)
            shared = jnp.sum(chances * prob_grad, axis=0, keepdims=True)
            score_grad = (chances * (prob_grad - shared)).astype(BF)
            dvs[:, here] += dot(chances.astype(BF), grads)
            dks[:, here] += dot(score_grad, queries)
            turned = pick_heads(dot(kt[here, :], score_grad)) * SCALE
            dq_ref[pl.ds(first, BLOCK), here] += turned.astype(BF)
        return carry

    lax.fori_loop(start, stop, one_block, 0)
    tail = jnp.zeros((padded - frames, feats), F32)
    dks[frames:, :] = tail
    dvs[frames:, :] = tail
    dkv_ref[0, 0] = (dks[...] * SCALE).T.astype(BF)
    dkv_ref[0, 1] = dvs[...].T.astype(BF)

    @pl.when(doc == 1)
    def _():
        sum_ref[...] = jnp.sum(dq_ref[...].astype(F32), axis=0, keepdims=True)
        total[...] = dot(dq_ref[...], wq_ref[...])
        split_out(scal, total, send_ref, keep_ref, rows // 2)


def cross_backward(scal, own, other, w_out, q, lse, k, v, wq, frames):
    half, width = own.shape
    rows = 2 * half
    _, padded, feats = k.shape
    pairs = feats // PAIR
    blocks = rows // BLOCK
    keyed = pl.BlockSpec((1, padded, feats), lambda j, s: (j, 0, 0))

    def kernel(*refs):
        cross_backward_kernel(*refs, frames=frames)

    return call(
        kernel,
        (2,),
        [
            whole(half, width),
            whole(half, width),
            whole(feats // 2, width),
            whole(feats // 2, width),
            whole(rows, feats),
            whole(pairs, blocks, 1, 2 * BLOCK),
            keyed,
            keyed,
            whole(1, feats // 2, width),
            whole(1, feats // 2, width),
        ],
        [
            whole(rows, width),
            whole(rows, feats),
            pl.BlockSpec((1, 2, feats, padded), lambda j, s: (j, 0, 0, 0)),
            whole(1, feats),
            whole(half, width),
            whole(half, width),
        ],
        [
            shaped((rows, width), BF),
            shaped((rows, feats), BF),
            shaped((2, 2, feats, padded), BF),
            shaped((1, feats), F32),
            shaped((half, width), BF),
            shaped((half, width), F32),
        ],
        [
            pltpu.VMEM((rows, width), F32),
            pltpu.VMEM((feats, padded), BF),
            pltpu.VMEM((rows, feats), BF),
            pltpu.VMEM((padded, feats), F32),
            pltpu.VMEM((padded, feats), F32),
            pltpu.VMEM((feats, width), BF),
            pltpu.VMEM((feats, width), BF),
        ],
        (4 * rows * width * feats + 10 * rows * padded * feats, rows * padded * 6, 18 << 20),
        "cross_backward",
        BACK_VMEM,
    )(scal, own, other, *w_out, q, lse, k, v, *wq)


def finish_sums_kernel(scal, sum_ref, gain_ref, shift_ref, bias_ref, self_ref, cross_ref, fc_ref):
    part = self_ref.shape[1]
    for norm in range(3):
        gain_ref[norm : norm + 1, :] = sum_ref[4 * norm : 4 * norm + 1, :]
        shift_ref[norm : norm + 1, :] = sum_ref[4 * norm + 1 : 4 * norm + 2, :]
    for number, line in enumerate((6, 10, 11)):
        bias_ref[number : number + 1, :] = sum_ref[line : line + 1, :]
    self_ref[...] = sum_ref[12:14, :part]
    cross_ref[...] = sum_ref[14:16, :part]
    fc_ref[...] = sum_ref[16:17, :]


def finish_sums(scal, sums, part):
    rows, width = sums.shape
    shapes = [(3, width)] * 3 + [(2, part)] * 2 + [(1, width)]
    return call(
        finish_sums_kernel,
        (1,),
        [whole(rows, width)],
        [whole(*shape) for shape in shapes],
        [shaped(shape, F32) for shape in shapes],
        [],
        (0, 0, 0),
        "finish_sums",
        SMALL_VMEM,
    )(scal, sums)


def place_rows(scal, refs, full_ref):
    core, chip, edge = scal[0], scal[1], scal[2]
    half = refs[0].shape[-2]
    shift = full_ref.shape[0] - 2 * half
    for number, ref in enumerate(refs):
        which_chip = chip if number < 2 else 1 - chip
        which_core = core if number % 2 == 0 else 1 - core
        first = pl.multiple_of(which_chip * shift + which_core * half, 64)
        row = first + lax.broadcasted_iota(jnp.int32, (half, 1), 0)
        valid = (row < edge) == (which_chip == 0)
        part = (ref[...] if ref.ndim == 2 else ref[0]).astype(full_ref.dtype)
        full_ref[pl.ds(first, half), :] = jnp.where(valid, part, full_ref[pl.ds(first, half), :])


def place_kernel(scal, a_ref, b_ref, c_ref, d_ref, out_ref):
    place_rows(scal, (a_ref, b_ref, c_ref, d_ref), out_ref)


def place(scal, own, far, got, length, dtype):
    half, width = own.shape
    near_half = pl.BlockSpec((1, half, width), lambda *_: (0, 0, 0))
    far_half = pl.BlockSpec((1, half, width), lambda *_: (1, 0, 0))
    return call(
        place_kernel,
        (1,),
        [whole(half, width), near_half, whole(half, width), far_half],
        whole(length, width),
        shaped((length, width), dtype),
        [],
        (0, 0, 0),
        "place_rows",
        SMALL_VMEM,
    )(scal, own, got, far, got)


def window_shares(scal, full_ref, send_ref, keep_ref):
    core, chip = scal[0], scal[1]
    half = keep_ref.shape[1]
    shift = full_ref.shape[0] - 2 * half
    for slot in range(2):
        first = (chip if slot == 0 else 1 - chip) * shift
        near = pl.multiple_of(first + core * half, 64)
        far = pl.multiple_of(first + (1 - core) * half, 64)
        keep_ref[slot] = full_ref[pl.ds(near, half), :]
        send_ref[slot] = full_ref[pl.ds(far, half), :].astype(BF)


def second_product_kernel(scal, g_ref, w_ref, send_ref, keep_ref, full_ref):
    full_ref[...] = dot(g_ref[...], w_ref[...])
    window_shares(scal, full_ref, send_ref, keep_ref)


def second_product(scal, g, w_out, half):
    length, hidden = g.shape
    width = w_out.shape[1]
    return call(
        second_product_kernel,
        (1,),
        [whole(length, hidden), whole(hidden, width)],
        [whole(2, half, width)] * 2,
        [shaped((2, half, width), BF), shaped((2, half, width), F32)],
        [pltpu.VMEM((length, width), F32)],
        (0, 0, 0),
        "second_product",
    )(scal, g, w_out)


def fold_kernel(scal, keep_ref, got_ref, out_ref):
    keep = keep_ref[0] if keep_ref.ndim > out_ref.ndim else keep_ref[...]
    out_ref[...] = (keep + got_ref[0].astype(F32)).astype(BF)


def fold(scal, keep, got):
    shape = got.shape[1:]
    second = pl.BlockSpec((1, *shape), lambda i, s: (1, *(0,) * len(shape)))
    return call(
        fold_kernel,
        (1,),
        [second if keep.ndim == got.ndim else whole(*shape), second],
        whole(*shape),
        shaped(shape, BF),
        [],
        (0, 0, 0),
        "fold",
        SMALL_VMEM,
    )(scal, keep, got)


def output_rows_kernel(scal, x_ref, keep_ref, near_ref, far_ref, bias_ref, out_ref):
    value = keep_ref[0] + near_ref[0].astype(F32) + far_ref[...].astype(F32)
    out_ref[...] = (x_ref[...] + value + bias_ref[...]).astype(BF)


def output_rows(scal, x, keep, near, far, bias):
    half, width = x.shape
    first = pl.BlockSpec((1, half, width), lambda i, s: (0, 0, 0))
    return call(
        output_rows_kernel,
        (1,),
        [whole(half, width), first, first, whole(half, width), whole(1, width)],
        whole(half, width),
        shaped((half, width), BF),
        [],
        (0, 0, 0),
        "output_rows",
        SMALL_VMEM,
    )(scal, x, keep, near, far, bias)


def feed_forward_kernel(
    scal, a_ref, b_ref, c_ref, d_ref, dy_ref, wi_ref, bi_ref, wo_ref,
    h_ref, g_ref, du_ref, send_ref, keep_ref, sum_ref, dh_ref,
):
    step = pl.program_id(0)
    size = dy_ref.shape[0]

    @pl.when(step == 0)
    def _():
        place_rows(scal, (a_ref, b_ref, c_ref, d_ref), h_ref)
        sum_ref[...] = jnp.zeros_like(sum_ref)

    rows = h_ref[pl.ds(pl.multiple_of(step * size, size), size), :]
    value = dot(rows, wi_ref[...]) + bi_ref[...]
    normal = 0.5 + 0.5 * lax.erf(value * (0.5**0.5))
    g_ref[...] = (value * normal).astype(BF)
    density = jnp.exp2(value * value * (-0.5 * LOG2E)) * 0.3989422804014327
    grad = dot(dy_ref[...], wo_ref[...], NT) * (normal + value * density)
    low = grad.astype(BF)
    du_ref[...] = low
    sum_ref[...] += jnp.sum(low.astype(F32), axis=0, keepdims=True)
    dh_ref[pl.ds(pl.multiple_of(step * size, size), size), :] = dot(low, wi_ref[...], NT)

    @pl.when(step == pl.num_programs(0) - 1)
    def _():
        window_shares(scal, dh_ref, send_ref, keep_ref)


def feed_forward(scal, parts, dy, w_in, b_in, w_out):
    length, width = dy.shape
    hidden = w_in.shape[1]
    half = parts[0].shape[0]
    size = FEED
    return call(
        feed_forward_kernel,
        (length // size,),
        [whole(half, width)] * 4
        + [
            pl.BlockSpec((size, width), lambda i, s: (i, 0)),
            whole(width, hidden),
            whole(1, hidden),
            whole(hidden, width),
        ],
        [
            whole(length, width),
            pl.BlockSpec((size, hidden), lambda i, s: (i, 0)),
            pl.BlockSpec((size, hidden), lambda i, s: (i, 0)),
            whole(2, half, width),
            whole(2, half, width),
            whole(1, hidden),
        ],
        [
            shaped((length, width), BF),
            shaped((length, hidden), BF),
            shaped((length, hidden), BF),
            shaped((2, half, width), BF),
            shaped((2, half, width), F32),
            shaped((1, hidden), F32),
        ],
        [pltpu.VMEM((length, width), F32)],
        (6 * length * width * hidden, 2 * length * hidden, 14 << 20),
        "feed_forward",
    )(scal, *parts, dy, w_in, b_in, w_out)


def memory_back_kernel(
    scal, dkv_ref, w_own, w_peer, send_ref, near_ref, far_ref, w_ref, part_ref
):
    core, chip = scal[0], scal[1]
    share, frames = near_ref.shape[1:]
    part = w_own.shape[1]

    @pl.when(pl.program_id(0) == 0)
    def _():
        for number in range(2):
            for place, ref in enumerate((w_own, w_peer)):
                first = (2 * number + place) * part
                w_ref[:, first : first + part] = flip(ref[1 + number])

    dkv = dkv_ref[0].reshape(w_ref.shape[1], dkv_ref.shape[3])
    part_ref[...] = dot(w_ref[...], dkv)
    for slot, keep_ref in enumerate((near_ref, far_ref)):
        which = chip if slot == 0 else 1 - chip
        near = pl.ds(pl.multiple_of((2 * which + core) * share, 64), share)
        far = pl.ds(pl.multiple_of((2 * which + 1 - core) * share, 64), share)
        keep_ref[0] = part_ref[near, :frames]
        send_ref[slot, 0] = part_ref[far, :frames].astype(BF)


def memory_back(scal, dkv, w_in, frames):
    _, _, feats, padded = dkv.shape
    _, part, width = w_in[0].shape
    share = width // 4
    out = pl.BlockSpec((2, 1, share, frames), lambda j, s: (0, j, 0, 0))
    return call(
        memory_back_kernel,
        (2,),
        [
            pl.BlockSpec((1, 2, feats, padded), lambda j, s: (j, 0, 0, 0)),
            whole(3, part, width),
            whole(3, part, width),
        ],
        [out] + [pl.BlockSpec((1, share, frames), lambda j, s: (j, 0, 0))] * 2,
        [shaped((2, 2, share, frames), BF)] + [shaped((2, share, frames), F32)] * 2,
        [pltpu.VMEM((width, 2 * feats), BF), pltpu.VMEM((width, padded), F32)],
        (8 * frames * width * feats, 0, 14 << 20),
        "memory_back",
    )(scal, dkv, *w_in)


def memory_place_kernel(scal, keep_ref, got_ref, far_ref, out_ref):
    source = pl.program_id(0)

    @pl.when(source < 2)
    def _():
        out_ref[...] = (keep_ref[...] + got_ref[0].astype(F32)).astype(BF)

    @pl.when(source >= 2)
    def _():
        out_ref[...] = far_ref[...]


def memory_place(scal, keep, got, far):
    _, share, frames = keep.shape
    kept = pl.BlockSpec((1, share, frames), lambda i, s: (jnp.minimum(i, 1), 0, 0))
    near = pl.BlockSpec((1, 1, share, frames), lambda i, s: (0, jnp.minimum(i, 1), 0, 0))
    return call(
        memory_place_kernel,
        (4,),
        [kept, near, pl.BlockSpec((1, share, frames), lambda i, s: (jnp.maximum(i - 2, 0), 0, 0))],
        pl.BlockSpec((1, share, frames), lambda i, s: (s[9 + i], 0, 0)),
        shaped((4, share, frames), BF),
        [],
        (0, 0, 0),
        "memory_place",
    )(scal, keep, got, far)


def cross_weights_kernel(
    scal, mem_ref, dkv_ref, h_ref, dq_ref, dx_ref, o_ref,
    weights_ref, one_ref, two_ref, sum_ref, full_ref, grads, tail_ref,
):
    doc = pl.program_id(0)
    frames = mem_ref.shape[1]
    body = frames // BLOCK * BLOCK
    feats, padded = dkv_ref.shape[2:]

    @pl.when(doc == 0)
    def _():
        sum_ref[...] = jnp.zeros_like(sum_ref)
        tail_ref[...] = jnp.zeros_like(tail_ref)
        put_weights(
            scal,
            full_ref,
            weights_ref,
            two_ref,
            1,
            jnp.concatenate([dot(dq_ref[...], h_ref[...], TN), dot(o_ref[...], dx_ref[...], TN)], axis=0),
        )

    tail_ref[: frames - body, :] = mem_ref[0, body:, :]
    rows = dkv_ref[0].reshape(2 * feats, padded)
    part = dot(rows[:, :body], mem_ref[0, :body, :]) + dot(rows[:, body:], tail_ref[...])
    sum_ref[...] += dot(jnp.ones((8, padded), BF), dkv_ref[0, 1], NT)[0:1]

    @pl.when(doc == 0)
    def _():
        grads[...] = part

    @pl.when(doc == 1)
    def _():
        put_weights(scal, full_ref, weights_ref, one_ref, 0, grads[...] + part)


def cross_weights(scal, memory, dkv, h, dq, dx, o, n_dp):
    _, frames, width = memory.shape
    _, _, feats, padded = dkv.shape
    rows = h.shape[0]
    specs, shapes, blocked = weights_specs(width, feats, n_dp)
    return call(
        cross_weights_kernel,
        (2,),
        [
            pl.BlockSpec((1, frames, width), lambda j, s: (s[9 + j], 0, 0)),
            pl.BlockSpec((1, 2, feats, padded), lambda j, s: (j, 0, 0, 0)),
            whole(rows, width),
            whole(rows, feats),
            whole(rows, width),
            whole(rows, feats),
        ],
        specs + [whole(1, feats)],
        shapes + [shaped((1, feats), F32)],
        [blocked, pltpu.VMEM((2 * feats, width), F32), pltpu.VMEM((BLOCK, width), BF)],
        (8 * frames * width * feats, 0, 14 << 20),
        "cross_weights",
        WEIGHTS_VMEM,
    )(scal, memory, dkv, h, dq, dx, o)


def per_device(
    inputs, memory, segments, documents, cotangent, norm_gain, norm_shift, attn_in, attn_bias,
    attn_out, cross_in, cross_bias, cross_out, fc_in, fc_in_bias, fc_out, out_bias, n_dp,
):
    length, width = inputs.shape
    docs, frames, _ = memory.shape
    padded = -(-frames // BLOCK) * BLOCK
    longest = length - 2 * (length // 5)
    rows = min(length, -(-longest // BLOCK) * BLOCK)
    half = rows // 2
    shift = length - rows
    slot = lax.axis_index("tensor")
    core, chip = slot % 2, slot // 2
    place_dp = lax.axis_index("dp")
    bits = n_dp.bit_length() - 1

    def swap(value, axis, bit):
        size = n_dp if axis == "dp" else 4
        return lax.ppermute(value, axis, [(i, i ^ bit) for i in range(size)])

    def to_core(value):
        return swap(value, "tensor", 1)

    def to_chip(value):
        return swap(value, "tensor", 2)

    numbers = jnp.arange(docs, dtype=jnp.int32)
    edges = jnp.sum((segments[None, :] < numbers[:, None]).astype(jnp.int32), axis=1)
    which = jnp.max(jnp.where(segments[None, :] == numbers[:, None], documents[None, :], 0), axis=1)
    which = which - place_dp * docs
    first_chip = chip == 0
    edge_one = jnp.where(first_chip, edges[1], edges[2] - shift)
    edge_two = jnp.where(first_chip, edges[2], edges[3] - shift)
    mine = jnp.where(first_chip, which, jnp.roll(which, 2))
    scal = jnp.concatenate(
        [
            jnp.stack(
                [
                    core,
                    chip,
                    edges[2],
                    edge_one,
                    edge_two,
                    jnp.where(first_chip, 0, edge_one),
                    jnp.where(first_chip, edge_one, edge_two),
                    jnp.where(first_chip, edge_one, edge_two),
                    jnp.where(first_chip, edge_two, rows),
                ]
            ),
            mine,
            jnp.stack([place_dp & 1, (place_dp >> 1) & 1]),
        ]
    ).astype(jnp.int32)

    def after(value, *earlier):
        return lax.optimization_barrier((value, earlier))[0]

    attn_in = jnp.swapaxes(attn_in, 1, 2)
    cross_in = jnp.swapaxes(cross_in, 1, 2)
    w_self = (attn_in, to_chip(attn_in))
    w_self_out = (attn_out, to_chip(attn_out))
    biases = jnp.concatenate([attn_bias, cross_bias], axis=0)
    biases = jnp.concatenate([biases, to_chip(biases)], axis=1)
    w_cross = (cross_in, to_chip(after(cross_in, w_self[1])))
    w_cross_out = (cross_out, to_chip(after(cross_out, w_self[1])))

    memory = with_layout_constraint(memory, Layout(major_to_minor=(0, 1, 2)))
    memory, peer_in = lax.optimization_barrier((memory, w_self[1]))
    w_self = (attn_in, peer_in)
    x_win = lax.dynamic_slice_in_dim(inputs, chip * shift, rows)
    dy_win = lax.dynamic_slice_in_dim(cotangent, chip * shift, rows)

    def row(matrix, index):
        return matrix[index : index + 1]

    h1, q1, k1, v1, o1, lse1 = self_forward(
        scal, x_win, row(norm_gain, 0), row(norm_shift, 0), w_self, biases[0:2]
    )
    send, keep = project_out(scal, o1, w_self_out)
    k2, v2 = memory_project(scal, memory, w_cross, biases[3:4], padded)
    x1, h2_own = add_norm(
        scal, x_win, keep, to_core(send), row(out_bias, 0), row(norm_gain, 1), row(norm_shift, 1), True
    )
    h2, q2, o2, lse2, send, keep = cross_forward(
        scal, h2_own, to_core(h2_own), w_cross, biases[2:3], k2, v2, w_cross_out, frames
    )
    x2, h3_own = add_norm(
        scal, x1, keep, to_core(send), row(out_bias, 1), row(norm_gain, 2), row(norm_shift, 2), False
    )

    def spread(value):
        far = to_chip(value)
        return (value, to_core(value), far, to_core(far))

    h3, g, du, send, keep, fc_sum = feed_forward(
        scal, spread(h3_own), cotangent, fc_in, fc_in_bias[None], fc_out
    )
    more = to_core(send)
    far = fold(scal, keep, more)
    got = to_chip(far)
    du, g_low = after((du, g), far)
    out_send, out_keep = second_product(scal, g_low, fc_out, half)
    out_near = to_core(out_send)
    fc_in_grad, fc_out_grad = dot(h3, du, TN), dot(cotangent, g_low, TN)
    far_out = fold(scal, out_keep, out_near)
    got_out = to_chip(after(far_out, got))

    def pick_bit(value, axis, bit):
        mine = (place_dp >> bit) & 1
        stay = lax.dynamic_index_in_dim(value, mine, axis, keepdims=False)
        return stay, lax.dynamic_index_in_dim(value, 1 - mine, axis, keepdims=False).astype(BF)

    others = list(range(2, bits))
    blocked = (2,) * bits + (width // n_dp,)

    def add(value, got):
        return value + got.astype(F32)

    def mlp_chain(matrices):
        value = jnp.stack(matrices).reshape(2, *blocked, -1)
        for number, bit in enumerate([0, 1] + others):
            axis = 1 + bits - 1 - bit if number == 0 else value.ndim - 3
            value, send = pick_bit(value, axis, bit)
            (got,) = yield [(send, "dp", 1 << bit)]
            value = add(value, got)
        return value

    def weights_chain(full, one_send, two_send):
        got = yield [(one_send, "dp", 1), (two_send, "dp", 2)]
        stay, one_send, two_send = shares_one(scal, full, *got)
        got = yield [(one_send, "dp", 2), (two_send, "dp", 1)]
        near, far = shares_two(scal, stay, *got)
        (got,) = yield [(far, "tensor", 2)]
        value = add(near, got)
        value = value.reshape(2, *(2,) * (bits - 2), *value.shape[2:])
        for bit in others:
            value, send = pick_bit(value, value.ndim - 3, bit)
            (got,) = yield [(send, "dp", 1 << bit)]
            value = add(value, got)
        return value

    def send_all(items):
        return [swap(*item) for item in items]

    mlp = mlp_chain([fc_in_grad, fc_out_grad])
    mlp_sent = next(mlp)
    mlp_got = send_all(mlp_sent)
    got = after(got, mlp_sent[0][0], far_out)
    dx2, dx2_low, sums_three = norm_back(
        scal, dy_win, keep, got, x2, row(norm_gain, 2), True, False, more
    )
    dx2_other = to_core(dx2_low)
    dx2_full, dq2, dkv2, q2_sum, send, keep = cross_backward(
        scal, dx2_low, dx2_other, w_cross_out, q2, lse2, k2, v2, w_cross, frames
    )
    mlp_got, got_out = after((mlp_got, got_out), q2_sum)
    mlp_sent = mlp.send(mlp_got)
    mlp_got = send_all(mlp_sent)
    dkv2 = after(dkv2, mlp_sent[0][0])
    *cross_grads, v2_sum = cross_weights(scal, memory, dkv2, h2, dq2, dx2_full, o2, n_dp)
    cross = weights_chain(*cross_grads)
    cross_sent = next(cross)
    cross_got = send_all(cross_sent)
    out_own = output_rows(scal, x2, out_keep, out_near, got_out, row(out_bias, 2))
    out_far = to_chip(out_own)
    got = to_core(send)
    mlp_sent = mlp.send(after(mlp_got, v2_sum, out_own))
    mlp_got = send_all(mlp_sent)

    dkv2 = after(dkv2, cross_sent[0][0], cross_sent[1][0], mlp_sent[0][0], out_own, got)
    mem_send, mem_near, mem_keep = memory_back(scal, dkv2, w_cross, frames)
    mem_got = to_core(mem_send)
    keep = after(keep, mem_send)
    dx1, dx1_low, sums_two = norm_back(
        scal, dx2, keep, got, x1, row(norm_gain, 1), False, False, cost=1 << 26
    )
    mem_far = fold(scal, mem_keep, mem_got)
    dx1_other = after(to_core(dx1_low), mem_far)
    *own_grads, self_sum, send, keep = self_backward(
        scal, dx1_low, dx1_other, w_self_out, h1, q1, k1, v1, o1, lse1, w_self, n_dp
    )
    mem_far = to_chip(mem_far)
    out_far = after(out_far, self_sum)
    own = weights_chain(*own_grads)
    own_sent = next(own)
    own_got = send_all(own_sent)
    input_own, input_low, sums_one = norm_back(
        scal, dx1, keep, to_core(send), x_win, row(norm_gain, 0), False, True
    )
    cross_sent = cross.send(after(cross_got, sums_one))
    mlp_got = after(mlp_got, sums_one)
    mem_far = after(mem_far, cross_sent[0][0])
    input_low = after(input_low, mem_far)
    out_own, out_far, mlp_got = after((out_own, out_far, mlp_got), sums_one)

    def input_chain(value):
        (far,) = yield [(value, "tensor", 2)]
        (got,) = yield [(jnp.stack([value, far]), "tensor", 1)]
        return value, far, got

    def output_chain(value, far):
        (got,) = yield [(jnp.stack([value, far]), "tensor", 1)]
        return value, far, got

    part = self_sum.shape[1] // 2

    def sums_chain():
        heads = jnp.concatenate([self_sum, q2_sum, v2_sum])
        sums = jnp.concatenate(
            [sums_one, sums_two, sums_three, jnp.pad(heads, ((0, 0), (0, width - 2 * part))), fc_sum]
        )
        number = jnp.arange(sums.shape[0])[:, None]
        near, far, far_other = yield [(sums, "tensor", which) for which in (1, 2, 3)]
        turned = jnp.where(number < 16, jnp.roll(far, -part, axis=1), 0.0)
        sums = jnp.where(number < 12, (sums + near) + (far + far_other), sums + turned)
        for bit in range(bits):
            (got,) = yield [(sums, "dp", 1 << bit)]
            sums = sums + got
        return sums

    chains = [
        (0, own, own_sent, own_got),
        (0, input_chain(input_low), None, None),
        (0, sums_chain(), None, None),
        (OUT_ROUND, output_chain(out_own, out_far), None, None),
        (0, cross, cross_sent, None),
        (0, mlp, mlp_sent, mlp_got),
    ]
    results = [None] * len(chains)
    pending, came = {}, {}
    number = 0
    while number < 3 or pending:
        for i, (start, chain, sent, got) in enumerate(chains):
            if start == number:
                if sent is not None and got is not None:
                    came[i] = got
                elif sent is not None:
                    pending[i] = sent
                else:
                    pending[i] = next(chain) if got is None else chain.send(got)
        values = lax.optimization_barrier([[item[0] for item in items] for items in pending.values()])
        for i, held in zip(pending, values):
            came[i] = [swap(value, *item[1:]) for value, item in zip(held, pending[i])]
        if number == 1:
            mem_far, *_ = lax.optimization_barrier((mem_far, values))
            memory_grad = memory_place(scal, mem_near, mem_got, mem_far)
            came, memory_grad = lax.optimization_barrier((came, memory_grad))
        else:
            came = lax.optimization_barrier(came)
        pending = {}
        for i, got in came.items():
            try:
                pending[i] = chains[i][1].send(got)
            except StopIteration as stop:
                results[i] = stop.value
        came = {}
        number += 1
    own_share, input_parts, sums, output_parts, cross_share, mlp_share = results
    input_grad = place(scal, *input_parts, length, F32)
    output = place(scal, *output_parts, length, BF)
    memory_grad = jnp.swapaxes(memory_grad, 1, 2)
    gain_sum, shift_sum, out_sum, self_total, cross_total, fc_total = finish_sums(scal, sums, part)
    return (
        output,
        input_grad,
        memory_grad,
        gain_sum,
        shift_sum,
        jnp.stack([own_share[0, :, :part], own_share[0, :, part:], own_share[1, :, :part]]),
        self_total,
        own_share[1, :, part:].T,
        jnp.stack([cross_share[1, :, :part], cross_share[0, :, :part], cross_share[0, :, part:]]),
        cross_total,
        cross_share[1, :, part:].T,
        mlp_share[0],
        fc_total[0],
        mlp_share[1].T,
        out_sum,
    )


def solution(mesh):
    n_dp = mesh.shape["dp"]

    def run(*args):
        return per_device(*args, n_dp)

    return jax.shard_map(
        run,
        mesh=mesh,
        in_specs=(
            P("dp", None),
            P("dp", None, None),
            P("dp"),
            P("dp"),
            P("dp", None),
            P(),
            P(),
            P(None, None, "tensor"),
            P(None, "tensor"),
            P("tensor", None),
            P(None, None, "tensor"),
            P(None, "tensor"),
            P("tensor", None),
            P(None, "tensor"),
            P("tensor"),
            P("tensor", None),
            P(),
        ),
        out_specs=(
            P("dp", None),
            P("dp", None),
            P("dp", None, "tensor"),
            P(),
            P(),
            P(None, "dp", "tensor"),
            P(None, "tensor"),
            P("tensor", "dp"),
            P(None, "dp", "tensor"),
            P(None, "tensor"),
            P("tensor", "dp"),
            P("dp", "tensor"),
            P("tensor"),
            P("tensor", "dp"),
            P(),
        ),
        check_vma=False,
    )
```

```python
import jax
import jax.numpy as jnp
from jax import lax
from jax.experimental import pallas as pl
from jax.experimental.layout import Layout, with_layout_constraint
from jax.experimental.pallas import tpu as pltpu
from jax.sharding import PartitionSpec as P

HEAD = 64
PAIR = 2 * HEAD
BLOCK = 128
ROWS = 160
EPSILON = 1e-05
LOG2E = 1.4426950408889634
SCALE = HEAD ** (-0.5)
NEG = -1e30
BIG = 1e30
BF = jnp.bfloat16
F32 = jnp.float32
VMEM = 20 << 20
SMALL_VMEM = 12 << 20
OUT_ROUND = 2
CROSS_VMEM = 34 << 20
BACK_VMEM = 54 << 20
SELF_VMEM = 20 << 20
WEIGHTS_VMEM = 20 << 20
PROJECT = 512
FEED = 256
COST = 4

NT = (((1,), (1,)), ((), ()))
NN = (((1,), (0,)), ((), ()))
TN = (((0,), (0,)), ((), ()))


def dot(left, right, dims=NN):
    return lax.dot_general(left, right, dims, preferred_element_type=F32)


def norm_parts(values):
    centred = values - jnp.mean(values, axis=-1, keepdims=True)
    inverse = lax.rsqrt(jnp.mean(centred * centred, axis=-1, keepdims=True) + EPSILON)
    return centred * inverse, inverse


def call(kernel, grid, in_specs, out_specs, out_shape, scratch, cost, name, vmem=VMEM):
    flops, exps, moved = cost
    return pl.pallas_call(
        kernel,
        grid_spec=pltpu.PrefetchScalarGridSpec(
            num_scalar_prefetch=1,
            grid=grid,
            in_specs=in_specs,
            out_specs=out_specs,
            scratch_shapes=scratch,
        ),
        out_shape=out_shape,
        compiler_params=pltpu.CompilerParams(
            dimension_semantics=("arbitrary",) * len(grid), vmem_limit_bytes=vmem
        ),
        cost_estimate=pl.CostEstimate(
            flops=COST * flops + 1, transcendentals=COST * exps, bytes_accessed=COST * moved + 1
        ),
        name=name,
    )


def whole(*shape):
    zeros = (0,) * len(shape)
    return pl.BlockSpec(shape, lambda *_: zeros)


def shaped(shape, dtype):
    return jax.ShapeDtypeStruct(shape, dtype)


def two_heads(rows):
    lane = lax.broadcasted_iota(jnp.int32, rows.shape, 1)
    zero = jnp.zeros_like(rows)
    return jnp.concatenate(
        [jnp.where(lane < HEAD, rows, zero), jnp.where(lane < HEAD, zero, rows)], axis=0
    )


def pick_heads(both):
    row = lax.broadcasted_iota(jnp.int32, (PAIR, BLOCK), 0)
    return jnp.where(row < HEAD, both[:, :BLOCK], both[:, BLOCK:]).T


def row_lanes(first):
    lane = lax.broadcasted_iota(jnp.int32, (1, 2 * BLOCK), 1)
    return first + jnp.where(lane < BLOCK, lane, lane - BLOCK)


def flip(matrix):
    return matrix.astype(F32).T.astype(BF)


def split_out(scal, total, send_ref, keep_ref, half):
    core = scal[0]
    here = pl.multiple_of(core * half, half)
    there = pl.multiple_of((1 - core) * half, half)
    keep_ref[...] = total[pl.ds(here, half), :]
    send_ref[...] = total[pl.ds(there, half), :].astype(BF)


def join_halves(scal, own_ref, other_ref, full_ref, half):
    core = scal[0]
    full_ref[pl.ds(pl.multiple_of(core * half, half), half), :] = own_ref[...]
    full_ref[pl.ds(pl.multiple_of((1 - core) * half, half), half), :] = other_ref[...]


def join_weights(own_ref, peer_ref, full_ref):
    part = own_ref.shape[-2]
    full_ref[..., :part, :] = own_ref[...]
    full_ref[..., part:, :] = peer_ref[...]


def join_stack(own_ref, peer_ref, full_ref):
    count, part, _ = own_ref.shape
    for number in range(count):
        first = 2 * part * number
        full_ref[first : first + part, :] = own_ref[number]
        full_ref[first + part : first + 2 * part, :] = peer_ref[number]


def put_weights(scal, full_ref, stay_ref, send_ref, group, rows):
    part = rows.shape[0] // 4
    count, size = full_ref.shape[:2]
    for side in range(2):
        one = rows[side * part : (side + 1) * part]
        two = rows[(2 + side) * part : (3 + side) * part]
        turned = jnp.concatenate([one, two], axis=0).T
        for block in range(count):
            full_ref[block] = turned[block * size : (block + 1) * size]
        for rest in range(count // 4):
            for other in range(2):
                stay = 2 * other + scal[13] if group == 0 else 2 * scal[14] + other
                send = 2 * other + 1 - scal[13] if group == 0 else 2 * (1 - scal[14]) + other
                stay_ref[group, side, rest, other] = full_ref[4 * rest + stay]
                send_ref[side, rest, other] = full_ref[4 * rest + send].astype(BF)


def weights_specs(width, feats, n_dp):
    size = width // n_dp
    half = (2, n_dp // 4, 2, size, feats)
    return (
        [whole(2, *half), whole(*half), whole(*half)],
        [shaped((2, *half), F32), shaped(half, BF), shaped(half, BF)],
        pltpu.VMEM((n_dp, size, feats), F32),
    )


def shares_one_kernel(scal, full_ref, one_ref, two_ref, stay_ref, one_send, two_send):
    low, high = scal[13], scal[14]
    for side in range(2):
        for rest in range(one_ref.shape[1]):

            def one_sum(bit):
                return full_ref[0, side, rest, bit] + one_ref[side, rest, bit].astype(F32)

            def two_sum(bit):
                return full_ref[1, side, rest, bit] + two_ref[side, rest, bit].astype(F32)

            stay_ref[0, side, rest] = one_sum(high)
            one_send[side, rest] = one_sum(1 - high).astype(BF)
            stay_ref[1, side, rest] = two_sum(low)
            two_send[side, rest] = two_sum(1 - low).astype(BF)


def shares_one(scal, full, one, two):
    _, _, count, _, size, feats = full.shape
    stay = (2, 2, count, size, feats)
    send = (2, count, size, feats)
    return call(
        shares_one_kernel,
        (1,),
        [whole(*full.shape), whole(*one.shape), whole(*one.shape)],
        [whole(*stay), whole(*send), whole(*send)],
        [shaped(stay, F32), shaped(send, BF), shaped(send, BF)],
        [],
        (0, 0, 0),
        "shares_one",
        SMALL_VMEM,
    )(scal, full, one, two)


def shares_two_kernel(scal, stay_ref, one_ref, two_ref, near_ref, far_ref):
    for group, got in enumerate((one_ref, two_ref)):
        near_ref[group] = stay_ref[group, 0] + got[0].astype(F32)
        far_ref[group] = (stay_ref[group, 1] + got[1].astype(F32)).astype(BF)


def shares_two(scal, stay, one, two):
    out = (2, *stay.shape[2:])
    return call(
        shares_two_kernel,
        (1,),
        [whole(*stay.shape), whole(*one.shape), whole(*one.shape)],
        [whole(*out), whole(*out)],
        [shaped(out, F32), shaped(out, BF)],
        [],
        (0, 0, 0),
        "shares_two",
        SMALL_VMEM,
    )(scal, stay, one, two)


def self_mask(scal, count, first):
    rows = row_lanes(first)
    edge_one, edge_two = scal[3], scal[4]
    begin = jnp.where(rows >= edge_two, edge_two, jnp.where(rows >= edge_one, edge_one, 0))
    keys = lax.broadcasted_iota(jnp.int32, (count, 2 * BLOCK), 0)
    return (keys >= begin) & (keys <= rows)


def self_forward_kernel(
    scal, x_ref, gain_ref, shift_ref, w_own, w_peer, b_ref,
    h_ref, q_ref, k_ref, v_ref, o_ref, lse_ref, vt, w_ref,
):
    rows = x_ref.shape[0]
    join_stack(w_own, w_peer, w_ref)
    normed, _ = norm_parts(x_ref[...].astype(F32))
    h_ref[...] = (normed * gain_ref[...] + shift_ref[...]).astype(BF)
    part = q_ref.shape[1]
    projected = dot(h_ref[...], w_ref[...], NT)
    q_ref[...] = (projected[:, :part] + b_ref[0:1, :]).astype(BF)
    k_ref[...] = projected[:, part : 2 * part].astype(BF)
    v_ref[...] = (projected[:, 2 * part :] + b_ref[1:2, :]).astype(BF)
    vt[...] = flip(v_ref[...])
    for block in range(rows // BLOCK):
        first = block * BLOCK
        count = first + BLOCK
        kept = self_mask(scal, count, first)
        for pair in range(part // PAIR):
            here = lanes(pair)
            queries = two_heads(q_ref[first : first + BLOCK, here])
            scores = jnp.where(kept, dot(k_ref[:count, here], queries, NT), NEG)
            largest = jnp.max(scores, axis=0, keepdims=True)
            chances = jnp.exp2((scores - largest) * (SCALE * LOG2E))
            totals = jnp.sum(chances, axis=0, keepdims=True)
            mixed = dot(vt[here, :count], chances.astype(BF)) * (1.0 / totals)
            o_ref[first : first + BLOCK, here] = pick_heads(mixed).astype(BF)
            lse_ref[pair, block] = largest * (SCALE * LOG2E) + jnp.log(totals) * LOG2E


def project_out_kernel(scal, o_ref, wo_own, wo_peer, send_ref, keep_ref, total):
    part = wo_own.shape[0]
    wo = jnp.concatenate([wo_own[...], wo_peer[...]], axis=0)
    total[...] = dot(o_ref[...], wo)
    split_out(scal, total, send_ref, keep_ref, o_ref.shape[0] // 2)


def project_out(scal, mixed, w_out):
    rows, feats = mixed.shape
    part, width = w_out[0].shape
    half = rows // 2
    return call(
        project_out_kernel,
        (1,),
        [whole(rows, feats), whole(part, width), whole(part, width)],
        [whole(half, width)] * 2,
        [shaped((half, width), BF), shaped((half, width), F32)],
        [pltpu.VMEM((rows, width), F32)],
        (0, 0, 0),
        "project_out",
        SMALL_VMEM,
    )(scal, mixed, *w_out)


def self_forward(scal, x_win, gain, shift, w_in, bias):
    rows, width = x_win.shape
    part = w_in[0].shape[1]
    feats = 2 * part
    pairs = feats // PAIR
    blocks = rows // BLOCK
    return call(
        self_forward_kernel,
        (1,),
        [
            whole(rows, width),
            whole(1, width),
            whole(1, width),
            whole(3, part, width),
            whole(3, part, width),
            whole(2, feats),
        ],
        [whole(rows, width)]
        + [whole(rows, feats)] * 4
        + [whole(pairs, blocks, 1, 2 * BLOCK)],
        [shaped((rows, width), BF)]
        + [shaped((rows, feats), BF)] * 4
        + [shaped((pairs, blocks, 1, 2 * BLOCK), F32)],
        [
            pltpu.VMEM((feats, rows), BF),
            pltpu.VMEM((3 * feats, width), BF),
        ],
        (8 * rows * width * feats + 4 * rows * rows * feats, rows * rows * 6, 12 << 20),
        "self_forward",
    )(scal, x_win, gain, shift, *w_in, bias)


def self_backward_kernel(
    scal, own_ref, other_ref, wo_own, wo_peer, h_ref, q_ref, k_ref, v_ref, o_ref, lse_ref,
    w_own, w_peer, weights_ref, one_ref, two_ref, sum_ref, send_ref, keep_ref,
    full_ref, dx_ref, grad_ref, total, kt, do, dks, dvs, w_ref, wo_ref,
):
    rows, feats = q_ref.shape
    join_halves(scal, own_ref, other_ref, dx_ref, rows // 2)
    join_stack(w_own, w_peer, w_ref)
    join_weights(wo_own, wo_peer, wo_ref)
    do[...] = dot(dx_ref[...], wo_ref[...], NT).astype(BF)
    kt[...] = flip(k_ref[...])
    for block in reversed(range(rows // BLOCK)):
        first = block * BLOCK
        count = first + BLOCK
        kept = self_mask(scal, count, first)
        for pair in range(feats // PAIR):
            here = lanes(pair)
            queries = two_heads(q_ref[first : first + BLOCK, here])
            grads = two_heads(do[first : first + BLOCK, here])
            scores = dot(k_ref[:count, here], queries, NT)
            chances = jnp.exp2(scores * (SCALE * LOG2E) - lse_ref[pair, block])
            chances = jnp.where(kept, chances, 0.0)
            prob_grad = dot(v_ref[:count, here], grads, NT)
            shared = jnp.sum(chances * prob_grad, axis=0, keepdims=True)
            score_grad = (chances * (prob_grad - shared)).astype(BF)
            dv = dot(chances.astype(BF), grads)
            dk = dot(score_grad, queries)
            if count == rows:
                dvs[:, here] = dv
                dks[:, here] = dk
            else:
                dvs[:count, here] += dv
                dks[:count, here] += dk
            turned = pick_heads(dot(kt[here, :count], score_grad)) * SCALE
            grad_ref[first : first + BLOCK, here] = turned.astype(BF)
    grad_ref[:, feats : 2 * feats] = (dks[...] * SCALE).astype(BF)
    grad_ref[:, 2 * feats :] = dvs[...].astype(BF)
    sum_ref[0:1, :] = jnp.sum(grad_ref[:, :feats].astype(F32), axis=0, keepdims=True)
    sum_ref[1:2, :] = jnp.sum(grad_ref[:, 2 * feats :].astype(F32), axis=0, keepdims=True)
    total[...] = dot(grad_ref[...], w_ref[...])
    split_out(scal, total, send_ref, keep_ref, rows // 2)
    hidden = h_ref[...]
    put_weights(scal, full_ref, weights_ref, one_ref, 0, dot(grad_ref[:, : 2 * feats], hidden, TN))
    put_weights(
        scal,
        full_ref,
        weights_ref,
        two_ref,
        1,
        jnp.concatenate(
            [dot(grad_ref[:, 2 * feats :], hidden, TN), dot(o_ref[...], dx_ref[...], TN)], axis=0
        ),
    )


def self_backward(scal, own, other, w_out, h, q, k, v, o, lse, w_in, n_dp):
    rows, feats = q.shape
    width = own.shape[1]
    part = feats // 2
    pairs = feats // PAIR
    blocks = rows // BLOCK
    half = rows // 2
    specs, shapes, blocked = weights_specs(width, feats, n_dp)
    return call(
        self_backward_kernel,
        (1,),
        [whole(half, width)] * 2
        + [whole(part, width)] * 2
        + [whole(rows, width)]
        + [whole(rows, feats)] * 4
        + [whole(pairs, blocks, 1, 2 * BLOCK)]
        + [whole(3, part, width)] * 2,
        specs
        + [
            whole(2, feats),
            whole(half, width),
            whole(half, width),
        ],
        shapes
        + [
            shaped((2, feats), F32),
            shaped((half, width), BF),
            shaped((half, width), F32),
        ],
        [
            blocked,
            pltpu.VMEM((rows, width), BF),
            pltpu.VMEM((rows, 3 * feats), BF),
            pltpu.VMEM((rows, width), F32),
            pltpu.VMEM((feats, rows), BF),
            pltpu.VMEM((rows, feats), BF),
            pltpu.VMEM((rows, feats), F32),
            pltpu.VMEM((rows, feats), F32),
            pltpu.VMEM((3 * feats, width), BF),
            pltpu.VMEM((feats, width), BF),
        ],
        (8 * rows * width * feats + 10 * rows * rows * feats, rows * rows * 6, 14 << 20),
        "self_backward",
        SELF_VMEM,
    )(scal, own, other, *w_out, h, q, k, v, o, lse, *w_in)


def add_norm_kernel(scal, base_ref, keep_ref, got_ref, bias_ref, gain_ref, shift_ref, x_ref, h_ref):
    value = base_ref[...].astype(F32) + (keep_ref[...] + got_ref[...].astype(F32)) + bias_ref[...]
    x_ref[...] = value
    normed, _ = norm_parts(value)
    h_ref[...] = (normed * gain_ref[...] + shift_ref[...]).astype(BF)


def add_norm(scal, base, keep, got, bias, gain, shift, by_core):
    half, width = keep.shape
    steps = half // ROWS
    block = pl.BlockSpec((ROWS, width), lambda i, s: (i, 0))
    base_spec = pl.BlockSpec((ROWS, width), lambda i, s: (s[0] * steps + i, 0)) if by_core else block
    return call(
        add_norm_kernel,
        (steps,),
        [base_spec, block, block] + [whole(1, width)] * 3,
        [block] * 2,
        [shaped((half, width), F32), shaped((half, width), BF)],
        [],
        (0, 0, 0),
        "add_norm",
        SMALL_VMEM,
    )(scal, base, keep, got, bias, gain, shift)


def norm_back_more_kernel(
    scal, base_ref, keep_ref, got_ref, x_ref, gain_ref, more_ref, dx_ref, low_ref, sum_ref
):
    norm_back_body(
        scal, base_ref, keep_ref[0] + more_ref[0].astype(F32), got_ref, x_ref, gain_ref,
        dx_ref, low_ref, sum_ref,
    )


def norm_back_kernel(scal, base_ref, keep_ref, got_ref, x_ref, gain_ref, dx_ref, low_ref, sum_ref):
    norm_back_body(
        scal, base_ref, keep_ref[...], got_ref, x_ref, gain_ref, dx_ref, low_ref, sum_ref
    )


def norm_back_body(scal, base_ref, keep, got_ref, x_ref, gain_ref, dx_ref, low_ref, sum_ref):
    step, steps = pl.program_id(0), pl.num_programs(0)
    base = base_ref[...].astype(F32)
    grad = keep + got_ref[...].astype(F32)
    row = (scal[0] * steps + step) * ROWS + lax.broadcasted_iota(jnp.int32, (ROWS, 1), 0)
    valid = (row >= scal[5]) & (row < scal[8])
    grad = jnp.where(valid, grad, 0.0)
    base = jnp.where(valid, base, 0.0)
    normed, inverse = norm_parts(x_ref[...].astype(F32))
    scaled = grad * gain_ref[...]
    total = base + inverse * (
        scaled
        - jnp.mean(scaled, axis=-1, keepdims=True)
        - normed * jnp.mean(scaled * normed, axis=-1, keepdims=True)
    )
    dx_ref[...] = total
    low_ref[...] = total.astype(BF)

    @pl.when(step == 0)
    def _():
        sum_ref[...] = jnp.zeros_like(sum_ref)

    sum_ref[0:1, :] += jnp.sum(grad * normed, axis=0, keepdims=True)
    sum_ref[1:2, :] += jnp.sum(grad, axis=0, keepdims=True)
    sum_ref[2:3, :] += jnp.sum(total, axis=0, keepdims=True)
    sum_ref[3:4, :] += jnp.sum(base, axis=0, keepdims=True)


def norm_back(scal, base, keep, got, x, gain, base_by_core, x_by_core, more=None, cost=0):
    half, width = got.shape

    steps = half // ROWS
    block = pl.BlockSpec((ROWS, width), lambda i, s: (i, 0))
    cored = pl.BlockSpec((ROWS, width), lambda i, s: (s[0] * steps + i, 0))

    stacked = pl.BlockSpec((1, ROWS, width), lambda i, s: (0, i, 0))

    def spec(by_core):
        return cored if by_core else block

    return call(
        norm_back_kernel if more is None else norm_back_more_kernel,
        (steps,),
        [
            spec(base_by_core),
            block if more is None else stacked,
            block,
            spec(x_by_core),
            whole(1, width),
        ]
        + [stacked] * (more is not None),
        [block, block, whole(4, width)],
        [shaped((half, width), F32), shaped((half, width), BF), shaped((4, width), F32)],
        [],
        (0, 0, cost),
        "norm_back",
        SMALL_VMEM,
    )(scal, base, keep, got, x, gain, *([] if more is None else [more]))


def pieces(total, size):
    return [(first, min(size, total - first)) for first in range(0, total, size)]


def memory_project_kernel(scal, mem_ref, w_own, w_peer, b_ref, k_ref, v_ref, w_ref):
    feats = k_ref.shape[2]

    @pl.when(pl.program_id(0) == 0)
    def _():
        for number in range(2):
            rows = slice(number * feats, (number + 1) * feats)
            join_weights(w_own.at[1 + number], w_peer.at[1 + number], w_ref.at[rows])

    frames = mem_ref.shape[1]
    padded = k_ref.shape[1]
    tail = padded - BLOCK
    k_ref[0, tail:padded, :] = jnp.zeros((BLOCK, k_ref.shape[2]), BF)
    v_ref[0, tail:padded, :] = jnp.zeros((BLOCK, k_ref.shape[2]), BF)
    for first, size in pieces(frames, PROJECT):
        both = dot(mem_ref[0, first : first + size, :], w_ref[...], NT)
        k_ref[0, first : first + size, :] = both[:, :feats].astype(BF)
        v_ref[0, first : first + size, :] = (both[:, feats:] + b_ref[...]).astype(BF)


def memory_project(scal, memory, w_kv, bias, padded):
    _, frames, width = memory.shape
    part = w_kv[0].shape[1]
    feats = 2 * part
    out = pl.BlockSpec((1, padded, feats), lambda j, s: (j, 0, 0))
    return call(
        memory_project_kernel,
        (2,),
        [
            pl.BlockSpec((1, frames, width), lambda j, s: (s[9 + j], 0, 0)),
            whole(3, part, width),
            whole(3, part, width),
            whole(1, feats),
        ],
        [out, out],
        [shaped((2, padded, feats), BF)] * 2,
        [pltpu.VMEM((2 * feats, width), BF)],
        (8 * frames * width * feats, 0, 12 << 20),
        "memory_project",
    )(scal, memory, *w_kv, bias)


def block_span(scal, doc):
    low, high = scal[5 + 2 * doc], scal[6 + 2 * doc]
    return low, high, low // BLOCK, (high + BLOCK - 1) // BLOCK


def lanes(pair):
    return slice(pair * PAIR, (pair + 1) * PAIR)


def cross_forward_kernel(
    scal, own_ref, other_ref, wq_own, wq_peer, bq_ref, k_ref, v_ref, wo_own, wo_peer,
    h_ref, q_ref, o_ref, lse_ref, send_ref, keep_ref, total, vt, s_ref, wq_ref, wo_ref, *, frames,
):
    doc = pl.program_id(0)
    rows, feats = q_ref.shape
    padded = k_ref.shape[1]

    @pl.when(doc == 0)
    def _():
        join_halves(scal, own_ref, other_ref, h_ref, rows // 2)
        join_weights(wq_own.at[0], wq_peer.at[0], wq_ref)
        join_weights(wo_own, wo_peer, wo_ref)
        q_ref[...] = (dot(h_ref[...], wq_ref[...], NT) + bq_ref[...]).astype(BF)
        o_ref[...] = jnp.zeros_like(o_ref)
        lse_ref[...] = jnp.zeros_like(lse_ref)

    vt[...] = flip(v_ref[0])
    low, high, start, stop = block_span(scal, doc)

    def one_block(block, carry):
        first = pl.multiple_of(block * BLOCK, BLOCK)
        number = row_lanes(first)
        inside = (number >= low) & (number < high)
        for pair in range(feats // PAIR):
            here = lanes(pair)
            queries = two_heads(q_ref[pl.ds(first, BLOCK), here])
            s_ref[pair] = dot(k_ref[0, :, here], queries, NT)
            s_ref[pair, frames:padded, :] = jnp.full((padded - frames, 2 * BLOCK), NEG, F32)
            scores = s_ref[pair]
            largest = jnp.max(scores, axis=0, keepdims=True)
            chances = jnp.exp2((scores - largest) * (SCALE * LOG2E))
            totals = jnp.sum(chances, axis=0, keepdims=True)
            mixed = dot(vt[here, :], chances.astype(BF)) * jnp.where(inside, 1.0 / totals, 0.0)
            o_ref[pl.ds(first, BLOCK), here] += pick_heads(mixed).astype(BF)
            log_total = largest * (SCALE * LOG2E) + jnp.log(totals) * LOG2E
            lse_ref[pair, block] = jnp.where(inside, log_total, lse_ref[pair, block])
        return carry

    lax.fori_loop(start, stop, one_block, 0)

    @pl.when(doc == 1)
    def _():
        total[...] = dot(o_ref[...], wo_ref[...])
        split_out(scal, total, send_ref, keep_ref, rows // 2)


def cross_forward(scal, own, other, wq, bq, k, v, w_out, frames):
    half, width = own.shape
    rows = 2 * half
    _, padded, feats = k.shape
    pairs = feats // PAIR
    blocks = rows // BLOCK
    keyed = pl.BlockSpec((1, padded, feats), lambda j, s: (j, 0, 0))

    def kernel(*refs):
        cross_forward_kernel(*refs, frames=frames)

    return call(
        kernel,
        (2,),
        [
            whole(half, width),
            whole(half, width),
            whole(1, feats // 2, width),
            whole(1, feats // 2, width),
            whole(1, feats),
            keyed,
            keyed,
            whole(feats // 2, width),
            whole(feats // 2, width),
        ],
        [
            whole(rows, width),
            whole(rows, feats),
            whole(rows, feats),
            whole(pairs, blocks, 1, 2 * BLOCK),
            whole(half, width),
            whole(half, width),
        ],
        [
            shaped((rows, width), BF),
            shaped((rows, feats), BF),
            shaped((rows, feats), BF),
            shaped((pairs, blocks, 1, 2 * BLOCK), F32),
            shaped((half, width), BF),
            shaped((half, width), F32),
        ],
        [
            pltpu.VMEM((rows, width), F32),
            pltpu.VMEM((feats, padded), BF),
            pltpu.VMEM((pairs, padded, 2 * BLOCK), F32),
            pltpu.VMEM((feats, width), BF),
            pltpu.VMEM((feats, width), BF),
        ],
        (4 * rows * width * feats + 4 * rows * padded * feats, rows * padded * 6, 14 << 20),
        "cross_forward",
        CROSS_VMEM,
    )(scal, own, other, *wq, bq, k, v, *w_out)


def cross_backward_kernel(
    scal, own_ref, other_ref, wo_own, wo_peer, q_ref, lse_ref, k_ref, v_ref, wq_own, wq_peer,
    dx_ref, dq_ref, dkv_ref, sum_ref, send_ref, keep_ref,
    total, kt, do, dks, dvs, wq_ref, wo_ref, *, frames,
):
    doc = pl.program_id(0)
    rows, feats = q_ref.shape
    padded = k_ref.shape[1]

    @pl.when(doc == 0)
    def _():
        join_halves(scal, own_ref, other_ref, dx_ref, rows // 2)
        join_weights(wq_own.at[0], wq_peer.at[0], wq_ref)
        join_weights(wo_own, wo_peer, wo_ref)
        do[...] = dot(dx_ref[...], wo_ref[...], NT).astype(BF)
        dq_ref[...] = jnp.zeros_like(dq_ref)

    kt[...] = flip(k_ref[0])
    dks[...] = jnp.zeros_like(dks)
    dvs[...] = jnp.zeros_like(dvs)
    low, high, start, stop = block_span(scal, doc)

    def one_block(block, carry):
        first = pl.multiple_of(block * BLOCK, BLOCK)
        number = row_lanes(first)
        inside = (number >= low) & (number < high)
        for pair in range(feats // PAIR):
            here = lanes(pair)
            queries = two_heads(q_ref[pl.ds(first, BLOCK), here])
            grads = two_heads(do[pl.ds(first, BLOCK), here])
            log_total = jnp.where(inside, lse_ref[pair, block], BIG)
            chances = jnp.exp2(dot(k_ref[0, :, here], queries, NT) * (SCALE * LOG2E) - log_total)
            prob_grad = dot(v_ref[0, :, here], grads, NT)
            shared = jnp.sum(chances * prob_grad, axis=0, keepdims=True)
            score_grad = (chances * (prob_grad - shared)).astype(BF)
            dvs[:, here] += dot(chances.astype(BF), grads)
            dks[:, here] += dot(score_grad, queries)
            turned = pick_heads(dot(kt[here, :], score_grad)) * SCALE
            dq_ref[pl.ds(first, BLOCK), here] += turned.astype(BF)
        return carry

    lax.fori_loop(start, stop, one_block, 0)
    tail = jnp.zeros((padded - frames, feats), F32)
    dks[frames:, :] = tail
    dvs[frames:, :] = tail
    dkv_ref[0, 0] = (dks[...] * SCALE).T.astype(BF)
    dkv_ref[0, 1] = dvs[...].T.astype(BF)

    @pl.when(doc == 1)
    def _():
        sum_ref[...] = jnp.sum(dq_ref[...].astype(F32), axis=0, keepdims=True)
        total[...] = dot(dq_ref[...], wq_ref[...])
        split_out(scal, total, send_ref, keep_ref, rows // 2)


def cross_backward(scal, own, other, w_out, q, lse, k, v, wq, frames):
    half, width = own.shape
    rows = 2 * half
    _, padded, feats = k.shape
    pairs = feats // PAIR
    blocks = rows // BLOCK
    keyed = pl.BlockSpec((1, padded, feats), lambda j, s: (j, 0, 0))

    def kernel(*refs):
        cross_backward_kernel(*refs, frames=frames)

    return call(
        kernel,
        (2,),
        [
            whole(half, width),
            whole(half, width),
            whole(feats // 2, width),
            whole(feats // 2, width),
            whole(rows, feats),
            whole(pairs, blocks, 1, 2 * BLOCK),
            keyed,
            keyed,
            whole(1, feats // 2, width),
            whole(1, feats // 2, width),
        ],
        [
            whole(rows, width),
            whole(rows, feats),
            pl.BlockSpec((1, 2, feats, padded), lambda j, s: (j, 0, 0, 0)),
            whole(1, feats),
            whole(half, width),
            whole(half, width),
        ],
        [
            shaped((rows, width), BF),
            shaped((rows, feats), BF),
            shaped((2, 2, feats, padded), BF),
            shaped((1, feats), F32),
            shaped((half, width), BF),
            shaped((half, width), F32),
        ],
        [
            pltpu.VMEM((rows, width), F32),
            pltpu.VMEM((feats, padded), BF),
            pltpu.VMEM((rows, feats), BF),
            pltpu.VMEM((padded, feats), F32),
            pltpu.VMEM((padded, feats), F32),
            pltpu.VMEM((feats, width), BF),
            pltpu.VMEM((feats, width), BF),
        ],
        (4 * rows * width * feats + 10 * rows * padded * feats, rows * padded * 6, 18 << 20),
        "cross_backward",
        BACK_VMEM,
    )(scal, own, other, *w_out, q, lse, k, v, *wq)


def finish_sums_kernel(scal, sum_ref, gain_ref, shift_ref, bias_ref, self_ref, cross_ref, fc_ref):
    part = self_ref.shape[1]
    for norm in range(3):
        gain_ref[norm : norm + 1, :] = sum_ref[4 * norm : 4 * norm + 1, :]
        shift_ref[norm : norm + 1, :] = sum_ref[4 * norm + 1 : 4 * norm + 2, :]
    for number, line in enumerate((6, 10, 11)):
        bias_ref[number : number + 1, :] = sum_ref[line : line + 1, :]
    self_ref[...] = sum_ref[12:14, :part]
    cross_ref[...] = sum_ref[14:16, :part]
    fc_ref[...] = sum_ref[16:17, :]


def finish_sums(scal, sums, part):
    rows, width = sums.shape
    shapes = [(3, width)] * 3 + [(2, part)] * 2 + [(1, width)]
    return call(
        finish_sums_kernel,
        (1,),
        [whole(rows, width)],
        [whole(*shape) for shape in shapes],
        [shaped(shape, F32) for shape in shapes],
        [],
        (0, 0, 0),
        "finish_sums",
        SMALL_VMEM,
    )(scal, sums)


def place_rows(scal, refs, full_ref):
    core, chip, edge = scal[0], scal[1], scal[2]
    half = refs[0].shape[-2]
    shift = full_ref.shape[0] - 2 * half
    for number, ref in enumerate(refs):
        which_chip = chip if number < 2 else 1 - chip
        which_core = core if number % 2 == 0 else 1 - core
        first = pl.multiple_of(which_chip * shift + which_core * half, 64)
        row = first + lax.broadcasted_iota(jnp.int32, (half, 1), 0)
        valid = (row < edge) == (which_chip == 0)
        part = (ref[...] if ref.ndim == 2 else ref[0]).astype(full_ref.dtype)
        full_ref[pl.ds(first, half), :] = jnp.where(valid, part, full_ref[pl.ds(first, half), :])


def place_kernel(scal, a_ref, b_ref, c_ref, d_ref, out_ref):
    place_rows(scal, (a_ref, b_ref, c_ref, d_ref), out_ref)


def place(scal, own, far, got, length, dtype):
    half, width = own.shape
    near_half = pl.BlockSpec((1, half, width), lambda *_: (0, 0, 0))
    far_half = pl.BlockSpec((1, half, width), lambda *_: (1, 0, 0))
    return call(
        place_kernel,
        (1,),
        [whole(half, width), near_half, whole(half, width), far_half],
        whole(length, width),
        shaped((length, width), dtype),
        [],
        (0, 0, 0),
        "place_rows",
        SMALL_VMEM,
    )(scal, own, got, far, got)


def window_shares(scal, full_ref, send_ref, keep_ref):
    core, chip = scal[0], scal[1]
    half = keep_ref.shape[1]
    shift = full_ref.shape[0] - 2 * half
    for slot in range(2):
        first = (chip if slot == 0 else 1 - chip) * shift
        near = pl.multiple_of(first + core * half, 64)
        far = pl.multiple_of(first + (1 - core) * half, 64)
        keep_ref[slot] = full_ref[pl.ds(near, half), :]
        send_ref[slot] = full_ref[pl.ds(far, half), :].astype(BF)


def second_product_kernel(scal, g_ref, w_ref, send_ref, keep_ref, full_ref):
    full_ref[...] = dot(g_ref[...], w_ref[...])
    window_shares(scal, full_ref, send_ref, keep_ref)


def second_product(scal, g, w_out, half):
    length, hidden = g.shape
    width = w_out.shape[1]
    return call(
        second_product_kernel,
        (1,),
        [whole(length, hidden), whole(hidden, width)],
        [whole(2, half, width)] * 2,
        [shaped((2, half, width), BF), shaped((2, half, width), F32)],
        [pltpu.VMEM((length, width), F32)],
        (0, 0, 0),
        "second_product",
    )(scal, g, w_out)


def fold_kernel(scal, keep_ref, got_ref, out_ref):
    keep = keep_ref[0] if keep_ref.ndim > out_ref.ndim else keep_ref[...]
    out_ref[...] = (keep + got_ref[0].astype(F32)).astype(BF)


def fold(scal, keep, got):
    shape = got.shape[1:]
    second = pl.BlockSpec((1, *shape), lambda i, s: (1, *(0,) * len(shape)))
    return call(
        fold_kernel,
        (1,),
        [second if keep.ndim == got.ndim else whole(*shape), second],
        whole(*shape),
        shaped(shape, BF),
        [],
        (0, 0, 0),
        "fold",
        SMALL_VMEM,
    )(scal, keep, got)


def output_rows_kernel(scal, x_ref, keep_ref, near_ref, far_ref, bias_ref, out_ref):
    value = keep_ref[0] + near_ref[0].astype(F32) + far_ref[...].astype(F32)
    out_ref[...] = (x_ref[...] + value + bias_ref[...]).astype(BF)


def output_rows(scal, x, keep, near, far, bias):
    half, width = x.shape
    first = pl.BlockSpec((1, half, width), lambda i, s: (0, 0, 0))
    return call(
        output_rows_kernel,
        (1,),
        [whole(half, width), first, first, whole(half, width), whole(1, width)],
        whole(half, width),
        shaped((half, width), BF),
        [],
        (0, 0, 0),
        "output_rows",
        SMALL_VMEM,
    )(scal, x, keep, near, far, bias)


def feed_forward_kernel(
    scal, a_ref, b_ref, c_ref, d_ref, dy_ref, wi_ref, bi_ref, wo_ref,
    h_ref, g_ref, du_ref, send_ref, keep_ref, sum_ref, dh_ref,
):
    step = pl.program_id(0)
    size = dy_ref.shape[0]

    @pl.when(step == 0)
    def _():
        place_rows(scal, (a_ref, b_ref, c_ref, d_ref), h_ref)
        sum_ref[...] = jnp.zeros_like(sum_ref)

    rows = h_ref[pl.ds(pl.multiple_of(step * size, size), size), :]
    value = dot(rows, wi_ref[...]) + bi_ref[...]
    normal = 0.5 + 0.5 * lax.erf(value * (0.5**0.5))
    g_ref[...] = (value * normal).astype(BF)
    density = jnp.exp2(value * value * (-0.5 * LOG2E)) * 0.3989422804014327
    grad = dot(dy_ref[...], wo_ref[...], NT) * (normal + value * density)
    low = grad.astype(BF)
    du_ref[...] = low
    sum_ref[...] += jnp.sum(low.astype(F32), axis=0, keepdims=True)
    dh_ref[pl.ds(pl.multiple_of(step * size, size), size), :] = dot(low, wi_ref[...], NT)

    @pl.when(step == pl.num_programs(0) - 1)
    def _():
        window_shares(scal, dh_ref, send_ref, keep_ref)


def feed_forward(scal, parts, dy, w_in, b_in, w_out):
    length, width = dy.shape
    hidden = w_in.shape[1]
    half = parts[0].shape[0]
    size = FEED
    return call(
        feed_forward_kernel,
        (length // size,),
        [whole(half, width)] * 4
        + [
            pl.BlockSpec((size, width), lambda i, s: (i, 0)),
            whole(width, hidden),
            whole(1, hidden),
            whole(hidden, width),
        ],
        [
            whole(length, width),
            pl.BlockSpec((size, hidden), lambda i, s: (i, 0)),
            pl.BlockSpec((size, hidden), lambda i, s: (i, 0)),
            whole(2, half, width),
            whole(2, half, width),
            whole(1, hidden),
        ],
        [
            shaped((length, width), BF),
            shaped((length, hidden), BF),
            shaped((length, hidden), BF),
            shaped((2, half, width), BF),
            shaped((2, half, width), F32),
            shaped((1, hidden), F32),
        ],
        [pltpu.VMEM((length, width), F32)],
        (6 * length * width * hidden, 2 * length * hidden, 14 << 20),
        "feed_forward",
    )(scal, *parts, dy, w_in, b_in, w_out)


def memory_back_kernel(
    scal, dkv_ref, w_own, w_peer, send_ref, near_ref, far_ref, w_ref, part_ref
):
    core, chip = scal[0], scal[1]
    share, frames = near_ref.shape[1:]
    part = w_own.shape[1]

    @pl.when(pl.program_id(0) == 0)
    def _():
        for number in range(2):
            for place, ref in enumerate((w_own, w_peer)):
                first = (2 * number + place) * part
                w_ref[:, first : first + part] = flip(ref[1 + number])

    dkv = dkv_ref[0].reshape(w_ref.shape[1], dkv_ref.shape[3])
    part_ref[...] = dot(w_ref[...], dkv)
    for slot, keep_ref in enumerate((near_ref, far_ref)):
        which = chip if slot == 0 else 1 - chip
        near = pl.ds(pl.multiple_of((2 * which + core) * share, 64), share)
        far = pl.ds(pl.multiple_of((2 * which + 1 - core) * share, 64), share)
        keep_ref[0] = part_ref[near, :frames]
        send_ref[slot, 0] = part_ref[far, :frames].astype(BF)


def memory_back(scal, dkv, w_in, frames):
    _, _, feats, padded = dkv.shape
    _, part, width = w_in[0].shape
    share = width // 4
    out = pl.BlockSpec((2, 1, share, frames), lambda j, s: (0, j, 0, 0))
    return call(
        memory_back_kernel,
        (2,),
        [
            pl.BlockSpec((1, 2, feats, padded), lambda j, s: (j, 0, 0, 0)),
            whole(3, part, width),
            whole(3, part, width),
        ],
        [out] + [pl.BlockSpec((1, share, frames), lambda j, s: (j, 0, 0))] * 2,
        [shaped((2, 2, share, frames), BF)] + [shaped((2, share, frames), F32)] * 2,
        [pltpu.VMEM((width, 2 * feats), BF), pltpu.VMEM((width, padded), F32)],
        (8 * frames * width * feats, 0, 14 << 20),
        "memory_back",
    )(scal, dkv, *w_in)


def memory_place_kernel(scal, keep_ref, got_ref, far_ref, out_ref):
    source = pl.program_id(0)

    @pl.when(source < 2)
    def _():
        out_ref[...] = (keep_ref[...] + got_ref[0].astype(F32)).astype(BF)

    @pl.when(source >= 2)
    def _():
        out_ref[...] = far_ref[...]


def memory_place(scal, keep, got, far):
    _, share, frames = keep.shape
    kept = pl.BlockSpec((1, share, frames), lambda i, s: (jnp.minimum(i, 1), 0, 0))
    near = pl.BlockSpec((1, 1, share, frames), lambda i, s: (0, jnp.minimum(i, 1), 0, 0))
    return call(
        memory_place_kernel,
        (4,),
        [kept, near, pl.BlockSpec((1, share, frames), lambda i, s: (jnp.maximum(i - 2, 0), 0, 0))],
        pl.BlockSpec((1, share, frames), lambda i, s: (s[9 + i], 0, 0)),
        shaped((4, share, frames), BF),
        [],
        (0, 0, 0),
        "memory_place",
    )(scal, keep, got, far)


def cross_weights_kernel(
    scal, mem_ref, dkv_ref, h_ref, dq_ref, dx_ref, o_ref,
    weights_ref, one_ref, two_ref, sum_ref, full_ref, grads, tail_ref,
):
    doc = pl.program_id(0)
    frames = mem_ref.shape[1]
    body = frames // BLOCK * BLOCK
    feats, padded = dkv_ref.shape[2:]

    @pl.when(doc == 0)
    def _():
        sum_ref[...] = jnp.zeros_like(sum_ref)
        tail_ref[...] = jnp.zeros_like(tail_ref)
        put_weights(
            scal,
            full_ref,
            weights_ref,
            two_ref,
            1,
            jnp.concatenate([dot(dq_ref[...], h_ref[...], TN), dot(o_ref[...], dx_ref[...], TN)], axis=0),
        )

    tail_ref[: frames - body, :] = mem_ref[0, body:, :]
    rows = dkv_ref[0].reshape(2 * feats, padded)
    part = dot(rows[:, :body], mem_ref[0, :body, :]) + dot(rows[:, body:], tail_ref[...])
    sum_ref[...] += dot(jnp.ones((8, padded), BF), dkv_ref[0, 1], NT)[0:1]

    @pl.when(doc == 0)
    def _():
        grads[...] = part

    @pl.when(doc == 1)
    def _():
        put_weights(scal, full_ref, weights_ref, one_ref, 0, grads[...] + part)


def cross_weights(scal, memory, dkv, h, dq, dx, o, n_dp):
    _, frames, width = memory.shape
    _, _, feats, padded = dkv.shape
    rows = h.shape[0]
    specs, shapes, blocked = weights_specs(width, feats, n_dp)
    return call(
        cross_weights_kernel,
        (2,),
        [
            pl.BlockSpec((1, frames, width), lambda j, s: (s[9 + j], 0, 0)),
            pl.BlockSpec((1, 2, feats, padded), lambda j, s: (j, 0, 0, 0)),
            whole(rows, width),
            whole(rows, feats),
            whole(rows, width),
            whole(rows, feats),
        ],
        specs + [whole(1, feats)],
        shapes + [shaped((1, feats), F32)],
        [blocked, pltpu.VMEM((2 * feats, width), F32), pltpu.VMEM((BLOCK, width), BF)],
        (8 * frames * width * feats, 0, 14 << 20),
        "cross_weights",
        WEIGHTS_VMEM,
    )(scal, memory, dkv, h, dq, dx, o)


def per_device(
    inputs, memory, segments, documents, cotangent, norm_gain, norm_shift, attn_in, attn_bias,
    attn_out, cross_in, cross_bias, cross_out, fc_in, fc_in_bias, fc_out, out_bias, n_dp,
):
    length, width = inputs.shape
    docs, frames, _ = memory.shape
    padded = -(-frames // BLOCK) * BLOCK
    longest = length - 2 * (length // 5)
    rows = min(length, -(-longest // BLOCK) * BLOCK)
    half = rows // 2
    shift = length - rows
    slot = lax.axis_index("tensor")
    core, chip = slot % 2, slot // 2
    place_dp = lax.axis_index("dp")
    bits = n_dp.bit_length() - 1

    def swap(value, axis, bit):
        size = n_dp if axis == "dp" else 4
        return lax.ppermute(value, axis, [(i, i ^ bit) for i in range(size)])

    def to_core(value):
        return swap(value, "tensor", 1)

    def to_chip(value):
        return swap(value, "tensor", 2)

    numbers = jnp.arange(docs, dtype=jnp.int32)
    edges = jnp.sum((segments[None, :] < numbers[:, None]).astype(jnp.int32), axis=1)
    which = jnp.max(jnp.where(segments[None, :] == numbers[:, None], documents[None, :], 0), axis=1)
    which = which - place_dp * docs
    first_chip = chip == 0
    edge_one = jnp.where(first_chip, edges[1], edges[2] - shift)
    edge_two = jnp.where(first_chip, edges[2], edges[3] - shift)
    mine = jnp.where(first_chip, which, jnp.roll(which, 2))
    scal = jnp.concatenate(
        [
            jnp.stack(
                [
                    core,
                    chip,
                    edges[2],
                    edge_one,
                    edge_two,
                    jnp.where(first_chip, 0, edge_one),
                    jnp.where(first_chip, edge_one, edge_two),
                    jnp.where(first_chip, edge_one, edge_two),
                    jnp.where(first_chip, edge_two, rows),
                ]
            ),
            mine,
            jnp.stack([place_dp & 1, (place_dp >> 1) & 1]),
        ]
    ).astype(jnp.int32)

    def after(value, *earlier):
        return lax.optimization_barrier((value, earlier))[0]

    attn_in = jnp.swapaxes(attn_in, 1, 2)
    cross_in = jnp.swapaxes(cross_in, 1, 2)
    w_self = (attn_in, to_chip(attn_in))
    w_self_out = (attn_out, to_chip(attn_out))
    biases = jnp.concatenate([attn_bias, cross_bias], axis=0)
    biases = jnp.concatenate([biases, to_chip(biases)], axis=1)
    w_cross = (cross_in, to_chip(after(cross_in, w_self[1])))
    w_cross_out = (cross_out, to_chip(after(cross_out, w_self[1])))

    memory = with_layout_constraint(memory, Layout(major_to_minor=(0, 1, 2)))
    memory, peer_in = lax.optimization_barrier((memory, w_self[1]))
    w_self = (attn_in, peer_in)
    x_win = lax.dynamic_slice_in_dim(inputs, chip * shift, rows)
    dy_win = lax.dynamic_slice_in_dim(cotangent, chip * shift, rows)

    def row(matrix, index):
        return matrix[index : index + 1]

    h1, q1, k1, v1, o1, lse1 = self_forward(
        scal, x_win, row(norm_gain, 0), row(norm_shift, 0), w_self, biases[0:2]
    )
    send, keep = project_out(scal, o1, w_self_out)
    k2, v2 = memory_project(scal, memory, w_cross, biases[3:4], padded)
    x1, h2_own = add_norm(
        scal, x_win, keep, to_core(send), row(out_bias, 0), row(norm_gain, 1), row(norm_shift, 1), True
    )
    h2, q2, o2, lse2, send, keep = cross_forward(
        scal, h2_own, to_core(h2_own), w_cross, biases[2:3], k2, v2, w_cross_out, frames
    )
    x2, h3_own = add_norm(
        scal, x1, keep, to_core(send), row(out_bias, 1), row(norm_gain, 2), row(norm_shift, 2), False
    )

    def spread(value):
        far = to_chip(value)
        return (value, to_core(value), far, to_core(far))

    h3, g, du, send, keep, fc_sum = feed_forward(
        scal, spread(h3_own), cotangent, fc_in, fc_in_bias[None], fc_out
    )
    more = to_core(send)
    far = fold(scal, keep, more)
    got = to_chip(far)
    du, g_low = after((du, g), far)
    out_send, out_keep = second_product(scal, g_low, fc_out, half)
    out_near = to_core(out_send)
    fc_in_grad, fc_out_grad = dot(h3, du, TN), dot(cotangent, g_low, TN)
    far_out = fold(scal, out_keep, out_near)
    got_out = to_chip(after(far_out, got))

    def pick_bit(value, axis, bit):
        mine = (place_dp >> bit) & 1
        stay = lax.dynamic_index_in_dim(value, mine, axis, keepdims=False)
        return stay, lax.dynamic_index_in_dim(value, 1 - mine, axis, keepdims=False).astype(BF)

    others = list(range(2, bits))
    blocked = (2,) * bits + (width // n_dp,)

    def add(value, got):
        return value + got.astype(F32)

    def mlp_chain(matrices):
        value = jnp.stack(matrices).reshape(2, *blocked, -1)
        for number, bit in enumerate([0, 1] + others):
            axis = 1 + bits - 1 - bit if number == 0 else value.ndim - 3
            value, send = pick_bit(value, axis, bit)
            (got,) = yield [(send, "dp", 1 << bit)]
            value = add(value, got)
        return value

    def weights_chain(full, one_send, two_send):
        got = yield [(one_send, "dp", 1), (two_send, "dp", 2)]
        stay, one_send, two_send = shares_one(scal, full, *got)
        got = yield [(one_send, "dp", 2), (two_send, "dp", 1)]
        near, far = shares_two(scal, stay, *got)
        (got,) = yield [(far, "tensor", 2)]
        value = add(near, got)
        value = value.reshape(2, *(2,) * (bits - 2), *value.shape[2:])
        for bit in others:
            value, send = pick_bit(value, value.ndim - 3, bit)
            (got,) = yield [(send, "dp", 1 << bit)]
            value = add(value, got)
        return value

    def send_all(items):
        return [swap(*item) for item in items]

    mlp = mlp_chain([fc_in_grad, fc_out_grad])
    mlp_sent = next(mlp)
    mlp_got = send_all(mlp_sent)
    got = after(got, mlp_sent[0][0], far_out)
    dx2, dx2_low, sums_three = norm_back(
        scal, dy_win, keep, got, x2, row(norm_gain, 2), True, False, more
    )
    dx2_other = to_core(dx2_low)
    dx2_full, dq2, dkv2, q2_sum, send, keep = cross_backward(
        scal, dx2_low, dx2_other, w_cross_out, q2, lse2, k2, v2, w_cross, frames
    )
    mlp_got, got_out = after((mlp_got, got_out), q2_sum)
    mlp_sent = mlp.send(mlp_got)
    mlp_got = send_all(mlp_sent)
    dkv2 = after(dkv2, mlp_sent[0][0])
    *cross_grads, v2_sum = cross_weights(scal, memory, dkv2, h2, dq2, dx2_full, o2, n_dp)
    cross = weights_chain(*cross_grads)
    cross_sent = next(cross)
    cross_got = send_all(cross_sent)
    out_own = output_rows(scal, x2, out_keep, out_near, got_out, row(out_bias, 2))
    out_far = to_chip(out_own)
    got = to_core(send)
    mlp_sent = mlp.send(after(mlp_got, v2_sum, out_own))
    mlp_got = send_all(mlp_sent)

    dkv2 = after(dkv2, cross_sent[0][0], cross_sent[1][0], mlp_sent[0][0], out_own, got)
    mem_send, mem_near, mem_keep = memory_back(scal, dkv2, w_cross, frames)
    mem_got = to_core(mem_send)
    keep = after(keep, mem_send)
    dx1, dx1_low, sums_two = norm_back(
        scal, dx2, keep, got, x1, row(norm_gain, 1), False, False, cost=1 << 26
    )
    mem_far = fold(scal, mem_keep, mem_got)
    dx1_other = after(to_core(dx1_low), mem_far)
    *own_grads, self_sum, send, keep = self_backward(
        scal, dx1_low, dx1_other, w_self_out, h1, q1, k1, v1, o1, lse1, w_self, n_dp
    )
    mem_far = to_chip(mem_far)
    out_far = after(out_far, self_sum)
    own = weights_chain(*own_grads)
    own_sent = next(own)
    own_got = send_all(own_sent)
    input_own, input_low, sums_one = norm_back(
        scal, dx1, keep, to_core(send), x_win, row(norm_gain, 0), False, True
    )
    cross_sent = cross.send(after(cross_got, sums_one))
    mlp_got = after(mlp_got, sums_one)
    mem_far = after(mem_far, cross_sent[0][0])
    input_low = after(input_low, mem_far)
    out_own, out_far, mlp_got = after((out_own, out_far, mlp_got), sums_one)

    def input_chain(value):
        (far,) = yield [(value, "tensor", 2)]
        (got,) = yield [(jnp.stack([value, far]), "tensor", 1)]
        return value, far, got

    def output_chain(value, far):
        (got,) = yield [(jnp.stack([value, far]), "tensor", 1)]
        return value, far, got

    part = self_sum.shape[1] // 2

    def sums_chain():
        heads = jnp.concatenate([self_sum, q2_sum, v2_sum])
        sums = jnp.concatenate(
            [sums_one, sums_two, sums_three, jnp.pad(heads, ((0, 0), (0, width - 2 * part))), fc_sum]
        )
        number = jnp.arange(sums.shape[0])[:, None]
        near, far, far_other = yield [(sums, "tensor", which) for which in (1, 2, 3)]
        turned = jnp.where(number < 16, jnp.roll(far, -part, axis=1), 0.0)
        sums = jnp.where(number < 12, (sums + near) + (far + far_other), sums + turned)
        for bit in range(bits):
            (got,) = yield [(sums, "dp", 1 << bit)]
            sums = sums + got
        return sums

    chains = [
        (0, own, own_sent, own_got),
        (0, input_chain(input_low), None, None),
        (0, sums_chain(), None, None),
        (OUT_ROUND, output_chain(out_own, out_far), None, None),
        (0, cross, cross_sent, None),
        (0, mlp, mlp_sent, mlp_got),
    ]
    results = [None] * len(chains)
    pending, came = {}, {}
    number = 0
    while number < 3 or pending:
        for i, (start, chain, sent, got) in enumerate(chains):
            if start == number:
                if sent is not None and got is not None:
                    came[i] = got
                elif sent is not None:
                    pending[i] = sent
                else:
                    pending[i] = next(chain) if got is None else chain.send(got)
        values = lax.optimization_barrier([[item[0] for item in items] for items in pending.values()])
        for i, held in zip(pending, values):
            came[i] = [swap(value, *item[1:]) for value, item in zip(held, pending[i])]
        if number == 1:
            mem_far, *_ = lax.optimization_barrier((mem_far, values))
            memory_grad = memory_place(scal, mem_near, mem_got, mem_far)
            came, memory_grad = lax.optimization_barrier((came, memory_grad))
        else:
            came = lax.optimization_barrier(came)
        pending = {}
        for i, got in came.items():
            try:
                pending[i] = chains[i][1].send(got)
            except StopIteration as stop:
                results[i] = stop.value
        came = {}
        number += 1
    own_share, input_parts, sums, output_parts, cross_share, mlp_share = results
    input_grad = place(scal, *input_parts, length, F32)
    output = place(scal, *output_parts, length, BF)
    memory_grad = jnp.swapaxes(memory_grad, 1, 2)
    gain_sum, shift_sum, out_sum, self_total, cross_total, fc_total = finish_sums(scal, sums, part)
    return (
        output,
        input_grad,
        memory_grad,
        gain_sum,
        shift_sum,
        jnp.stack([own_share[0, :, :part], own_share[0, :, part:], own_share[1, :, :part]]),
        self_total,
        own_share[1, :, part:].T,
        jnp.stack([cross_share[1, :, :part], cross_share[0, :, :part], cross_share[0, :, part:]]),
        cross_total,
        cross_share[1, :, part:].T,
        mlp_share[0],
        fc_total[0],
        mlp_share[1].T,
        out_sum,
    )


def solution(mesh):
    n_dp = mesh.shape["dp"]

    def run(*args):
        return per_device(*args, n_dp)

    return jax.shard_map(
        run,
        mesh=mesh,
        in_specs=(
            P("dp", None),
            P("dp", None, None),
            P("dp"),
            P("dp"),
            P("dp", None),
            P(),
            P(),
            P(None, None, "tensor"),
            P(None, "tensor"),
            P("tensor", None),
            P(None, None, "tensor"),
            P(None, "tensor"),
            P("tensor", None),
            P(None, "tensor"),
            P("tensor"),
            P("tensor", None),
            P(),
        ),
        out_specs=(
            P("dp", None),
            P("dp", None),
            P("dp", None, "tensor"),
            P(),
            P(),
            P(None, "dp", "tensor"),
            P(None, "tensor"),
            P("tensor", "dp"),
            P(None, "dp", "tensor"),
            P(None, "tensor"),
            P("tensor", "dp"),
            P("dp", "tensor"),
            P("tensor"),
            P("tensor", "dp"),
            P(),
        ),
        check_vma=False,
    )
```
